32 devices in a mesh: fsdp: 2 (over x), context: 4 (over y, core), tensor: 4 (over z).
Axes of the slice: x: 2, y: 2, z: 4, core: 2. Of those that a mesh axis runs over, the one named last changes fastest.
Arguments:
- hidden_in: bfloat16 [2, 1024, 2048], P('fsdp', ('context', 'tensor')), may hold values from -6 to 6
- segment_ids: int32 [2, 1024], P('fsdp'), may hold values from 0 to 15, never falling along the last dimension, each value on 1 to 512 neighbouring positions
- pad_mask: int32 [2, 1024], P('fsdp'), may hold values from 0 to 1, as said below
- attn_gain: bfloat16 [2048], P(('fsdp', 'context')), may hold values from 0.5 to 1.5
- w_query: bfloat16 [2048, 2048], P(('fsdp', 'context'), 'tensor'), may hold values from -0.1875 to 0.1875
- w_key: bfloat16 [2048, 256], P(('fsdp', 'context'), 'tensor'), may hold values from -0.1875 to 0.1875
- w_value: bfloat16 [2048, 256], P(('fsdp', 'context'), 'tensor'), may hold values from -0.125 to 0.125
- w_out: bfloat16 [2048, 2048], P('tensor', ('fsdp', 'context')), may hold values from -0.5 to 0.5
- mlp_gain: bfloat16 [2048], P(('fsdp', 'context')), may hold values from 0.5 to 1.5
- w_gate: bfloat16 [2048, 5632], P(('fsdp', 'context'), 'tensor'), may hold values from -0.125 to 0.125
- w_up: bfloat16 [2048, 5632], P(('fsdp', 'context'), 'tensor'), may hold values from -0.125 to 0.125
- w_down: bfloat16 [5632, 2048], P('tensor', ('fsdp', 'context')), may hold values from -0.078125 to 0.078125
- cotangent: bfloat16 [2, 1024, 2048], P('fsdp', ('context', 'tensor')), may hold values from -6 to 6
Outputs:
- block_out: bfloat16 [2, 1024, 2048], P('fsdp', ('context', 'tensor'))
- grad_hidden: float32 [2, 1024, 2048], P('fsdp', ('context', 'tensor'))
- grad_attn_gain: float32 [2048], P(('fsdp', 'context'))
- grad_query: float32 [2048, 2048], P(('fsdp', 'context'), 'tensor')
- grad_key: float32 [2048, 256], P(('fsdp', 'context'), 'tensor')
- grad_value: float32 [2048, 256], P(('fsdp', 'context'), 'tensor')
- grad_out: float32 [2048, 2048], P('tensor', ('fsdp', 'context'))
- grad_mlp_gain: float32 [2048], P(('fsdp', 'context'))
- grad_gate: float32 [2048, 5632], P(('fsdp', 'context'), 'tensor')
- grad_up: float32 [2048, 5632], P(('fsdp', 'context'), 'tensor')
- grad_down: float32 [5632, 2048], P('tensor', ('fsdp', 'context'))
The draws below stay inside these ranges and needn't reach their ends.
Inputs may be any that keep to these rules, and one draw needn't show every extreme that they name: `segment_ids`: ids never fall along a sequence; a document is a run of 1 to 512 consecutive tokens of one id. `pad_mask`: every sequence ends in one or more padding slots, and no other slot is padding.
All inputs are finite; a program needn't handle non-finite values.
Results may differ from the reference program's by a relative error of at most 0.013.
The reference program's roundings to bfloat16 on the way count: a program that leaves them out, or rounds other values in their place, can miss the bound.
Values may be sent and summed in bfloat16 or wider, within the bound.
A program may use at most 88 MiB of HBM per device.

```python
import math
import jax
import jax.numpy as jnp
import numpy as np
from jax import lax

D = 2048
HQ = 32
KV = 4
HD = 64
FF = 5632
LEN = 1024
DOCS = 16
SEQS = 2


def draw_pad_mask(key, part):
    pad_count = jax.random.randint(key, (SEQS, 1), 1, LEN // 8 + 1)
    columns = jnp.arange(LEN, dtype=jnp.int32)[None, :]
    return (columns < LEN - pad_count).astype(jnp.int32)


def levels(rng, shape, split, least, largest):
    loudness = 1.0
    for axis_at, parts in split:
        heights = jax.random.uniform(jax.random.fold_in(jax.random.fold_in(rng, 6), axis_at), (parts,), jnp.float32, least / len(split), largest / len(split))
        loudness = loudness * jnp.repeat(jnp.exp(heights), shape[axis_at] // parts).reshape((-1,) + (1,) * (len(shape) - 1 - axis_at))
    return loudness


def length_profile(number_of, total, limit, lean):
    weights = [(1 << 20) // math.isqrt(grade ** lean) + 1 for grade in range(2, number_of + 1)]
    spare, counts = total - limit - (number_of - 1), [1] * (number_of - 1)
    while spare > 0:
        movable = [i for i in range(number_of - 1) if counts[i] < limit]
        whole, left = sum([weights[i] for i in movable]), spare
        for i in movable:
            extra = min(limit - counts[i], max(1, left * weights[i] // whole), spare)
            counts[i] = counts[i] + extra
            spare = spare - extra
    return np.array([limit] + counts)


def ragged_sizes(rng, count, total, reach, lean):
    if count == 2:
        one = jax.random.randint(rng, (), max(1, total - reach), min(reach, total - 1) + 1)
        return jnp.stack([one, total - one])
    tallies = jnp.asarray(length_profile(count, total, reach, lean), jnp.int32)
    twos = (count - 1) // 2
    source_of, taker = tallies[1:1 + 2 * twos:2], tallies[2:2 + 2 * twos:2]
    room = jnp.minimum(source_of - 1, reach - taker)
    shifted = jax.random.randint(jax.random.fold_in(rng, 1), (twos,), 0, 1 << 20) % (room + 1)
    tallies = tallies.at[1:1 + 2 * twos:2].set(source_of - shifted).at[2:2 + 2 * twos:2].set(taker + shifted)
    return tallies[jax.random.permutation(jax.random.fold_in(rng, 2), count)]


def scatter_about(key, dims, width, reach, shards=(), kind=jnp.bfloat16):
    values = width * jax.random.normal(key, dims, jnp.float32)
    if shards:
        values = values * levels(key, dims, shards, -0.22, 0.18)
    return jnp.clip(values, -reach, reach).astype(kind)


def setup_inputs(seed: int = 0) -> dict:
    streams_of = jax.random.split(jax.random.key(seed), 14)
    return {
        "hidden_in": scatter_about(streams_of[0], (SEQS, LEN, D), 1.0, 6.0, ((0, 2), (1, 16))),
        "segment_ids": jax.vmap(lambda own: jnp.searchsorted(jnp.cumsum(ragged_sizes(own, DOCS, LEN, LEN // 2, 2)), jnp.arange(LEN), side="right"))(jax.random.split(streams_of[1], SEQS)).reshape((SEQS, LEN)).astype(jnp.int32),
        "pad_mask": draw_pad_mask(jax.random.fold_in(streams_of[13], 71), 0),
        "attn_gain": jnp.clip(1.0 + 0.1 * jax.random.normal(streams_of[3], (D,), jnp.float32), 0.5, 1.5).astype(jnp.bfloat16),
        "w_query": scatter_about(streams_of[4], (D, HQ * HD), (D // 2) ** -0.5, 0.1875, ((0, 8), (1, 4))),
        "w_key": scatter_about(streams_of[5], (D, KV * HD), (D // 2) ** -0.5, 0.1875, ((0, 8), (1, 4))),
        "w_value": scatter_about(streams_of[6], (D, KV * HD), D ** -0.5, 0.125, ((0, 8), (1, 4))),
        "w_out": scatter_about(streams_of[7], (HQ * HD, D), (HQ * HD // 16) ** -0.5, 0.5, ((0, 4), (1, 8))),
        "mlp_gain": jnp.clip(1.0 + 0.1 * jax.random.normal(streams_of[8], (D,), jnp.float32), 0.5, 1.5).astype(jnp.bfloat16),
        "w_gate": scatter_about(streams_of[9], (D, FF), D ** -0.5, 0.125, ((0, 8), (1, 4))),
        "w_up": scatter_about(streams_of[10], (D, FF), D ** -0.5, 0.125, ((0, 8), (1, 4))),
        "w_down": scatter_about(streams_of[11], (FF, D), FF ** -0.5, 0.078125, ((0, 4), (1, 8))),
        "cotangent": scatter_about(streams_of[12], (SEQS, LEN, D), 1.0, 6.0, ((0, 2), (1, 16))),
    }


EPS = 1e-05
NEG = -1e+30
HIGHEST = lax.Precision.HIGHEST

@jax.custom_vjp
def low(v):
    return lax.optimization_barrier(v.astype(jnp.bfloat16)).astype(jnp.float32)

@jax.custom_vjp
def low_back(v):
    return v

def low_keep(v):
    return (low(v), None)

def low_pass(kept, grad):
    return (grad,)

def back_keep(v):
    return (v, None)

def back_low(kept, grad):
    return (low(grad),)
low.defvjp(low_keep, low_pass)
low_back.defvjp(back_keep, back_low)

def positions_of(segments):
    length = segments.shape[1]
    columns = jnp.arange(length, dtype=jnp.int32)[None, :]
    previous = jnp.concatenate([jnp.full((segments.shape[0], 1), -1, jnp.int32), segments[:, :-1]], axis=1)
    starts = jnp.where(segments != previous, columns, jnp.zeros_like(columns))
    return (columns - lax.cummax(starts, axis=1)).astype(jnp.int32)

def rope_tables(positions, head_size):
    half_size = head_size // 2
    frequency = jnp.exp(-(jnp.arange(half_size, dtype=jnp.float32) * (2.0 / head_size)) * math.log(10000.0))
    angles = positions.astype(jnp.float32)[..., None] * frequency
    return (jnp.cos(angles)[..., None, :], jnp.sin(angles)[..., None, :])

def rotate(vectors, cos_table, sin_table):
    half_size = vectors.shape[-1] // 2
    first_half = vectors[..., :half_size]
    second_half = vectors[..., half_size:]
    return jnp.concatenate([first_half * cos_table - second_half * sin_table, second_half * cos_table + first_half * sin_table], axis=-1)

def allowed_of(seg_row, pad_row):
    length = seg_row.shape[0]
    columns = jnp.arange(length, dtype=jnp.int32)
    same_doc = seg_row[:, None] == seg_row[None, :]
    causal = columns[None, :] <= columns[:, None]
    live_key = (pad_row[None, :] == 1) | (columns[:, None] == columns[None, :])
    return same_doc & causal & live_key

def high_dot(left_side, right_side):
    return jnp.dot(left_side, right_side, precision=HIGHEST, preferred_element_type=jnp.float32)

def rms_norm(vectors, gain_row):
    return vectors * lax.rsqrt(lax.optimization_barrier(jnp.mean(vectors * vectors, axis=-1, keepdims=True)) + EPS) * gain_row

def attend_sequence(packed_item):
    query_rows, key_rows, value_rows, seg_row, pad_row = packed_item
    grouped = query_rows.reshape(LEN, KV, HQ // KV, HD)
    scores = low_back(jnp.einsum('qkgd,tkd->kgqt', grouped, key_rows, precision=HIGHEST) * HD ** (-0.5))
    scores = jnp.where(allowed_of(seg_row, pad_row)[None, None], scores, NEG)
    row_max = lax.optimization_barrier(jnp.max(scores, axis=-1, keepdims=True))
    exp_scores = jnp.exp(scores - row_max)
    weights = exp_scores / lax.optimization_barrier(jnp.sum(exp_scores, axis=-1, keepdims=True))
    output = jnp.einsum('kgqt,tkd->qkgd', low(weights), value_rows, precision=HIGHEST)
    return output.reshape(LEN, HQ * HD)

def reference(hidden_in, segment_ids, pad_mask, attn_gain, w_query, w_key, w_value, w_out, mlp_gain, w_gate, w_up, w_down, cotangent):
    cos_table, sin_table = rope_tables(positions_of(segment_ids), HD)
    keep_rows = pad_mask.astype(jnp.float32)[..., None]

    def block_forward(hidden_f, gain_one, query_w, key_w, value_w, out_w, gain_two, gate_w, up_w, down_w):
        normed_one = low(rms_norm(hidden_f, gain_one))
        flat_one = normed_one.reshape(-1, D)
        query_pre = low_back(high_dot(flat_one, query_w)).reshape(SEQS, LEN, HQ, HD)
        queries = low(rotate(query_pre, cos_table, sin_table))
        key_pre = low_back(high_dot(flat_one, key_w)).reshape(SEQS, LEN, KV, HD)
        key_rows = low(rotate(key_pre, cos_table, sin_table))
        value_rows = low_back(low(high_dot(flat_one, value_w))).reshape(SEQS, LEN, KV, HD)
        attn_rows = lax.map(jax.checkpoint(attend_sequence), (queries, key_rows, value_rows, segment_ids, pad_mask))
        attn_rows = low_back(low(attn_rows)).reshape(-1, HQ * HD)
        branch_one = low_back(high_dot(attn_rows, out_w)).reshape(SEQS, LEN, D)
        middle = hidden_f + branch_one
        normed_two = low(rms_norm(middle, gain_two)).reshape(-1, D)
        gate_rows = low_back(high_dot(normed_two, gate_w))
        up_rows = low_back(high_dot(normed_two, up_w))
        inner_rows = low(jax.nn.silu(gate_rows) * up_rows)
        branch_two = low_back(high_dot(inner_rows, down_w)).reshape(SEQS, LEN, D)
        return keep_rows * (middle + branch_two)
    inputs_f = (hidden_in.astype(jnp.float32), attn_gain.astype(jnp.float32), w_query.astype(jnp.float32), w_key.astype(jnp.float32), w_value.astype(jnp.float32), w_out.astype(jnp.float32), mlp_gain.astype(jnp.float32), w_gate.astype(jnp.float32), w_up.astype(jnp.float32), w_down.astype(jnp.float32))
    result, pull_back = jax.vjp(block_forward, *inputs_f)
    gradients = pull_back(cotangent.astype(jnp.float32))
    return (result.astype(jnp.bfloat16), gradients[0], gradients[1], gradients[2], gradients[3], gradients[4], gradients[5], gradients[6], gradients[7], gradients[8], gradients[9])
```

```python
import math

import jax
import jax.numpy as jnp
from jax import lax
from jax.sharding import PartitionSpec as P

EPS = 1e-05
NEG = -1e30
BF = jnp.bfloat16
F32 = jnp.float32


def rope_tables(positions, head_size):
    half_size = head_size // 2
    frequency = jnp.exp(
        -(jnp.arange(half_size, dtype=F32) * (2.0 / head_size)) * math.log(10000.0)
    )
    angles = positions.astype(F32)[..., None] * frequency
    return (jnp.cos(angles)[..., None, :], jnp.sin(angles)[..., None, :])


def rotate(vectors, cos_table, sin_table):
    half_size = vectors.shape[-1] // 2
    first_half = vectors[..., :half_size]
    second_half = vectors[..., half_size:]
    return jnp.concatenate(
        [
            first_half * cos_table - second_half * sin_table,
            second_half * cos_table + first_half * sin_table,
        ],
        axis=-1,
    )


def mm(a, b, ca=1, cb=0):
    return lax.dot_general(a, b, (((ca,), (cb,)), ((), ())), preferred_element_type=F32)


def rows_gather(x):
    return lax.all_gather(x, "tensor", axis=0, tiled=True)


def rows_sum(x):
    return lax.psum_scatter(x.astype(BF), "tensor", scatter_dimension=0, tiled=True).astype(F32)


FC = ("fsdp", "context")


def gather_w(w, axis=0):
    return lax.all_gather(w, FC, axis=axis, tiled=True)


def scatter_g(g, axis=0):
    return lax.psum_scatter(g.astype(BF), FC, scatter_dimension=axis, tiled=True).astype(F32)


def norm_back(grad_normed, vectors, inv_scale, gain_row):
    unit_rows = vectors * inv_scale
    weighted = grad_normed * gain_row
    grad_gain = jnp.sum(grad_normed * unit_rows, axis=0)
    grad_vectors = inv_scale * (
        weighted - unit_rows * jnp.mean(weighted * unit_rows, axis=-1, keepdims=True)
    )
    return (grad_vectors, grad_gain)


def one_sequence(
    hidden_in, segment_ids, pad_mask, attn_gain, w_query, w_key, w_value, w_out,
    mlp_gain, w_gate, w_up, w_down, cotangent,
):
    row_count, model_width = hidden_in.shape
    context_count = lax.axis_size("context")
    tensor_count = lax.axis_size("tensor")
    context_index = lax.axis_index("context")
    tensor_index = lax.axis_index("tensor")
    length = segment_ids.shape[0]
    span = length // context_count
    hd = w_key.shape[1]
    start = context_index * span
    seg_span = lax.dynamic_slice_in_dim(segment_ids, start, span, 0)
    columns = jnp.arange(length, dtype=jnp.int32)
    row_at = start + jnp.arange(span, dtype=jnp.int32)
    first = jnp.sum((segment_ids[None, :] < seg_span[:, None]).astype(jnp.int32), axis=1)
    cos_t, sin_t = rope_tables(row_at - first, hd)
    row_start = start + tensor_index * row_count
    keep = lax.dynamic_slice_in_dim(pad_mask, row_start, row_count, 0).astype(F32)[:, None]
    allowed = (
        (seg_span[:, None] == segment_ids[None, :])
        & (columns[None, :] <= row_at[:, None])
        & ((pad_mask[None, :] == 1) | (columns[None, :] == row_at[:, None]))
    )
    gain_one = gather_w(attn_gain).astype(F32)
    gain_two = gather_w(mlp_gain).astype(F32)
    qkv_all = gather_w(jnp.concatenate([w_query, w_key, w_value], axis=1))
    out_all = gather_w(w_out, 1)
    gate_all = gather_w(w_gate)
    up_all = gather_w(w_up)
    down_all = gather_w(w_down, 1)
    qw = w_query.shape[1]

    hidden = hidden_in.astype(F32)
    scale_one = lax.rsqrt(jnp.mean(hidden * hidden, axis=-1, keepdims=True) + EPS)
    n1 = rows_gather((hidden * scale_one * gain_one).astype(BF))
    g_out = cotangent.astype(F32) * keep
    g_all = rows_gather(g_out.astype(BF))
    pre = mm(n1, qkv_all)
    q = rotate(pre[:, :qw].reshape(span, -1, hd), cos_t, sin_t).astype(BF)
    k = rotate(pre[:, None, qw:qw + hd], cos_t, sin_t).astype(BF)[:, 0]
    v = pre[:, qw + hd:].astype(BF)
    kv = lax.all_gather(jnp.concatenate([k, v], axis=1), "context", axis=0, tiled=True)
    k, v = kv[:, :hd], kv[:, hd:]
    scale = hd ** (-0.5)
    scores = jnp.einsum("qhd,td->hqt", q, k, preferred_element_type=F32) * scale
    scores = jnp.where(allowed[None], scores, NEG)
    top = jnp.max(scores, axis=-1, keepdims=True)
    e = jnp.exp(scores - top)
    probs = e / jnp.sum(e, axis=-1, keepdims=True)
    probs_b = probs.astype(BF)
    attn = jnp.einsum("hqt,td->qhd", probs_b, v, preferred_element_type=F32)
    attn = attn.reshape(span, -1).astype(BF)
    middle = hidden + rows_sum(mm(attn, out_all))
    scale_two = lax.rsqrt(jnp.mean(middle * middle, axis=-1, keepdims=True) + EPS)
    n2 = rows_gather((middle * scale_two * gain_two).astype(BF))
    gate = mm(n2, gate_all)
    up = mm(n2, up_all)
    sig = jax.nn.sigmoid(gate)
    inner = (gate * sig * up).astype(BF)
    block_out = (keep * (middle + rows_sum(mm(inner, down_all)))).astype(BF)

    grad_down = mm(inner, g_all, 0, 0)
    g_inner = mm(g_all, down_all, 1, 1)
    g_gate = (g_inner * up * sig * (1.0 + gate * (1.0 - sig))).astype(BF)
    g_up = (g_inner * gate * sig).astype(BF)
    g_n2 = rows_sum(mm(g_gate, gate_all, 1, 1) + mm(g_up, up_all, 1, 1))
    grad_gate = mm(n2, g_gate, 0, 0)
    grad_up = mm(n2, g_up, 0, 0)
    d_mid, grad_gain_two = norm_back(g_n2, middle, scale_two, gain_two)
    g_mid = g_out + d_mid
    gm_all = rows_gather(g_mid.astype(BF))
    grad_out = mm(attn, gm_all, 0, 0)
    g_attn = mm(gm_all, out_all, 1, 1).astype(BF).reshape(span, -1, hd)
    dp = jnp.einsum("qhd,td->hqt", g_attn, v, preferred_element_type=F32)
    delta = jnp.sum(probs * dp, axis=-1, keepdims=True)
    ds = (probs * (dp - delta)).astype(BF)
    g_q = jnp.einsum("hqt,td->qhd", ds, k, preferred_element_type=F32) * scale
    g_k = jnp.einsum("hqt,qhd->td", ds, q, preferred_element_type=F32) * scale
    g_v = jnp.einsum("hqt,qhd->td", probs_b, g_attn, preferred_element_type=F32)
    g_kv = lax.psum_scatter(
        jnp.concatenate([g_k, g_v], axis=1), "context", scatter_dimension=0, tiled=True
    )
    g_q = rotate(g_q, cos_t, -sin_t).astype(BF).reshape(span, -1)
    g_k = rotate(g_kv[:, None, :hd], cos_t, -sin_t).astype(BF)[:, 0]
    g_qkv = jnp.concatenate([g_q, g_k, g_kv[:, hd:].astype(BF)], axis=1)
    g_n1 = rows_sum(mm(g_qkv, qkv_all, 1, 1))
    grad_qkv = mm(n1, g_qkv, 0, 0)
    d_hid, grad_gain_one = norm_back(g_n1, hidden, scale_one, gain_one)
    gains = jnp.stack([grad_gain_one, grad_gain_two])
    return (
        block_out, g_mid + d_hid, gains, grad_qkv, grad_out, grad_gate, grad_up, grad_down,
    )


def body(hidden_in, segment_ids, pad_mask, attn_gain, w_query, w_key, w_value, w_out,
         mlp_gain, w_gate, w_up, w_down, cotangent):
    block_out, grad_hidden, gains, grad_qkv, grad_out, grad_gate, grad_up, grad_down = one_sequence(
        hidden_in[0], segment_ids[0], pad_mask[0], attn_gain, w_query, w_key, w_value, w_out,
        mlp_gain, w_gate, w_up, w_down, cotangent[0],
    )
    grad_down = scatter_g(grad_down, 1)
    grad_gate = scatter_g(grad_gate)
    grad_up = scatter_g(grad_up)
    grad_out = scatter_g(grad_out, 1)
    grad_qkv = scatter_g(grad_qkv)
    gains = lax.psum(gains, "tensor")
    gains = lax.psum_scatter(gains, FC, scatter_dimension=1, tiled=True)
    qw, hd = w_query.shape[1], w_key.shape[1]
    return (
        block_out[None], grad_hidden[None], gains[0], grad_qkv[:, :qw],
        grad_qkv[:, qw:qw + hd], grad_qkv[:, qw + hd:], grad_out, gains[1],
        grad_gate, grad_up, grad_down,
    )


def solution(mesh):
    fc = ("fsdp", "context")
    rows = P("fsdp", ("context", "tensor"), None)
    tail = (P(fc), P(fc, "tensor"), P(fc, "tensor"), P(fc, "tensor"), P("tensor", fc),
            P(fc), P(fc, "tensor"), P(fc, "tensor"), P("tensor", fc))
    in_specs = (rows, P("fsdp", None), P("fsdp", None)) + tail + (rows,)
    out_specs = (rows, rows) + tail
    return jax.shard_map(body, mesh=mesh, in_specs=in_specs, out_specs=out_specs, check_vma=False)
```

```python
import functools
import math

import jax
import jax.numpy as jnp
from jax import lax
from jax.experimental import pallas as pl
from jax.experimental.pallas import tpu as pltpu
from jax.sharding import PartitionSpec as P

EPS = 1e-05
NEG = -1e30
BF = jnp.bfloat16
F32 = jnp.float32
MESH = pl.DeviceIdType.MESH
FC = ("fsdp", "context")


def dot(a, b, ca=1, cb=0):
    return lax.dot_general(a, b, (((ca,), (cb,)), ((), ())), preferred_element_type=F32)


def chunks(total, step):
    return [(at, min(step, total - at)) for at in range(0, total, step)]


class Links:
    def __init__(self, sizes, send_sems, recv_sems):
        self.F, self.C, self.T = sizes
        self.f = lax.axis_index("fsdp")
        self.c = lax.axis_index("context")
        self.t = lax.axis_index("tensor")
        self.h = self.c // 2
        self.core = self.c % 2
        self.H = self.C // 2
        self.send_sems, self.recv_sems = send_sems, recv_sems
        self.used = 0
        self.open = []
        self.sib = (self.f, self.h * 2 + 1 - self.core, self.t)

    def chip(self, df, dh):
        return ((self.f + df) % self.F, ((self.h + dh) % self.H) * 2 + self.core, self.t)

    def block_of(self, df, dh, other=False):
        core = 1 - self.core if other else self.core
        return ((self.f - df) % self.F) * self.C + ((self.h - dh) % self.H) * 2 + core

    def zpeer(self, i):
        return (self.f, self.c, (self.t + i) % self.T)

    def cpeer(self, i):
        return (self.f, (self.c + i) % self.C, self.t)

    def send(self, src, dst, dev):
        n = self.used
        self.used += 1
        copy = pltpu.make_async_remote_copy(
            src_ref=src, dst_ref=dst, send_sem=self.send_sems.at[n],
            recv_sem=self.recv_sems.at[n], device_id=dev, device_id_type=MESH,
        )
        copy.start()
        self.open.append(copy)
        return copy

    def peers(self):
        out = []
        for df in range(self.F):
            for dc in range(self.C):
                if df or dc:
                    out.append(((self.f + df) % self.F, (self.c + dc) % self.C, self.t))
        return out + [self.zpeer(i) for i in range(1, self.T)]

    def barrier(self):
        sem = pltpu.get_barrier_semaphore()
        peers = self.peers()
        for dev in peers:
            pl.semaphore_signal(sem, inc=1, device_id=dev, device_id_type=MESH)
        pl.semaphore_wait(sem, len(peers))

    def finish(self):
        for copy in self.open:
            copy.wait_send()


class Gather:
    def __init__(self, links, full, rows):
        self.k, self.full, self.rows = links, full, rows

    def part(self, block, half=None):
        if half is None:
            return self.full.at[pl.ds(pl.multiple_of(block * self.rows, self.rows), self.rows)]
        n = self.rows // 2
        return self.full.at[pl.ds(pl.multiple_of(block * self.rows + half * n, n), n)]

    def first(self, own):
        k = self.k
        mine = self.part(k.block_of(0, 0))
        self.line = {}
        for df in range(1, k.F):
            self.line[df, 0] = k.send(own, mine, k.chip(df, 0))
        for dh in range(1, k.H):
            self.line[0, dh] = k.send(own, mine, k.chip(0, dh))
        self.twin = [k.send(own, mine, k.sib)]

    def second(self):
        k = self.k
        self.diag = {}
        for (df, dh), copy in self.line.items():
            copy.wait_recv()
            block = k.block_of(df, dh)
            half = 0 if df else 1
            piece = self.part(block, half)
            if df:
                for eh in range(1, k.H):
                    self.diag[df, eh, half] = k.send(piece, piece, k.chip(0, eh))
            else:
                for ef in range(1, k.F):
                    self.diag[ef, dh, half] = k.send(piece, piece, k.chip(ef, 0))
            whole = self.part(block)
            self.twin.append(k.send(whole, whole, k.sib))

    def third(self):
        k = self.k
        for copy in self.diag.values():
            copy.wait_recv()
        for df in range(1, k.F):
            for dh in range(1, k.H):
                whole = self.part(k.block_of(df, dh))
                self.twin.append(k.send(whole, whole, k.sib))

    def done(self):
        for copy in self.twin:
            copy.wait_recv()


def n_gather(F, H):
    a, b, d = F - 1, H - 1, (F - 1) * (H - 1)
    return a + b + 1 + 2 * d + a + b + d


def forward_kernel(
    sizes, hd,
    hidden_ref, seg_ref, segc_ref, pad_ref, cos_ref, sin_ref, gain_ref, wq_ref, wk_ref, wv_ref,
    wo_ref, wd_ref, gout_ref, wg_ref, wu_ref,
    n1_ref, q_ref, kv_ref, attn_ref, lse_ref, mid_ref, n2_ref, gall_ref, w_ref, gains_ref,
    gate_ref, up_ref, down_ref,
    dt, bias, part_f, part_b, slots, sends, recvs, local,
):
    k = Links(sizes, sends, recvs)
    rows, D = hidden_ref.shape
    R, QW = wq_ref.shape
    FB = wg_ref.shape[1]
    span = n1_ref.shape[0]
    length = seg_ref.shape[1]
    nh = QW // hd
    T = k.T
    mine = k.block_of(0, 0)

    aw = Gather(k, w_ref, R)
    own_w = aw.part(mine)
    own_w[:, :QW] = wq_ref[...]
    own_w[:, QW:QW + 2 * hd] = jnp.concatenate([wk_ref[...], wv_ref[...]], axis=1)
    own_w[:, QW + 2 * hd:] = wo_ref[...].astype(F32).T.astype(BF)
    gains_ref[mine] = gain_ref[...].astype(F32)
    k.barrier()
    own_gain = gains_ref.at[mine]
    gain_copies = [k.send(own_gain, own_gain, dev) for dev in k.peers()[: k.F * k.C - 1]]
    aw.first(own_w)
    gw, uw, dw = Gather(k, gate_ref, R), Gather(k, up_ref, R), Gather(k, down_ref, R)

    hidden = hidden_ref[...].astype(F32)
    scale_one = lax.rsqrt(jnp.mean(hidden * hidden, axis=-1, keepdims=True) + EPS)
    for copy in gain_copies:
        copy.wait_recv()

    def gain_row(which):
        return jnp.concatenate(
            [gains_ref[b][:, which * R:(which + 1) * R] for b in range(k.F * k.C)], axis=1
        )

    at_t = pl.ds(pl.multiple_of(k.t * rows, rows), rows)

    def z_gather(full):
        piece = full.at[at_t]
        return [k.send(piece, piece, k.zpeer(i)) for i in range(1, T)]

    n1_ref[at_t] = (hidden * scale_one * gain_row(0)).astype(BF)
    n1_copies = z_gather(n1_ref)
    dt[...] = wd_ref[...].astype(F32).T.astype(BF)
    local_copies = [
        pltpu.make_async_copy(wg_ref, gw.part(mine), local.at[0]),
        pltpu.make_async_copy(wu_ref, uw.part(mine), local.at[1]),
        pltpu.make_async_copy(dt, dw.part(mine), local.at[2]),
    ]
    for copy in local_copies:
        copy.start()
    seg_span = segc_ref[...]
    row_at = k.c * span + lax.broadcasted_iota(jnp.int32, (span, length), 0)
    column = lax.broadcasted_iota(jnp.int32, (span, length), 1)
    keep = (seg_span == seg_ref[...]) & (column <= row_at) & (
        (pad_ref[...] == 1) | (column == row_at)
    )
    bias[...] = jnp.where(keep, 0.0, NEG)
    aw.second()
    gw.first(wg_ref)
    aw.third()
    aw.done()
    for copy in n1_copies:
        copy.wait_recv()
    gall_ref[at_t] = gout_ref[...]
    g_copies = z_gather(gall_ref)

    cos, sin = cos_ref[...], sin_ref[...]
    lane = lax.broadcasted_iota(jnp.int32, (span, 2 * hd), 1)
    low = (lane % hd) < (hd // 2)

    def turn(x, sin_table):
        swapped = jnp.where(low, pltpu.roll(x, 2 * hd - hd // 2, 1), pltpu.roll(x, hd // 2, 1))
        return x * cos + swapped * sin_table

    n1 = n1_ref[...]
    for n in range(QW // (2 * hd)):
        at = n * 2 * hd
        pre = turn(dot(n1, w_ref[:, at:at + 2 * hd]), sin).astype(BF)
        q_ref[2 * n] = pre[:, :hd]
        q_ref[2 * n + 1] = pre[:, hd:]
    pre = dot(n1, w_ref[:, QW:QW + 2 * hd])
    at_c = pl.ds(pl.multiple_of(k.c * span, span), span)
    kv_ref[at_c] = jnp.where(lane < hd, turn(pre, sin), pre).astype(BF)
    own_kv = kv_ref.at[at_c]
    kv_copies = [k.send(own_kv, own_kv, k.cpeer(i)) for i in range(1, k.C)]
    gw.second()
    uw.first(wu_ref)
    for copy in kv_copies:
        copy.wait_recv()

    @pl.loop(0, nh)
    def _(n):
        scores = dot(q_ref[n], kv_ref[:, :hd], 1, 1) * hd ** (-0.5) + bias[...]
        top = jnp.max(scores, axis=-1, keepdims=True)
        e = jnp.exp(scores - top)
        total = jnp.sum(e, axis=-1, keepdims=True)
        attn_ref[n] = dot((e / total).astype(BF), kv_ref[:, hd:]).astype(BF)
        lse_ref[n] = top + jnp.log(total)

    attn = jnp.concatenate([attn_ref[n] for n in range(nh)], axis=1)

    @pl.loop(0, D // 256)
    def _(n):
        at = pl.ds(pl.multiple_of(n * 256, 256), 256)
        part = dot(attn, w_ref[at, QW + 2 * hd:], 1, 1)
        part_f[:, at] = part
        part_b[:, at] = part.astype(BF)

    part_copies = []
    for i in range(1, T):
        dest = (k.t + i) % T
        src = part_b.at[pl.ds(pl.multiple_of(dest * rows, rows), rows)]
        part_copies.append(k.send(src, slots.at[i - 1], k.zpeer(i)))
    gw.third()
    uw.second()
    dw.first(dt)
    middle = hidden + part_f[at_t]
    for i in range(1, T):
        part_copies[i - 1].wait_recv()
        middle = middle + slots[i - 1].astype(F32)
    mid_ref[...] = middle
    scale_two = lax.rsqrt(jnp.mean(middle * middle, axis=-1, keepdims=True) + EPS)
    n2_ref[at_t] = (middle * scale_two * gain_row(1)).astype(BF)
    n2_copies = z_gather(n2_ref)
    uw.third()
    dw.second()
    dw.third()
    for copy in n2_copies + g_copies:
        copy.wait_recv()
    for w in (gw, uw, dw):
        w.done()
    for copy in local_copies:
        copy.wait()
    k.finish()


def forward(sizes, hd, hidden, seg, seg_span, pad, cos, sin, gains, wq, wk, wv, wo, wd, g_out, wg, wu):
    F, C, T = sizes
    rows, D = hidden.shape
    R, QW = wq.shape
    FB = wg.shape[1]
    span, length, nh = rows * T, seg.shape[1], QW // hd
    vm = pl.BlockSpec(memory_space=pltpu.VMEM)
    hbm = pl.BlockSpec(memory_space=pl.ANY)
    H = C // 2
    n_sems = 4 * n_gather(F, H) + F * C - 1 + 4 * (T - 1) + C - 1
    S = jax.ShapeDtypeStruct
    return pl.pallas_call(
        functools.partial(forward_kernel, sizes, hd),
        out_shape=(
            S((span, D), BF), S((nh, span, hd), BF), S((length, 2 * hd), BF), S((nh, span, hd), BF),
            S((nh, span, 1), F32), S((rows, D), F32), S((span, D), BF), S((span, D), BF),
            S((D, 2 * QW + 2 * hd), BF), S((F * C, 1, 2 * R), F32),
            S((D, FB), BF), S((D, FB), BF), S((D, FB), BF),
        ),
        in_specs=[vm] * 13 + [hbm] * 2,
        out_specs=[vm] * 10 + [hbm] * 3,
        scratch_shapes=[
            pltpu.VMEM((R, FB), BF), pltpu.VMEM((span, length), F32), pltpu.VMEM((span, D), F32),
            pltpu.VMEM((span, D), BF), pltpu.VMEM((T - 1, rows, D), BF),
            pltpu.SemaphoreType.DMA((n_sems,)), pltpu.SemaphoreType.DMA((n_sems,)),
            pltpu.SemaphoreType.DMA((3,)),
        ],
        compiler_params=pltpu.CompilerParams(
            collective_id=0, has_side_effects=True, vmem_limit_bytes=56 * 2**20
        ),
        name="forward",
    )(hidden, seg, seg_span, pad, cos, sin, gains, wq, wk, wv, wo, wd, g_out, wg, wu)


def rotate_back(x, cos, sin, hd):
    half = hd // 2
    a, b = x[..., :half], x[..., half:]
    ct, st = cos[:, None, :half], sin[:, None, :half]
    return jnp.concatenate([a * ct + b * st, b * ct - a * st], axis=-1)


def rows_gather(x):
    return lax.all_gather(x, "tensor", axis=0, tiled=True)


def rows_sum(x):
    return lax.psum_scatter(x.astype(BF), "tensor", scatter_dimension=0, tiled=True).astype(F32)


def scatter_g(g):
    return lax.psum_scatter(g.astype(BF), FC, scatter_dimension=0, tiled=True).astype(F32)


def norm_back(grad_normed, vectors, inv_scale, gain_row):
    unit_rows = vectors * inv_scale
    weighted = grad_normed * gain_row
    grad_gain = jnp.sum(grad_normed * unit_rows, axis=0)
    grad_vectors = inv_scale * (
        weighted - unit_rows * jnp.mean(weighted * unit_rows, axis=-1, keepdims=True)
    )
    return (grad_vectors, grad_gain)


def body(hidden_in, segment_ids, pad_mask, attn_gain, w_query, w_key, w_value, w_out,
         mlp_gain, w_gate, w_up, w_down, cotangent):
    hidden_in, cotangent = hidden_in[0], cotangent[0]
    rows, D = hidden_in.shape
    sizes = tuple(lax.axis_size(n) for n in ("fsdp", "context", "tensor"))
    F, C, T = sizes
    c, t = lax.axis_index("context"), lax.axis_index("tensor")
    length = segment_ids.shape[1]
    span = length // C
    hd = w_key.shape[1]
    QW = w_query.shape[1]
    R = w_query.shape[0]
    nh = QW // hd
    start = c * span
    seg_span = lax.dynamic_slice_in_dim(segment_ids[0], start, span, 0)[:, None]
    row_at = start + jnp.arange(span, dtype=jnp.int32)
    first = jnp.sum((segment_ids < seg_span).astype(jnp.int32), axis=1)
    frequency = jnp.exp(
        -((jnp.arange(2 * hd) % (hd // 2)).astype(F32) * (2.0 / hd)) * math.log(10000.0)
    )
    sign = jnp.where(jnp.arange(2 * hd) % hd < hd // 2, -1.0, 1.0)
    angles = (row_at - first).astype(F32)[:, None] * frequency
    cos, sin = jnp.cos(angles), jnp.sin(angles) * sign
    keep = lax.dynamic_slice_in_dim(pad_mask[0], start + t * rows, rows, 0).astype(F32)[:, None]
    g_out = cotangent.astype(F32) * keep
    gains = jnp.concatenate([attn_gain, mlp_gain])[None]
    (n1, q, kv, attn, lse, middle, n2, g_all, w, gain_all, gate_all, up_all, down_all) = forward(
        sizes, hd, hidden_in, segment_ids, seg_span, pad_mask, cos, sin, gains,
        w_query, w_key, w_value, w_out, w_down, g_out.astype(BF), w_gate, w_up,
    )
    gain_one = gain_all[:, 0, :R].reshape(1, D)
    gain_two = gain_all[:, 0, R:].reshape(1, D)
    hidden = hidden_in.astype(F32)
    scale_one = lax.rsqrt(jnp.mean(hidden * hidden, axis=-1, keepdims=True) + EPS)
    scale_two = lax.rsqrt(jnp.mean(middle * middle, axis=-1, keepdims=True) + EPS)
    gate = dot(n2, gate_all)
    up = dot(n2, up_all)
    sig = jax.nn.sigmoid(gate)
    inner = (gate * sig * up).astype(BF)
    block_out = (keep * (middle + rows_sum(dot(inner, down_all, 1, 1)))).astype(BF)
    grad_down = dot(g_all, inner, 0, 0)
    g_inner = dot(g_all, down_all)
    g_gate = (g_inner * up * sig * (1.0 + gate * (1.0 - sig))).astype(BF)
    g_up = (g_inner * gate * sig).astype(BF)
    g_n2 = rows_sum(dot(g_gate, gate_all, 1, 1) + dot(g_up, up_all, 1, 1))
    grad_gate = dot(n2, g_gate, 0, 0)
    grad_up = dot(n2, g_up, 0, 0)
    d_mid, grad_gain_two = norm_back(g_n2, middle, scale_two, gain_two)
    g_mid = g_out + d_mid
    gm_all = rows_gather(g_mid.astype(BF))
    attn = jnp.swapaxes(attn, 0, 1).reshape(span, QW)
    grad_out = dot(gm_all, attn, 0, 0)
    out_t = w[:, QW + 2 * hd:]
    g_attn = dot(gm_all, out_t).astype(BF).reshape(span, nh, hd)
    seg, pad = segment_ids[0], pad_mask[0]
    columns = jnp.arange(length, dtype=jnp.int32)
    allowed = (
        (seg_span == seg[None, :])
        & (columns[None, :] <= row_at[:, None])
        & ((pad[None, :] == 1) | (columns[None, :] == row_at[:, None]))
    )
    key, value = kv[:, :hd], kv[:, hd:]
    scale = hd ** (-0.5)
    scores = jnp.einsum("hqd,td->hqt", q, key, preferred_element_type=F32) * scale
    probs = jnp.exp(jnp.where(allowed[None], scores, NEG) - lse)
    dp = jnp.einsum("qhd,td->hqt", g_attn, value, preferred_element_type=F32)
    delta = jnp.sum(probs * dp, axis=-1, keepdims=True)
    ds = (probs * (dp - delta)).astype(BF)
    g_q = jnp.einsum("hqt,td->qhd", ds, key, preferred_element_type=F32) * scale
    g_k = jnp.einsum("hqt,hqd->td", ds, q, preferred_element_type=F32) * scale
    g_v = jnp.einsum("hqt,qhd->td", probs.astype(BF), g_attn, preferred_element_type=F32)
    g_kv = lax.psum_scatter(
        jnp.concatenate([g_k, g_v], axis=1), "context", scatter_dimension=0, tiled=True
    )
    sin = sin * sign
    g_q = rotate_back(g_q, cos, sin, hd).astype(BF).reshape(span, -1)
    g_k = rotate_back(g_kv[:, None, :hd], cos, sin, hd).astype(BF)[:, 0]
    g_qkv = jnp.concatenate([g_q, g_k, g_kv[:, hd:].astype(BF)], axis=1)
    g_n1 = rows_sum(dot(g_qkv, w[:, :QW + 2 * hd], 1, 1))
    grad_qkv = dot(n1, g_qkv, 0, 0)
    d_hid, grad_gain_one = norm_back(g_n1, hidden, scale_one, gain_one)
    grads = jnp.stack([grad_gain_one, grad_gain_two])
    grad_down = scatter_g(grad_down)
    grad_gate = scatter_g(grad_gate)
    grad_up = scatter_g(grad_up)
    grad_out = scatter_g(grad_out)
    grad_qkv = scatter_g(grad_qkv)
    grads = lax.psum(grads, "tensor")
    grads = lax.psum_scatter(grads, FC, scatter_dimension=1, tiled=True)
    return (
        block_out[None], (g_mid + d_hid)[None], grads[0], grad_qkv[:, :QW],
        grad_qkv[:, QW:QW + hd], grad_qkv[:, QW + hd:], grad_out.T, grads[1],
        grad_gate, grad_up, grad_down.T,
    )


def solution(mesh):
    rows = P("fsdp", ("context", "tensor"), None)
    tail = (P(FC), P(FC, "tensor"), P(FC, "tensor"), P(FC, "tensor"), P("tensor", FC),
            P(FC), P(FC, "tensor"), P(FC, "tensor"), P("tensor", FC))
    in_specs = (rows, P("fsdp", None), P("fsdp", None)) + tail + (rows,)
    out_specs = (rows, rows) + tail
    return jax.shard_map(body, mesh=mesh, in_specs=in_specs, out_specs=out_specs, check_vma=False)
```

```python
import functools
import math

import jax
import jax.numpy as jnp
from jax import lax
from jax.experimental import pallas as pl
from jax.experimental.pallas import tpu as pltpu
from jax.sharding import PartitionSpec as P

EPS = 1e-05
NEG = -1e30
BF = jnp.bfloat16
F32 = jnp.float32
MESH = pl.DeviceIdType.MESH
FC = ("fsdp", "context")


def dot(a, b, ca=1, cb=0):
    return lax.dot_general(a, b, (((ca,), (cb,)), ((), ())), preferred_element_type=F32)


def chunks(total, step):
    return [(at, min(step, total - at)) for at in range(0, total, step)]


class Links:
    def __init__(self, sizes, send_sems, recv_sems):
        self.F, self.C, self.T = sizes
        self.f = lax.axis_index("fsdp")
        self.c = lax.axis_index("context")
        self.t = lax.axis_index("tensor")
        self.h = self.c // 2
        self.core = self.c % 2
        self.H = self.C // 2
        self.send_sems, self.recv_sems = send_sems, recv_sems
        self.used = 0
        self.open = []
        self.sib = (self.f, self.h * 2 + 1 - self.core, self.t)

    def chip(self, df, dh):
        return ((self.f + df) % self.F, ((self.h + dh) % self.H) * 2 + self.core, self.t)

    def block_of(self, df, dh, other=False):
        core = 1 - self.core if other else self.core
        return ((self.f - df) % self.F) * self.C + ((self.h - dh) % self.H) * 2 + core

    def zpeer(self, i):
        return (self.f, self.c, (self.t + i) % self.T)

    def cpeer(self, i):
        return (self.f, (self.c + i) % self.C, self.t)

    def send(self, src, dst, dev):
        n = self.used
        self.used += 1
        copy = pltpu.make_async_remote_copy(
            src_ref=src, dst_ref=dst, send_sem=self.send_sems.at[n],
            recv_sem=self.recv_sems.at[n], device_id=dev, device_id_type=MESH,
        )
        copy.start()
        self.open.append(copy)
        return copy

    def peers(self):
        out = []
        for df in range(self.F):
            for dc in range(self.C):
                if df or dc:
                    out.append(((self.f + df) % self.F, (self.c + dc) % self.C, self.t))
        return out + [self.zpeer(i) for i in range(1, self.T)]

    def barrier(self):
        sem = pltpu.get_barrier_semaphore()
        peers = self.peers()
        for dev in peers:
            pl.semaphore_signal(sem, inc=1, device_id=dev, device_id_type=MESH)
        pl.semaphore_wait(sem, len(peers))

    def finish(self, copies=None):
        for copy in list(self.open) if copies is None else copies:
            copy.wait_send()
            self.open.remove(copy)


class Gather:
    def __init__(self, links, full, rows):
        self.k, self.full, self.rows = links, full, rows

    def part(self, block, half=None):
        if half is None:
            return self.full.at[pl.ds(pl.multiple_of(block * self.rows, self.rows), self.rows)]
        n = self.rows // 2
        return self.full.at[pl.ds(pl.multiple_of(block * self.rows + half * n, n), n)]

    def first(self, own):
        k = self.k
        mine = self.part(k.block_of(0, 0))
        self.line = {}
        for df in range(1, k.F):
            self.line[df, 0] = k.send(own, mine, k.chip(df, 0))
        for dh in range(1, k.H):
            self.line[0, dh] = k.send(own, mine, k.chip(0, dh))
        self.twin = [k.send(own, mine, k.sib)]

    def second(self):
        k = self.k
        self.diag = {}
        for (df, dh), copy in self.line.items():
            copy.wait_recv()
            block = k.block_of(df, dh)
            half = 0 if df else 1
            piece = self.part(block, half)
            if df:
                for eh in range(1, k.H):
                    self.diag[df, eh, half] = k.send(piece, piece, k.chip(0, eh))
            else:
                for ef in range(1, k.F):
                    self.diag[ef, dh, half] = k.send(piece, piece, k.chip(ef, 0))
            whole = self.part(block)
            self.twin.append(k.send(whole, whole, k.sib))

    def third(self):
        k = self.k
        for copy in self.diag.values():
            copy.wait_recv()
        for df in range(1, k.F):
            for dh in range(1, k.H):
                whole = self.part(k.block_of(df, dh))
                self.twin.append(k.send(whole, whole, k.sib))

    def done(self):
        for copy in self.twin:
            copy.wait_recv()


def n_gather(F, H):
    a, b, d = F - 1, H - 1, (F - 1) * (H - 1)
    return a + b + 1 + 2 * d + a + b + d


def forward_kernel(
    sizes, hd,
    hidden_ref, seg_ref, segc_ref, pad_ref, cos_ref, sin_ref, gain_ref, wq_ref, wk_ref, wv_ref,
    wo_ref, wd_ref, gout_ref, wg_ref, wu_ref,
    n1_ref, q_ref, kv_ref, attn_ref, lse_ref, mid_ref, n2_ref, gall_ref, w_ref, gains_ref,
    gate_ref, up_ref, down_ref,
    dt, bias, part_f, part_b, slots, sends, recvs, local,
):
    k = Links(sizes, sends, recvs)
    rows, D = hidden_ref.shape
    R, QW = wq_ref.shape
    FB = wg_ref.shape[1]
    span = n1_ref.shape[0]
    length = seg_ref.shape[1]
    nh = QW // hd
    T = k.T
    mine = k.block_of(0, 0)

    aw = Gather(k, w_ref, R)
    own_w = aw.part(mine)
    own_w[:, :QW] = wq_ref[...]
    own_w[:, QW:QW + 2 * hd] = jnp.concatenate([wk_ref[...], wv_ref[...]], axis=1)
    own_w[:, QW + 2 * hd:] = wo_ref[...].astype(F32).T.astype(BF)
    gains_ref[mine] = gain_ref[...].astype(F32)
    k.barrier()
    own_gain = gains_ref.at[mine]
    gain_copies = [k.send(own_gain, own_gain, dev) for dev in k.peers()[: k.F * k.C - 1]]
    aw.first(own_w)
    gw, uw, dw = Gather(k, gate_ref, R), Gather(k, up_ref, R), Gather(k, down_ref, R)

    hidden = hidden_ref[...].astype(F32)
    scale_one = lax.rsqrt(jnp.mean(hidden * hidden, axis=-1, keepdims=True) + EPS)
    for copy in gain_copies:
        copy.wait_recv()

    def gain_row(which):
        return jnp.concatenate(
            [gains_ref[b][:, which * R:(which + 1) * R] for b in range(k.F * k.C)], axis=1
        )

    at_t = pl.ds(pl.multiple_of(k.t * rows, rows), rows)

    def z_gather(full):
        piece = full.at[at_t]
        return [k.send(piece, piece, k.zpeer(i)) for i in range(1, T)]

    n1_ref[at_t] = (hidden * scale_one * gain_row(0)).astype(BF)
    n1_copies = z_gather(n1_ref)
    dt[...] = wd_ref[...].astype(F32).T.astype(BF)
    local_copies = [
        pltpu.make_async_copy(wg_ref, gw.part(mine), local.at[0]),
        pltpu.make_async_copy(wu_ref, uw.part(mine), local.at[1]),
        pltpu.make_async_copy(dt, dw.part(mine), local.at[2]),
    ]
    for copy in local_copies:
        copy.start()
    seg_span = segc_ref[...]
    row_at = k.c * span + lax.broadcasted_iota(jnp.int32, (span, length), 0)
    column = lax.broadcasted_iota(jnp.int32, (span, length), 1)
    keep = (seg_span == seg_ref[...]) & (column <= row_at) & (
        (pad_ref[...] == 1) | (column == row_at)
    )
    bias[...] = jnp.where(keep, 0.0, NEG)
    aw.second()
    gw.first(wg_ref)
    aw.third()
    aw.done()
    for copy in n1_copies:
        copy.wait_recv()
    gall_ref[at_t] = gout_ref[...]
    g_copies = z_gather(gall_ref)

    cos, sin = cos_ref[...], sin_ref[...]
    lane = lax.broadcasted_iota(jnp.int32, (span, 2 * hd), 1)
    low = (lane % hd) < (hd // 2)

    def turn(x, sin_table):
        swapped = jnp.where(low, pltpu.roll(x, 2 * hd - hd // 2, 1), pltpu.roll(x, hd // 2, 1))
        return x * cos + swapped * sin_table

    n1 = n1_ref[...]
    for n in range(QW // (2 * hd)):
        at = n * 2 * hd
        pre = turn(dot(n1, w_ref[:, at:at + 2 * hd]), sin).astype(BF)
        q_ref[2 * n] = pre[:, :hd]
        q_ref[2 * n + 1] = pre[:, hd:]
    pre = dot(n1, w_ref[:, QW:QW + 2 * hd])
    at_c = pl.ds(pl.multiple_of(k.c * span, span), span)
    kv_ref[at_c] = jnp.where(lane < hd, turn(pre, sin), pre).astype(BF)
    own_kv = kv_ref.at[at_c]
    kv_copies = [k.send(own_kv, own_kv, k.cpeer(i)) for i in range(1, k.C)]
    gw.second()
    uw.first(wu_ref)
    for copy in kv_copies:
        copy.wait_recv()

    @pl.loop(0, nh)
    def _(n):
        scores = dot(q_ref[n], kv_ref[:, :hd], 1, 1) * hd ** (-0.5) + bias[...]
        top = jnp.max(scores, axis=-1, keepdims=True)
        e = jnp.exp(scores - top)
        total = jnp.sum(e, axis=-1, keepdims=True)
        attn_ref[n] = dot((e / total).astype(BF), kv_ref[:, hd:]).astype(BF)
        lse_ref[n] = top + jnp.log(total)

    attn = jnp.concatenate([attn_ref[n] for n in range(nh)], axis=1)

    @pl.loop(0, D // 256)
    def _(n):
        at = pl.ds(pl.multiple_of(n * 256, 256), 256)
        part = dot(attn, w_ref[at, QW + 2 * hd:], 1, 1)
        part_f[:, at] = part
        part_b[:, at] = part.astype(BF)

    part_copies = []
    for i in range(1, T):
        dest = (k.t + i) % T
        src = part_b.at[pl.ds(pl.multiple_of(dest * rows, rows), rows)]
        part_copies.append(k.send(src, slots.at[i - 1], k.zpeer(i)))
    gw.third()
    uw.second()
    dw.first(dt)
    middle = hidden + part_f[at_t]
    for i in range(1, T):
        part_copies[i - 1].wait_recv()
        middle = middle + slots[i - 1].astype(F32)
    mid_ref[...] = middle
    scale_two = lax.rsqrt(jnp.mean(middle * middle, axis=-1, keepdims=True) + EPS)
    n2_ref[at_t] = (middle * scale_two * gain_row(1)).astype(BF)
    n2_copies = z_gather(n2_ref)
    uw.third()
    dw.second()
    dw.third()
    for copy in n2_copies + g_copies:
        copy.wait_recv()
    for w in (gw, uw, dw):
        w.done()
    for copy in local_copies:
        copy.wait()
    k.finish()


def forward(sizes, hd, hidden, seg, seg_span, pad, cos, sin, gains, wq, wk, wv, wo, wd, g_out, wg, wu):
    F, C, T = sizes
    rows, D = hidden.shape
    R, QW = wq.shape
    FB = wg.shape[1]
    span, length, nh = rows * T, seg.shape[1], QW // hd
    vm = pl.BlockSpec(memory_space=pltpu.VMEM)
    hbm = pl.BlockSpec(memory_space=pl.ANY)
    H = C // 2
    n_sems = 4 * n_gather(F, H) + F * C - 1 + 4 * (T - 1) + C - 1
    S = jax.ShapeDtypeStruct
    return pl.pallas_call(
        functools.partial(forward_kernel, sizes, hd),
        out_shape=(
            S((span, D), BF), S((nh, span, hd), BF), S((length, 2 * hd), BF), S((nh, span, hd), BF),
            S((nh, span, 1), F32), S((rows, D), F32), S((span, D), BF), S((span, D), BF),
            S((D, 2 * QW + 2 * hd), BF), S((F * C, 1, 2 * R), F32),
            S((D, FB), BF), S((D, FB), BF), S((D, FB), BF),
        ),
        in_specs=[vm] * 13 + [hbm] * 2,
        out_specs=[vm] * 10 + [hbm] * 3,
        scratch_shapes=[
            pltpu.VMEM((R, FB), BF), pltpu.VMEM((span, length), F32), pltpu.VMEM((span, D), F32),
            pltpu.VMEM((span, D), BF), pltpu.VMEM((T - 1, rows, D), BF),
            pltpu.SemaphoreType.DMA((n_sems,)), pltpu.SemaphoreType.DMA((n_sems,)),
            pltpu.SemaphoreType.DMA((3,)),
        ],
        compiler_params=pltpu.CompilerParams(
            collective_id=0, has_side_effects=True, vmem_limit_bytes=56 * 2**20
        ),
        name="forward",
    )(hidden, seg, seg_span, pad, cos, sin, gains, wq, wk, wv, wo, wd, g_out, wg, wu)


def backward_kernel(
    sizes, hd,
    hidden_ref, seg_ref, segc_ref, pad_ref, cos_ref, sin_ref, keep_ref, n1_ref, q_ref, kv_ref,
    attn_ref, lse_ref, mid_ref, n2_ref, gall_ref, gains_ref, w_hbm, gate_hbm, up_hbm, down_hbm,
    out_ref, hid_ref, gg_ref, sum_down, sum_gate, sum_up, sum_out, sum_qkv,
    w_v, gate_v, up_v, down_v, xt_a, xt_b, inner, g_gate, g_up, gm, bias, part_f, part_b, part2_b,
    slots, slots2, slots3, twin_down, twin_gate, twin_up, twin_out, twin_qkv, g_attn, g_q, g_qkv,
    g_kv, g_kvb, kv_slots, gz, gz_slots, gx, gx_slots, sends, recvs, local,
):
    k = Links(sizes, sends, recvs)
    rows, D = hidden_ref.shape
    T, F, C, H = k.T, k.F, k.C, k.H
    FC_ = F * C
    R = D // FC_
    span = n1_ref.shape[0]
    length = seg_ref.shape[1]
    nh = q_ref.shape[0]
    QW = nh * hd
    QKV = QW + 2 * hd
    FB = gate_v.shape[1]
    scale = hd ** (-0.5)
    loads = [
        pltpu.make_async_copy(src, dst, local.at[i])
        for i, (src, dst) in enumerate(
            ((gate_hbm, gate_v), (up_hbm, up_v), (down_hbm, down_v), (w_hbm, w_v))
        )
    ]
    for copy in loads:
        copy.start()
    k.barrier()
    at_t = pl.ds(pl.multiple_of(k.t * rows, rows), rows)
    n2 = n2_ref[...]
    g_all = gall_ref[...]
    for copy in loads[:3]:
        copy.wait()

    for at, n in chunks(FB, 256):
        gate = dot(n2, gate_v[:, at:at + n])
        up = dot(n2, up_v[:, at:at + n])
        sig = jax.nn.sigmoid(gate)
        inner[:, at:at + n] = (gate * sig * up).astype(BF)
        g_in = dot(g_all, down_v[:, at:at + n])
        g_gate[:, at:at + n] = (g_in * up * sig * (1.0 + gate * (1.0 - sig))).astype(BF)
        g_up[:, at:at + n] = (g_in * gate * sig).astype(BF)

    def z_scatter(src, dst):
        copies = []
        for i in range(1, T):
            dest = (k.t + i) % T
            piece = src.at[pl.ds(pl.multiple_of(dest * rows, rows), rows)]
            copies.append(k.send(piece, dst.at[i - 1], k.zpeer(i)))
        return copies

    def z_gather(full):
        piece = full.at[at_t]
        return [k.send(piece, piece, k.zpeer(i)) for i in range(1, T)]

    @pl.loop(0, D // 256)
    def _(n):
        at = pl.ds(pl.multiple_of(n * 256, 256), 256)
        part = dot(g_gate[...], gate_v[at], 1, 1) + dot(g_up[...], up_v[at], 1, 1)
        part_f[:, at] = part
        part_b[:, at] = part.astype(BF)

    gn2_copies = z_scatter(part_b, slots)
    own_gn2 = part_f[at_t]

    def turn_over(src, dst):
        @pl.loop(0, D // 256)
        def _(n):
            at = pl.ds(pl.multiple_of(n * 256, 256), 256)
            dst[at] = src[:, at].astype(F32).T.astype(BF)

    turn_over(gall_ref, xt_a)
    turn_over(n2_ref, xt_b)

    def block_at(s, core):
        df, dh = s // H, s % H
        b = ((k.f + df) % F) * C + ((k.h + dh) % H) * 2 + core
        return pl.ds(pl.multiple_of(b * R, R), R)

    class Grad:
        def __init__(self, xt, y, width, stage, lanes, twin, out):
            self.xt, self.y, self.width, self.stage = xt, y, width, stage
            self.lanes, self.twin, self.out = lanes, twin, out

        def piece(self, s, core):
            return self.stage.at[block_at(s, core), self.lanes[0]:self.lanes[0] + self.width]

        def first(self):
            @pl.loop(0, F * H)
            def _(s):
                at = block_at(s, 1 - k.core)
                x = self.xt[at]
                for a, n in chunks(self.width, 256):
                    lane = self.lanes[0] + a
                    self.stage[at, lane:lane + n] = dot(x, self.y[:, a:a + n]).astype(BF)

            self.twins = [
                k.send(self.piece(s, 1 - k.core), self.twin.at[s], k.sib) for s in range(F * H)
            ]

        def second(self, sem):
            for copy in self.twins:
                copy.wait_recv()

            @pl.loop(0, F * H)
            def _(s):
                at = block_at(s, k.core)
                x = self.xt[at]
                for a, n in chunks(self.width, 256):
                    lane = self.lanes[0] + a
                    total = dot(x, self.y[:, a:a + n]) + self.twin[s, :, a:a + n].astype(F32)
                    self.stage[at, lane:lane + n] = total.astype(BF)

            self.far = [
                k.send(self.piece(s, k.core), self.out.at[s], k.chip(s // H, s % H))
                for s in range(1, F * H)
            ]
            self.own = pltpu.make_async_copy(self.piece(0, k.core), self.out.at[0], sem)
            self.own.start()

        def done(self):
            for copy in self.far:
                copy.wait_recv()
            self.own.wait()

    @pl.loop(0, D // 256)
    def _(n):
        at = pl.ds(pl.multiple_of(n * 256, 256), 256)
        part = dot(inner[...], down_v[at], 1, 1)
        part_f[:, at] = part
        part2_b[:, at] = part.astype(BF)

    own_two = part_f[at_t]
    down = Grad(xt_a, inner, FB, down_v, (0,), twin_down, sum_down)
    gate_g = Grad(xt_b, g_gate, FB, gate_v, (0,), twin_gate, sum_gate)
    up_g = Grad(xt_b, g_up, FB, up_v, (0,), twin_up, sum_up)
    down.first()
    gate_g.first()
    down.second(local.at[4])
    up_g.first()
    gate_g.second(local.at[5])
    up_g.second(local.at[6])

    def gain_row(which):
        return jnp.concatenate(
            [gains_ref[b][:, which * R:(which + 1) * R] for b in range(FC_)], axis=1
        )

    def norm_back(grad, vectors, gain):
        inv = lax.rsqrt(jnp.mean(vectors * vectors, axis=-1, keepdims=True) + EPS)
        unit = vectors * inv
        weighted = grad * gain
        g_gain = jnp.sum(grad * unit, axis=0, keepdims=True)
        return inv * (weighted - unit * jnp.mean(weighted * unit, axis=-1, keepdims=True)), g_gain

    total = own_gn2
    for i in range(1, T):
        gn2_copies[i - 1].wait_recv()
        total = total + slots[i - 1].astype(F32)
    d_mid, gain_two = norm_back(total, mid_ref[...], gain_row(1))
    g_mid = gall_ref[at_t].astype(F32) + d_mid
    hid_ref[...] = g_mid
    gm[at_t] = g_mid.astype(BF)
    gm_copies = z_gather(gm)

    seg_span = segc_ref[...]
    row_at = k.c * span + lax.broadcasted_iota(jnp.int32, (span, length), 0)
    column = lax.broadcasted_iota(jnp.int32, (span, length), 1)
    keep = (seg_span == seg_ref[...]) & (column <= row_at) & (
        (pad_ref[...] == 1) | (column == row_at)
    )
    bias[...] = jnp.where(keep, 0.0, NEG)
    turn_over(n1_ref, xt_b)
    loads[3].wait()
    for copy in gm_copies:
        copy.wait_recv()
    two_copies = z_scatter(part2_b, slots2)
    turn_over(gm, xt_a)
    gm_rows = gm[...]
    for n in range(nh // 2):
        at = QKV + n * 2 * hd
        pair = dot(gm_rows, w_v[:, at:at + 2 * hd]).astype(BF)
        g_attn[2 * n] = pair[:, :hd]
        g_attn[2 * n + 1] = pair[:, hd:]
    attn = jnp.concatenate([attn_ref[n] for n in range(nh)], axis=1)
    inner[:, :QW] = attn
    out_g = Grad(xt_a, inner, QW, w_v, (QKV,), twin_out, sum_out)
    out_g.first()

    g_kv[...] = jnp.zeros_like(g_kv)

    @pl.loop(0, nh)
    def _(n):
        scores = dot(q_ref[n], kv_ref[:, :hd], 1, 1) * scale + bias[...]
        p = jnp.exp(scores - lse_ref[n])
        dp = dot(g_attn[n], kv_ref[:, hd:], 1, 1)
        delta = jnp.sum(p * dp, axis=-1, keepdims=True)
        ds = (p * (dp - delta)).astype(BF)
        g_q[n] = dot(ds, kv_ref[:, :hd]) * scale
        g_key = dot(ds, q_ref[n], 0, 0) * scale
        g_value = dot(p.astype(BF), g_attn[n], 0, 0)
        g_kv[...] += jnp.concatenate([g_key, g_value], axis=1)

    g_kvb[...] = g_kv[...].astype(BF)
    kv_copies = []
    for i in range(1, C):
        dest = (k.c + i) % C
        piece = g_kvb.at[pl.ds(pl.multiple_of(dest * span, span), span)]
        kv_copies.append(k.send(piece, kv_slots.at[i - 1], k.cpeer(i)))
    out_g.second(local.at[7])
    cos, sin = cos_ref[...], sin_ref[...]
    lane = lax.broadcasted_iota(jnp.int32, (span, 2 * hd), 1)
    low = (lane % hd) < (hd // 2)

    def turn_back(x):
        swapped = jnp.where(low, pltpu.roll(x, 2 * hd - hd // 2, 1), pltpu.roll(x, hd // 2, 1))
        return x * cos - swapped * sin

    for n in range(nh // 2):
        pair = jnp.concatenate([g_q[2 * n], g_q[2 * n + 1]], axis=1)
        g_qkv[:, n * 2 * hd:(n + 1) * 2 * hd] = turn_back(pair).astype(BF)
    own_kv = g_kv[pl.ds(pl.multiple_of(k.c * span, span), span)]
    for i in range(1, C):
        kv_copies[i - 1].wait_recv()
        own_kv = own_kv + kv_slots[i - 1].astype(F32)
    g_qkv[:, QW:] = jnp.where(lane < hd, turn_back(own_kv), own_kv).astype(BF)
    k.finish(gn2_copies)

    @pl.loop(0, D // 256)
    def _(n):
        at = pl.ds(pl.multiple_of(n * 256, 256), 256)
        part = dot(g_qkv[...], w_v[at, :QKV], 1, 1)
        part_f[:, at] = part
        part_b[:, at] = part.astype(BF)

    n1_copies = z_scatter(part_b, slots3)
    qkv_g = Grad(xt_b, g_qkv, QKV, w_v, (0,), twin_qkv, sum_qkv)
    qkv_g.first()
    total = mid_ref[...] + own_two
    for i in range(1, T):
        two_copies[i - 1].wait_recv()
        total = total + slots2[i - 1].astype(F32)
    out_ref[...] = (keep_ref[...] * total).astype(BF)
    qkv_g.second(local.at[8])
    total = part_f[at_t]
    for i in range(1, T):
        n1_copies[i - 1].wait_recv()
        total = total + slots3[i - 1].astype(F32)
    d_hid, gain_one = norm_back(total, hidden_ref[...].astype(F32), gain_row(0))
    hid_ref[...] = hid_ref[...] + d_hid

    for b in range(FC_):
        gz[b] = jnp.concatenate(
            [gain_one[:, b * R:(b + 1) * R], gain_two[:, b * R:(b + 1) * R]], axis=1
        )
    z_copies = [k.send(gz, gz_slots.at[i - 1], k.zpeer(i)) for i in range(1, T)]
    both = gz[...]
    for i in range(1, T):
        z_copies[i - 1].wait_recv()
        both = both + gz_slots[i - 1]
    gx[...] = both
    x_copies = []
    for n, (df, dc) in enumerate((df, dc) for df in range(F) for dc in range(C) if df or dc):
        f, c = (k.f + df) % F, (k.c + dc) % C
        x_copies.append(k.send(gx.at[f * C + c], gx_slots.at[n], (f, c, k.t)))
    both = gx[k.f * C + k.c]
    for n, copy in enumerate(x_copies):
        copy.wait_recv()
        both = both + gx_slots[n]
    gg_ref[...] = both
    for grad in (down, gate_g, up_g, out_g, qkv_g):
        grad.done()
    k.finish()


def backward(sizes, hd, vm_args, hbm_args):
    F, C, T = sizes
    H = C // 2
    hidden, q, n2, kv, gate = vm_args[0], vm_args[8], vm_args[13], vm_args[9], hbm_args[1]
    rows, D = hidden.shape
    FB = gate.shape[1]
    nh, span, _ = q.shape
    length = kv.shape[0]
    QW, QKV = nh * hd, nh * hd + 2 * hd
    R = D // (F * C)
    FH = F * H
    vm = pl.BlockSpec(memory_space=pltpu.VMEM)
    hbm = pl.BlockSpec(memory_space=pl.ANY)
    n_sems = 5 * (T - 1) + 5 * (2 * FH - 1) + C - 1 + F * C - 1
    S = jax.ShapeDtypeStruct
    V = pltpu.VMEM
    return pl.pallas_call(
        functools.partial(backward_kernel, sizes, hd),
        out_shape=(
            S((rows, D), BF), S((rows, D), F32), S((1, 2 * R), F32),
            S((FH, R, FB), BF), S((FH, R, FB), BF), S((FH, R, FB), BF),
            S((FH, R, QW), BF), S((FH, R, QKV), BF),
        ),
        in_specs=[vm] * 16 + [hbm] * 4,
        out_specs=[vm] * 3 + [hbm] * 5,
        scratch_shapes=[
            V((D, QW + QKV), BF), V((D, FB), BF), V((D, FB), BF), V((D, FB), BF),
            V((D, span), BF), V((D, span), BF),
            V((span, FB), BF), V((span, FB), BF), V((span, FB), BF), V((span, D), BF),
            V((span, length), F32), V((span, D), F32), V((span, D), BF), V((span, D), BF),
            V((T - 1, rows, D), BF), V((T - 1, rows, D), BF), V((T - 1, rows, D), BF),
            V((FH, R, FB), BF), V((FH, R, FB), BF), V((FH, R, FB), BF),
            V((FH, R, QW), BF), V((FH, R, QKV), BF),
            V((nh, span, hd), BF), V((nh, span, hd), F32), V((span, QKV), BF),
            V((length, 2 * hd), F32), V((length, 2 * hd), BF), V((C - 1, span, 2 * hd), BF),
            V((F * C, 1, 2 * R), F32), V((T - 1, F * C, 1, 2 * R), F32),
            V((F * C, 1, 2 * R), F32), V((F * C - 1, 1, 2 * R), F32),
            pltpu.SemaphoreType.DMA((n_sems,)), pltpu.SemaphoreType.DMA((n_sems,)),
            pltpu.SemaphoreType.DMA((9,)),
        ],
        compiler_params=pltpu.CompilerParams(
            collective_id=1, has_side_effects=True, vmem_limit_bytes=60 * 2**20
        ),
        name="backward",
    )(*vm_args, *hbm_args)


def body(hidden_in, segment_ids, pad_mask, attn_gain, w_query, w_key, w_value, w_out,
         mlp_gain, w_gate, w_up, w_down, cotangent):
    hidden_in, cotangent = hidden_in[0], cotangent[0]
    rows, D = hidden_in.shape
    sizes = tuple(lax.axis_size(n) for n in ("fsdp", "context", "tensor"))
    F, C, T = sizes
    c, t = lax.axis_index("context"), lax.axis_index("tensor")
    length = segment_ids.shape[1]
    span = length // C
    hd = w_key.shape[1]
    R, QW = w_query.shape
    start = c * span
    seg_span = lax.dynamic_slice_in_dim(segment_ids[0], start, span, 0)[:, None]
    row_at = start + jnp.arange(span, dtype=jnp.int32)
    first = jnp.sum((segment_ids < seg_span).astype(jnp.int32), axis=1)
    frequency = jnp.exp(
        -((jnp.arange(2 * hd) % (hd // 2)).astype(F32) * (2.0 / hd)) * math.log(10000.0)
    )
    sign = jnp.where(jnp.arange(2 * hd) % hd < hd // 2, -1.0, 1.0)
    angles = (row_at - first).astype(F32)[:, None] * frequency
    cos, sin = jnp.cos(angles), jnp.sin(angles) * sign
    keep = lax.dynamic_slice_in_dim(pad_mask[0], start + t * rows, rows, 0).astype(F32)[:, None]
    g_out = (cotangent.astype(F32) * keep).astype(BF)
    gains = jnp.concatenate([attn_gain, mlp_gain])[None]
    (n1, q, kv, attn, lse, middle, n2, g_all, w, gain_all, gate_all, up_all, down_all) = forward(
        sizes, hd, hidden_in, segment_ids, seg_span, pad_mask, cos, sin, gains,
        w_query, w_key, w_value, w_out, w_down, g_out, w_gate, w_up,
    )
    block_out, grad_hidden, gg, s_down, s_gate, s_up, s_out, s_qkv = backward(
        sizes, hd,
        (hidden_in, segment_ids, seg_span, pad_mask, cos, sin, keep, n1, q, kv, attn, lse, middle,
         n2, g_all, gain_all),
        (w, gate_all, up_all, down_all),
    )

    def total(parts):
        return jnp.sum(parts.astype(F32), axis=0)

    grad_qkv = total(s_qkv)
    return (
        block_out[None], grad_hidden[None], gg[0, :R], grad_qkv[:, :QW],
        grad_qkv[:, QW:QW + hd], grad_qkv[:, QW + hd:], total(s_out).T, gg[0, R:],
        total(s_gate), total(s_up), total(s_down).T,
    )


def solution(mesh):
    rows = P("fsdp", ("context", "tensor"), None)
    tail = (P(FC), P(FC, "tensor"), P(FC, "tensor"), P(FC, "tensor"), P("tensor", FC),
            P(FC), P(FC, "tensor"), P(FC, "tensor"), P("tensor", FC))
    in_specs = (rows, P("fsdp", None), P("fsdp", None)) + tail + (rows,)
    out_specs = (rows, rows) + tail
    return jax.shard_map(body, mesh=mesh, in_specs=in_specs, out_specs=out_specs, check_vma=False)
```

```python
import functools
import math

import jax
import jax.numpy as jnp
from jax import lax
from jax.experimental import pallas as pl
from jax.experimental.pallas import tpu as pltpu
from jax.sharding import PartitionSpec as P

EPS = 1e-05
NEG = -1e30
BF = jnp.bfloat16
F32 = jnp.float32
MESH = pl.DeviceIdType.MESH
FC = ("fsdp", "context")


def dot(a, b, ca=1, cb=0):
    return lax.dot_general(a, b, (((ca,), (cb,)), ((), ())), preferred_element_type=F32)


def chunks(total, step):
    return [(at, min(step, total - at)) for at in range(0, total, step)]


def ds(start, size):
    return pl.ds(pl.multiple_of(start, size), size)


class Links:
    def __init__(self, sizes, send_sems, recv_sems):
        self.F, self.C, self.T = sizes
        self.f = lax.axis_index("fsdp")
        self.c = lax.axis_index("context")
        self.t = lax.axis_index("tensor")
        self.h = self.c // 2
        self.core = self.c % 2
        self.H = self.C // 2
        self.send_sems, self.recv_sems = send_sems, recv_sems
        self.used = 0
        self.open = []
        self.sib = (self.f, self.h * 2 + 1 - self.core, self.t)

    def chip(self, df, dh):
        return ((self.f + df) % self.F, ((self.h + dh) % self.H) * 2 + self.core, self.t)

    def block(self, df, dh, core):
        return ((self.f + df) % self.F) * self.C + ((self.h + dh) % self.H) * 2 + core

    def zpeer(self, i):
        return (self.f, self.c, (self.t + i) % self.T)

    def cpeer(self, i):
        return (self.f, (self.c + i) % self.C, self.t)

    def new(self, src, dst, dev, recv=None):
        n = self.used
        self.used += 1
        copy = pltpu.make_async_remote_copy(
            src_ref=src, dst_ref=dst, send_sem=self.send_sems.at[n],
            recv_sem=self.recv_sems.at[n if recv is None else recv],
            device_id=dev, device_id_type=MESH,
        )
        return copy, n

    def start(self, copy, cond=None):
        if cond is None:
            copy.start()
        else:
            pl.when(cond)(copy.start)
        self.open.append((copy, cond))

    def send(self, src, dst, dev):
        copy, _ = self.new(src, dst, dev)
        self.start(copy)
        return copy

    def plane_peers(self):
        return [
            ((self.f + df) % self.F, (self.c + dc) % self.C, self.t)
            for df in range(self.F) for dc in range(self.C) if df or dc
        ]

    def peers(self):
        return self.plane_peers() + [self.zpeer(i) for i in range(1, self.T)]

    def greet(self):
        self.bar = pltpu.get_barrier_semaphore()
        for dev in self.peers():
            pl.semaphore_signal(self.bar, inc=1, device_id=dev, device_id_type=MESH)

    def meet(self):
        pl.semaphore_wait(self.bar, len(self.peers()))

    def finish(self, copies=None):
        wanted = None if copies is None else [id(c) for c in copies]
        left = []
        for copy, cond in self.open:
            if wanted is not None and id(copy) not in wanted:
                left.append((copy, cond))
            elif cond is None:
                copy.wait_send()
            else:
                pl.when(cond)(copy.wait_send)
        self.open = left


class Gather:
    def __init__(self, links, full, rows):
        self.k, self.full, self.rows = links, full, rows

    def part(self, df=0, dh=0, half=None):
        block = self.k.block(-df, -dh, self.k.core)
        if half is None:
            return self.full.at[ds(block * self.rows, self.rows)]
        n = self.rows // 2
        return self.full.at[ds(block * self.rows + half * n, n)]

    def first(self, own):
        k = self.k
        mine = self.part()
        self.line = {}
        for df in range(1, k.F):
            self.line[df, 0] = k.send(own, mine, k.chip(df, 0))
        for dh in range(1, k.H):
            self.line[0, dh] = k.send(own, mine, k.chip(0, dh))
        self.twin = [k.send(own, mine, k.sib)]

    def second(self):
        k = self.k
        self.diag = {}
        for (df, dh), copy in self.line.items():
            copy.wait_recv()
            half = 0 if df else 1
            piece = self.part(df, dh, half)
            if df:
                for eh in range(1, k.H):
                    self.diag[df, eh, half] = k.send(piece, piece, k.chip(0, eh))
            else:
                for ef in range(1, k.F):
                    self.diag[ef, dh, half] = k.send(piece, piece, k.chip(ef, 0))
            whole = self.part(df, dh)
            self.twin.append(k.send(whole, whole, k.sib))

    def third(self):
        k = self.k
        for copy in self.diag.values():
            copy.wait_recv()
        for df in range(1, k.F):
            for dh in range(1, k.H):
                whole = self.part(df, dh)
                self.twin.append(k.send(whole, whole, k.sib))

    def done(self):
        for copy in self.twin:
            copy.wait_recv()

    def sent(self):
        self.k.finish(list(self.line.values()) + list(self.diag.values()) + self.twin)


class ZGather:
    def __init__(self, k, full, rows):
        self.k, self.full, self.rows = k, full, rows
        T = k.T
        piece = full.at[ds(k.t * rows, rows)]
        self.copies = {i: k.new(piece, piece, k.zpeer(i)) for i in range(1, T)}
        for i in [2, 1, 3] if T == 4 else range(1, T):
            cond = None
            if T == 4 and i != 2:
                cond = (k.t < 3) if i == 1 else (k.t > 0)
            k.start(self.copies[i][0], cond)
        self.left = list(range(1, T))

    def relay(self):
        k = self.k
        if k.T != 4:
            return
        self.copies[2][0].wait_recv()
        self.left = [1, 3]
        for at, origin, i in ((2, 0, 3), (1, 3, 1)):
            piece = self.full.at[ds(origin * self.rows, self.rows)]
            copy, _ = k.new(piece, piece, (k.f, k.c, 3 - origin), recv=self.copies[i][1])
            k.start(copy, k.t == at)

    def wait(self):
        for i in self.left:
            self.copies[i][0].wait_recv()


class ZScatter:
    def __init__(self, k, part, slots, middle, rows):
        self.k, self.part, self.slots, self.middle, self.rows = k, part, slots, middle, rows
        T = k.T
        self.line = T == 4
        self.end = (k.t == 0) | (k.t == T - 1)
        if self.line:
            src = part.at[ds((3 - k.t) * rows, rows)]
            self.far, _ = k.new(src, middle, (k.f, k.c, 1 + k.t // 3))
            k.start(self.far, self.end)
        self.copies = {}
        for i in range(1, T):
            src = part.at[ds(((k.t + i) % T) * rows, rows)]
            self.copies[i], _ = k.new(src, slots.at[i - 1], k.zpeer(i))
        if self.line:
            k.start(self.copies[2], self.end)
            k.start(self.copies[1], k.t < 3)
            k.start(self.copies[3], k.t > 0)
        else:
            for i in range(1, T):
                k.start(self.copies[i])

    def relay(self):
        k = self.k
        if not self.line:
            return
        inner = (k.t > 0) & (k.t < 3)

        @pl.when(inner)
        def _():
            self.far.wait_recv()
            at = ds(((k.t + 2) % 4) * self.rows, self.rows)
            both = self.part[at].astype(F32) + self.middle[...].astype(F32)
            self.part[at] = both.astype(BF)
            self.copies[2].start()

        k.open.append((self.copies[2], inner))

    def total(self):
        k = self.k
        for i in range(1, k.T):
            if not self.line or i == 2:
                self.copies[i].wait_recv()
                continue
            there = (k.t > 0) if i == 1 else (k.t < 3)
            pl.when(there)(self.copies[i].wait_recv)

            @pl.when(jnp.logical_not(there))
            def _():
                self.slots[i - 1] = jnp.zeros(self.slots.shape[1:], BF)

        total = self.part[ds(k.t * self.rows, self.rows)].astype(F32)
        for i in range(1, k.T):
            total = total + self.slots[i - 1].astype(F32)
        return total


class Grad:
    def __init__(self, k, xt, y, width, stage, lane, twin, relay, out):
        self.k, self.xt, self.y, self.width, self.stage = k, xt, y, width, stage
        self.lane, self.twin, self.relay, self.out = lane, twin, relay, out
        self.R = xt.shape[0] // (k.F * k.C)

    def rows_of(self, s, core):
        return ds(self.k.block(s // self.k.H, s % self.k.H, core) * self.R, self.R)

    def piece(self, df, dh, core, half=None):
        block = self.k.block(df, dh, core)
        at = ds(block * self.R, self.R)
        if half is not None:
            n = self.R // 2
            at = ds(block * self.R + half * n, n)
        return self.stage.at[at, self.lane:self.lane + self.width]

    def first(self):
        k = self.k

        @pl.loop(0, k.F * k.H)
        def _(s):
            at = self.rows_of(s, 1 - k.core)
            x = self.xt[at]
            for a, n in chunks(self.width, 256):
                self.stage[at, self.lane + a:self.lane + a + n] = dot(x, self.y[:, a:a + n]).astype(BF)

        self.twins = [
            k.send(self.piece(s // k.H, s % k.H, 1 - k.core), self.twin.at[s], k.sib)
            for s in range(k.F * k.H)
        ]

    def second(self, sem):
        k = self.k
        for copy in self.twins:
            copy.wait_recv()

        @pl.loop(0, k.F * k.H)
        def _(s):
            at = self.rows_of(s, k.core)
            x = self.xt[at]
            for a, n in chunks(self.width, 256):
                total = dot(x, self.y[:, a:a + n]) + self.twin[s, :, a:a + n].astype(F32)
                self.stage[at, self.lane + a:self.lane + a + n] = total.astype(BF)

        self.diag = {}
        n = 0
        for df in range(1, k.F):
            for dh in range(1, k.H):
                for half, dev in ((0, k.chip(df, 0)), (1, k.chip(0, dh))):
                    self.diag[df, dh, half] = n, half, k.send(
                        self.piece(df, dh, k.core, half), self.relay.at[n, half], dev
                    )
                n += 1
        self.own = pltpu.make_async_copy(self.piece(0, 0, k.core), self.out.at[0], sem)
        self.own.start()

    def add(self, df, dh, half):
        piece = self.piece(df, dh, self.k.core, half)
        total = piece[...].astype(F32)
        for (ef, eh, other), (n, _, copy) in self.diag.items():
            if other == half and (ef == df or df == 0) and (eh == dh or dh == 0):
                copy.wait_recv()
                total = total + self.relay[n, half].astype(F32)
        piece[...] = total.astype(BF)

    def third(self):
        k = self.k
        self.far = []
        for dh in range(1, k.H):
            if k.F > 1:
                self.add(0, dh, 0)
            self.far.append(k.send(self.piece(0, dh, k.core), self.out.at[k.F - 1 + dh], k.chip(0, dh)))
        for df in range(1, k.F):
            if k.H > 1:
                self.add(df, 0, 1)
            self.far.append(k.send(self.piece(df, 0, k.core), self.out.at[df], k.chip(df, 0)))

    def done(self):
        for copy in self.far:
            copy.wait_recv()
        self.own.wait()


def n_semaphores(F, C, T):
    H = C // 2
    a, b, d = F - 1, H - 1, (F - 1) * (H - 1)
    gather = a + b + 1 + 2 * d + a + b + d
    grad = F * H + 2 * d + a + b
    return 4 * gather + 5 * grad + 2 * (F * C - 1) + 2 * (C - 1) + 9 * (T + 1)


def layer_kernel(
    sizes, hd,
    hidden_ref, seg_ref, pad_ref, ga_ref, gm_ref, wq_ref, wk_ref, wv_ref, wo_ref, wd_ref, cot_ref,
    wg_hbm, wu_hbm,
    out_ref, hid_ref, gg_ref, sum_down, sum_gate, sum_up, sum_out, sum_qkv,
    w_v, gate_v, up_v, down_v, n1_s, n2_s, gall, gm, xt_a, xt_b, inner, g_gate, g_up,
    q_s, attn_s, g_attn, g_qkv, lse_s, kv_s, k_s, v_s, g_kv, g_kvb, kv_slots, bias, cos_s, sin_s,
    padc, part_b, part2_b, slots, slots2, middle_a, middle_b, mid_s,
    twin_down, twin_gate, twin_up, twin_out, twin_qkv,
    relay_down, relay_gate, relay_up, relay_out, relay_qkv,
    gains_s, gz, gz_slots, gx, gx_slots, sends, recvs, local,
):
    k = Links(sizes, sends, recvs)
    T, F, C, H = k.T, k.F, k.C, k.H
    rows, D = hidden_ref.shape
    R, QW = wq_ref.shape
    FB = wg_hbm.shape[1]
    span, length = bias.shape
    nh = QW // hd
    QKV = QW + 2 * hd
    pair = 2 * hd
    scale = hd ** (-0.5)
    at_t = ds(k.t * rows, rows)
    at_c = ds(k.c * span, span)
    k.greet()

    aw, gw, uw, dw = (Gather(k, full, R) for full in (w_v, gate_v, up_v, down_v))
    mine = k.block(0, 0, k.core)
    own_w = aw.part()
    own_w[:, :QW] = wq_ref[...]
    kv_w = jnp.concatenate([wk_ref[...], wv_ref[...]], axis=0)
    own_w[:, QW:QKV] = kv_w.astype(F32).T.astype(BF)
    own_w[:, QKV:] = wo_ref[...].astype(F32).T.astype(BF)
    gains_s[mine] = jnp.concatenate([ga_ref[...], gm_ref[...]], axis=1).astype(F32)
    loads = [
        pltpu.make_async_copy(wg_hbm, gw.part(), local.at[0]),
        pltpu.make_async_copy(wu_hbm, uw.part(), local.at[1]),
    ]
    for copy in loads:
        copy.start()
    k.meet()
    own_gain = gains_s.at[mine]
    gain_copies = [k.send(own_gain, own_gain, dev) for dev in k.plane_peers()]
    aw.first(own_w)

    hidden = hidden_ref[...].astype(F32)
    scale_one = lax.rsqrt(jnp.mean(hidden * hidden, axis=-1, keepdims=True) + EPS)
    hidden = hidden * scale_one
    for copy in gain_copies:
        copy.wait_recv()

    def gain_row(which):
        return jnp.concatenate(
            [gains_s[b][:, which * R:(which + 1) * R] for b in range(F * C)], axis=1
        )

    n1_s[at_t] = (hidden * gain_row(0)).astype(BF)
    n1_gather = ZGather(k, n1_s, rows)
    down_v[ds(mine * R, R)] = wd_ref[...].astype(F32).T.astype(BF)

    def column_of(row):
        return jnp.broadcast_to(row.astype(F32), (8, span)).T[:, :1]

    seg = seg_ref[...].astype(F32)
    seg_col = column_of(seg_ref[:, at_c])
    padc[...] = column_of(pad_ref[:, at_c])
    row_at = k.c * span + lax.broadcasted_iota(jnp.int32, (span, 1), 0)
    column = lax.broadcasted_iota(jnp.int32, (span, length), 1)
    first = jnp.sum(jnp.where(seg < seg_col, 1.0, 0.0), axis=1, keepdims=True)
    lane = lax.broadcasted_iota(jnp.int32, (1, pair), 1)
    frequency = jnp.exp(-((lane % (hd // 2)).astype(F32) * (2.0 / hd)) * math.log(10000.0))
    low = (lane % hd) < (hd // 2)
    angles = (row_at.astype(F32) - first) * frequency
    cos_s[...] = jnp.cos(angles)
    sin_s[...] = jnp.where(low, -1.0, 1.0) * jnp.sin(angles)
    allowed = (seg == seg_col) & (column <= row_at) & ((pad_ref[...] == 1) | (column == row_at))
    bias[...] = jnp.where(allowed, 0.0, NEG)
    keep = padc[at_t]
    gall[at_t] = (cot_ref[...].astype(F32) * keep).astype(BF)

    def swap_halves(x):
        return jnp.where(low, pltpu.roll(x, pair - hd // 2, 1), pltpu.roll(x, hd // 2, 1))

    def turn(x):
        return x * cos_s[...] + swap_halves(x) * sin_s[...]

    def turn_back(x):
        return x * cos_s[...] - swap_halves(x) * sin_s[...]

    aw.second()
    gw.first(wg_hbm)
    n1_gather.relay()
    aw.third()
    n1_gather.wait()
    g_gather = ZGather(k, gall, rows)
    aw.done()

    pre = dot(n1_s[...], w_v[:, QW:QKV])
    kv_s[at_c] = jnp.where(lane < hd, turn(pre), pre).astype(BF)
    own_kv = kv_s.at[at_c]
    kv_copies = [k.send(own_kv, own_kv, k.cpeer(i)) for i in range(1, C)]
    for at, n in chunks(QW, 256):
        pre = dot(n1_s[...], w_v[:, at:at + n])
        for b in range(0, n, pair):
            q_s[:, at + b:at + b + pair] = turn(pre[:, b:b + pair]).astype(BF)
    for copy in kv_copies:
        copy.wait_recv()
    k_s[...] = kv_s[:, :hd]
    v_s[...] = kv_s[:, hd:]
    gw.second()
    uw.first(wu_hbm)
    lse_s[...] = jnp.zeros_like(lse_s)

    @pl.loop(0, nh // 2)
    def _(n):
        at = ds(n * pair, pair)
        two = q_s[:, at] * BF(scale)
        outs = []
        for e in range(2):
            scores = dot(two[:, e * hd:(e + 1) * hd], k_s[...], 1, 1) + bias[...]
            top = jnp.max(scores, axis=-1, keepdims=True)
            weights = jnp.exp(scores - top)
            total = jnp.sum(weights, axis=-1, keepdims=True)
            outs.append(dot((weights * (1.0 / total)).astype(BF), v_s[...]))
            lse_s[...] = jnp.where(lane == 2 * n + e, top + jnp.log(total), lse_s[...])
        attn_s[:, at] = jnp.concatenate(outs, axis=1).astype(BF)

    g_gather.relay()

    @pl.loop(0, D // 256)
    def _(n):
        at = ds(n * 256, 256)
        part_b[:, at] = dot(attn_s[...], w_v[at, QKV:], 1, 1).astype(BF)

    one = ZScatter(k, part_b, slots, middle_a, rows)
    gw.third()
    one.relay()
    uw.second()
    dw.first(dw.part())

    def turn_over(src, dst):
        @pl.loop(0, D // 256)
        def _(n):
            at = ds(n * 256, 256)
            dst[at] = src[:, at].astype(F32).T.astype(BF)

    g_gather.wait()
    turn_over(gall, xt_a)
    mid = hidden_ref[...].astype(F32) + one.total()
    mid_s[...] = mid
    scale_two = lax.rsqrt(jnp.mean(mid * mid, axis=-1, keepdims=True) + EPS)
    n2_s[at_t] = (mid * scale_two * gain_row(1)).astype(BF)
    n2_gather = ZGather(k, n2_s, rows)
    uw.third()
    n2_gather.relay()
    dw.second()
    n2_gather.wait()
    dw.third()
    for weight in (gw, uw, dw):
        weight.done()
    for copy in loads:
        copy.wait()
    k.finish([one.far] * one.line + list(one.copies.values()))

    for at, n in chunks(FB, 256):
        gate = dot(n2_s[...], gate_v[:, at:at + n])
        up = dot(n2_s[...], up_v[:, at:at + n])
        sig = jax.nn.sigmoid(gate)
        inner[:, at:at + n] = (gate * sig * up).astype(BF)
        g_in = dot(gall[...], down_v[:, at:at + n])
        g_gate[:, at:at + n] = (g_in * up * sig * (1.0 + gate * (1.0 - sig))).astype(BF)
        g_up[:, at:at + n] = (g_in * gate * sig).astype(BF)

    @pl.loop(0, D // 256)
    def _(n):
        at = ds(n * 256, 256)
        part = dot(g_gate[...], gate_v[at], 1, 1) + dot(g_up[...], up_v[at], 1, 1)
        part_b[:, at] = part.astype(BF)

    two = ZScatter(k, part_b, slots, middle_a, rows)
    for weight in (aw, gw, uw, dw):
        weight.sent()
    down_g = Grad(k, xt_a, inner, FB, gate_v, 0, twin_down, relay_down, sum_down)
    gate_g = Grad(k, xt_b, g_gate, FB, up_v, 0, twin_gate, relay_gate, sum_gate)
    up_g = Grad(k, xt_b, g_up, FB, down_v, 0, twin_up, relay_up, sum_up)
    down_g.first()
    turn_over(n2_s, xt_b)
    gate_g.first()
    down_g.second(local.at[2])
    two.relay()

    @pl.loop(0, D // 256)
    def _(n):
        at = ds(n * 256, 256)
        part2_b[:, at] = dot(inner[...], down_v[at], 1, 1).astype(BF)

    up_g.first()
    gate_g.second(local.at[3])
    up_g.second(local.at[4])
    down_g.third()

    def norm_back(grad, vectors, gain):
        inv = lax.rsqrt(jnp.mean(vectors * vectors, axis=-1, keepdims=True) + EPS)
        unit = vectors * inv
        weighted = grad * gain
        g_gain = jnp.sum(grad * unit, axis=0, keepdims=True)
        return inv * (weighted - unit * jnp.mean(weighted * unit, axis=-1, keepdims=True)), g_gain

    d_mid, gain_two = norm_back(two.total(), mid_s[...], gain_row(1))
    g_mid = gall[at_t].astype(F32) + d_mid
    hid_ref[...] = g_mid
    gm[at_t] = g_mid.astype(BF)
    gm_gather = ZGather(k, gm, rows)
    gate_g.third()
    turn_over(n1_s, xt_b)
    gm_gather.relay()
    up_g.third()
    gm_gather.wait()
    branch = ZScatter(k, part2_b, slots2, middle_b, rows)
    for at, n in chunks(QW, 256):
        g_attn[:, at:at + n] = dot(gm[...], w_v[:, QKV + at:QKV + at + n]).astype(BF)
    g_kv[...] = jnp.zeros_like(g_kv)

    @pl.loop(0, nh // 2)
    def _(n):
        at = ds(n * pair, pair)
        two_q = q_s[:, at] * BF(scale)
        two_g = g_attn[:, at]
        g_qs, g_kvs = [], []
        for e in range(2):
            q_one, g_one = two_q[:, e * hd:(e + 1) * hd], two_g[:, e * hd:(e + 1) * hd]
            lse = jnp.sum(jnp.where(lane == 2 * n + e, lse_s[...], 0.0), axis=1, keepdims=True)
            p = jnp.exp(dot(q_one, k_s[...], 1, 1) + bias[...] - lse)
            dp = dot(g_one, v_s[...], 1, 1)
            delta = jnp.sum(p * dp, axis=-1, keepdims=True)
            d_scores = (p * (dp - delta)).astype(BF)
            g_qs.append(dot(d_scores, k_s[...]) * scale)
            g_kvs.append(
                jnp.concatenate([dot(d_scores, q_one, 0, 0), dot(p.astype(BF), g_one, 0, 0)], axis=1)
            )
        g_qkv[:, at] = turn_back(jnp.concatenate(g_qs, axis=1)).astype(BF)
        g_kv[...] += g_kvs[0] + g_kvs[1]

    g_kvb[...] = g_kv[...].astype(BF)
    kv_copies = []
    for i in range(1, C):
        piece = g_kvb.at[ds(((k.c + i) % C) * span, span)]
        kv_copies.append(k.send(piece, kv_slots.at[i - 1], k.cpeer(i)))
    branch.relay()
    turn_over(gm, xt_a)
    out_g = Grad(k, xt_a, attn_s, QW, w_v, QKV, twin_out, relay_out, sum_out)
    out_g.first()
    own_kv = g_kv[at_c]
    for i in range(1, C):
        kv_copies[i - 1].wait_recv()
        own_kv = own_kv + kv_slots[i - 1].astype(F32)
    g_qkv[:, QW:] = jnp.where(lane < hd, turn_back(own_kv), own_kv).astype(BF)
    k.finish([two.far] * two.line + list(two.copies.values()))

    @pl.loop(0, D // 256)
    def _(n):
        at = ds(n * 256, 256)
        part_b[:, at] = dot(g_qkv[...], w_v[at, :QKV], 1, 1).astype(BF)

    last = ZScatter(k, part_b, slots, middle_a, rows)
    out_g.second(local.at[5])
    qkv_g = Grad(k, xt_b, g_qkv, QKV, w_v, 0, twin_qkv, relay_qkv, sum_qkv)
    qkv_g.first()
    last.relay()
    qkv_g.second(local.at[6])
    out_ref[...] = (padc[at_t] * (mid_s[...] + branch.total())).astype(BF)
    out_g.third()
    qkv_g.third()
    d_hid, gain_one = norm_back(last.total(), hidden_ref[...].astype(F32), gain_row(0))
    hid_ref[...] = hid_ref[...] + d_hid

    for b in range(F * C):
        gz[b] = jnp.concatenate(
            [gain_one[:, b * R:(b + 1) * R], gain_two[:, b * R:(b + 1) * R]], axis=1
        )
    z_copies = [k.send(gz, gz_slots.at[i - 1], k.zpeer(i)) for i in range(1, T)]
    both = gz[...]
    for i in range(1, T):
        z_copies[i - 1].wait_recv()
        both = both + gz_slots[i - 1]
    gx[...] = both
    x_copies = []
    for n, dev in enumerate(k.plane_peers()):
        x_copies.append(k.send(gx.at[dev[0] * C + dev[1]], gx_slots.at[n], dev))
    both = gx[mine]
    for n, copy in enumerate(x_copies):
        copy.wait_recv()
        both = both + gx_slots[n]
    gg_ref[...] = both
    for grad in (down_g, gate_g, up_g, out_g, qkv_g):
        grad.done()
    k.finish()


def layer(sizes, hd, hidden, seg, pad, ga, gm, wq, wk, wv, wo, wd, cot, wg, wu):
    F, C, T = sizes
    H = C // 2
    rows, D = hidden.shape
    R, QW = wq.shape
    FB = wg.shape[1]
    span, length, QKV = rows * T, seg.shape[1], QW + 2 * hd
    vm = pl.BlockSpec(memory_space=pltpu.VMEM)
    hbm = pl.BlockSpec(memory_space=pl.ANY)
    n_sems = n_semaphores(F, C, T)
    S = jax.ShapeDtypeStruct
    V = pltpu.VMEM
    FH, lines, diag = F * H, F + H - 1, max(1, (F - 1) * (H - 1))
    widths = (FB, FB, FB, QW, QKV)
    return pl.pallas_call(
        functools.partial(layer_kernel, sizes, hd),
        out_shape=(
            S((rows, D), BF), S((rows, D), F32), S((1, 2 * R), F32),
            *[S((lines, R, n), BF) for n in widths],
        ),
        in_specs=[vm] * 11 + [hbm] * 2,
        out_specs=[vm] * 3 + [hbm] * 5,
        scratch_shapes=[
            V((D, QW + QKV), BF), V((D, FB), BF), V((D, FB), BF), V((D, FB), BF),
            V((span, D), BF), V((span, D), BF), V((span, D), BF), V((span, D), BF),
            V((D, span), BF), V((D, span), BF),
            V((span, FB), BF), V((span, FB), BF), V((span, FB), BF),
            V((span, QW), BF), V((span, QW), BF), V((span, QW), BF), V((span, QKV), BF),
            V((span, 2 * hd), F32), V((length, 2 * hd), BF), V((length, hd), BF), V((length, hd), BF),
            V((length, 2 * hd), F32), V((length, 2 * hd), BF), V((C - 1, span, 2 * hd), BF),
            V((span, length), F32), V((span, 2 * hd), F32), V((span, 2 * hd), F32), V((span, 1), F32),
            V((span, D), BF), V((span, D), BF), V((T - 1, rows, D), BF), V((T - 1, rows, D), BF),
            V((rows, D), BF), V((rows, D), BF), V((rows, D), F32),
            *[V((FH, R, n), BF) for n in widths],
            *[V((diag, 2, R // 2, n), BF) for n in widths],
            V((F * C, 1, 2 * R), F32), V((F * C, 1, 2 * R), F32), V((T - 1, F * C, 1, 2 * R), F32),
            V((F * C, 1, 2 * R), F32), V((F * C - 1, 1, 2 * R), F32),
            pltpu.SemaphoreType.DMA((n_sems,)), pltpu.SemaphoreType.DMA((n_sems,)),
            pltpu.SemaphoreType.DMA((7,)),
        ],
        compiler_params=pltpu.CompilerParams(
            collective_id=0, has_side_effects=True, vmem_limit_bytes=62 * 2**20
        ),
        name="layer",
    )(hidden, seg, pad, ga, gm, wq, wk, wv, wo, wd, cot, wg, wu)


def body(hidden_in, segment_ids, pad_mask, attn_gain, w_query, w_key, w_value, w_out,
         mlp_gain, w_gate, w_up, w_down, cotangent):
    sizes = tuple(lax.axis_size(n) for n in ("fsdp", "context", "tensor"))
    hd = w_key.shape[1]
    R, QW = w_query.shape
    block_out, grad_hidden, gg, s_down, s_gate, s_up, s_out, s_qkv = layer(
        sizes, hd, hidden_in[0], segment_ids, pad_mask, attn_gain[None], mlp_gain[None],
        w_query, w_key.T, w_value.T, w_out, w_down, cotangent[0], w_gate, w_up,
    )

    def total(parts):
        return jnp.sum(parts.astype(F32), axis=0)

    grad_qkv = total(s_qkv)
    return (
        block_out[None], grad_hidden[None], gg[0, :R], grad_qkv[:, :QW],
        grad_qkv[:, QW:QW + hd], grad_qkv[:, QW + hd:], total(s_out).T, gg[0, R:],
        total(s_gate), total(s_up), total(s_down).T,
    )


def solution(mesh):
    rows = P("fsdp", ("context", "tensor"), None)
    tail = (P(FC), P(FC, "tensor"), P(FC, "tensor"), P(FC, "tensor"), P("tensor", FC),
            P(FC), P(FC, "tensor"), P(FC, "tensor"), P("tensor", FC))
    in_specs = (rows, P("fsdp", None), P("fsdp", None)) + tail + (rows,)
    out_specs = (rows, rows) + tail
    return jax.shard_map(body, mesh=mesh, in_specs=in_specs, out_specs=out_specs, check_vma=False)
```

```python
import functools
import math

import jax
import jax.numpy as jnp
from jax import lax
from jax.experimental import pallas as pl
from jax.experimental.pallas import tpu as pltpu
from jax.sharding import PartitionSpec as P

EPS = 1e-05
NEG = -1e30
DOC = 512
BF = jnp.bfloat16
F32 = jnp.float32
MESH = pl.DeviceIdType.MESH
FC = ("fsdp", "context")


def dot(a, b, ca=1, cb=0):
    return lax.dot_general(a, b, (((ca,), (cb,)), ((), ())), preferred_element_type=F32)


def chunks(total, step):
    return [(at, min(step, total - at)) for at in range(0, total, step)]


def ds(start, size):
    return pl.ds(pl.multiple_of(start, size), size)


class Links:
    def __init__(self, sizes, send_sems, recv_sems):
        self.F, self.C, self.T = sizes
        self.f = lax.axis_index("fsdp")
        self.c = lax.axis_index("context")
        self.t = lax.axis_index("tensor")
        self.h = self.c // 2
        self.core = self.c % 2
        self.H = self.C // 2
        self.send_sems, self.recv_sems = send_sems, recv_sems
        self.used = 0
        self.open = []
        self.sib = (self.f, self.h * 2 + 1 - self.core, self.t)

    def chip(self, df, dh):
        return ((self.f + df) % self.F, ((self.h + dh) % self.H) * 2 + self.core, self.t)

    def block(self, df, dh, core):
        return ((self.f + df) % self.F) * self.C + ((self.h + dh) % self.H) * 2 + core

    def zpeer(self, i):
        return (self.f, self.c, (self.t + i) % self.T)

    def cpeer(self, i):
        return (self.f, (self.c + i) % self.C, self.t)

    def new(self, src, dst, dev, recv=None):
        n = self.used
        self.used += 1
        copy = pltpu.make_async_remote_copy(
            src_ref=src, dst_ref=dst, send_sem=self.send_sems.at[n],
            recv_sem=self.recv_sems.at[n if recv is None else recv],
            device_id=dev, device_id_type=MESH,
        )
        return copy, n

    def start(self, copy, cond=None):
        if cond is None:
            copy.start()
        else:
            pl.when(cond)(copy.start)
        self.open.append((copy, cond))

    def send(self, src, dst, dev):
        copy, _ = self.new(src, dst, dev)
        self.start(copy)
        return copy

    def plane_peers(self):
        return [
            ((self.f + df) % self.F, (self.c + dc) % self.C, self.t)
            for df in range(self.F) for dc in range(self.C) if df or dc
        ]

    def peers(self):
        return self.plane_peers() + [self.zpeer(i) for i in range(1, self.T)]

    def greet(self):
        self.bar = pltpu.get_barrier_semaphore()
        for dev in self.peers():
            pl.semaphore_signal(self.bar, inc=1, device_id=dev, device_id_type=MESH)

    def meet(self):
        pl.semaphore_wait(self.bar, len(self.peers()))

    def finish(self, copies=None):
        wanted = None if copies is None else [id(c) for c in copies]
        left = []
        for copy, cond in self.open:
            if wanted is not None and id(copy) not in wanted:
                left.append((copy, cond))
            elif cond is None:
                copy.wait_send()
            else:
                pl.when(cond)(copy.wait_send)
        self.open = left


class Gather:
    def __init__(self, links, full, rows):
        self.k, self.full, self.rows = links, full, rows

    def part(self, df=0, dh=0, half=None):
        block = self.k.block(-df, -dh, self.k.core)
        if half is None:
            return self.full.at[ds(block * self.rows, self.rows)]
        n = self.rows // 2
        return self.full.at[ds(block * self.rows + half * n, n)]

    def first(self, own):
        k = self.k
        mine = self.part()
        self.line = {}
        for df in range(1, k.F):
            self.line[df, 0] = k.send(own, mine, k.chip(df, 0))
        for dh in range(1, k.H):
            self.line[0, dh] = k.send(own, mine, k.chip(0, dh))
        self.twin = [k.send(own, mine, k.sib)]

    def second(self):
        k = self.k
        self.diag = {}
        for (df, dh), copy in self.line.items():
            copy.wait_recv()
            half = 0 if df else 1
            piece = self.part(df, dh, half)
            if df:
                for eh in range(1, k.H):
                    self.diag[df, eh, half] = k.send(piece, piece, k.chip(0, eh))
            else:
                for ef in range(1, k.F):
                    self.diag[ef, dh, half] = k.send(piece, piece, k.chip(ef, 0))
            whole = self.part(df, dh)
            self.twin.append(k.send(whole, whole, k.sib))

    def third(self):
        k = self.k
        for copy in self.diag.values():
            copy.wait_recv()
        for df in range(1, k.F):
            for dh in range(1, k.H):
                whole = self.part(df, dh)
                self.twin.append(k.send(whole, whole, k.sib))

    def done(self):
        for copy in self.twin:
            copy.wait_recv()

    def sent(self):
        self.k.finish(list(self.line.values()) + list(self.diag.values()) + self.twin)


class ZGather:
    def __init__(self, k, full, rows, own=None):
        self.k, self.full, self.rows = k, full, rows
        T = k.T
        piece = full.at[ds(k.t * rows, rows)]
        own = piece if own is None else own
        self.copies = {i: k.new(own, piece, k.zpeer(i)) for i in range(1, T)}
        for i in [2, 1, 3] if T == 4 else range(1, T):
            cond = None
            if T == 4 and i != 2:
                cond = (k.t < 3) if i == 1 else (k.t > 0)
            k.start(self.copies[i][0], cond)
        self.left = list(range(1, T))
        self.relays = []

    def relay(self):
        k = self.k
        if k.T != 4:
            return
        self.copies[2][0].wait_recv()
        self.left = [1, 3]
        for at, origin, i in ((2, 0, 3), (1, 3, 1)):
            piece = self.full.at[ds(origin * self.rows, self.rows)]
            copy, _ = k.new(piece, piece, (k.f, k.c, 3 - origin), recv=self.copies[i][1])
            k.start(copy, k.t == at)
            self.relays.append(copy)

    def sent(self):
        self.k.finish([c for c, _ in self.copies.values()] + self.relays)

    def wait(self):
        for i in self.left:
            self.copies[i][0].wait_recv()


class ZScatter:
    def __init__(self, k, part, slots, middle, rows):
        self.k, self.part, self.slots, self.middle, self.rows = k, part, slots, middle, rows
        T = k.T
        self.line = T == 4
        self.end = (k.t == 0) | (k.t == T - 1)
        if self.line:
            src = part.at[ds((3 - k.t) * rows, rows)]
            self.far, _ = k.new(src, middle, (k.f, k.c, 1 + k.t // 3))
            k.start(self.far, self.end)
        self.copies = {}
        for i in range(1, T):
            src = part.at[ds(((k.t + i) % T) * rows, rows)]
            self.copies[i], _ = k.new(src, slots.at[i - 1], k.zpeer(i))
        if self.line:
            k.start(self.copies[2], self.end)
            k.start(self.copies[1], k.t < 3)
            k.start(self.copies[3], k.t > 0)
        else:
            for i in range(1, T):
                k.start(self.copies[i])

    def relay(self):
        k = self.k
        if not self.line:
            return
        inner = (k.t > 0) & (k.t < 3)

        @pl.when(inner)
        def _():
            self.far.wait_recv()
            at = ds(((k.t + 2) % 4) * self.rows, self.rows)
            both = self.part[at].astype(F32) + self.middle[...].astype(F32)
            self.part[at] = both.astype(BF)
            self.copies[2].start()

        k.open.append((self.copies[2], inner))

    def total(self):
        k = self.k
        for i in range(1, k.T):
            if not self.line or i == 2:
                self.copies[i].wait_recv()
                continue
            there = (k.t > 0) if i == 1 else (k.t < 3)
            pl.when(there)(self.copies[i].wait_recv)

            @pl.when(jnp.logical_not(there))
            def _():
                self.slots[i - 1] = jnp.zeros(self.slots.shape[1:], BF)

        total = self.part[ds(k.t * self.rows, self.rows)].astype(F32)
        for i in range(1, k.T):
            total = total + self.slots[i - 1].astype(F32)
        return total


class Grad:
    def __init__(self, k, xt, y, width, stage, twin, relay, out):
        self.k, self.xt, self.y, self.width, self.stage = k, xt, y, width, stage
        self.twin, self.relay, self.out = twin, relay, out
        self.R = xt.shape[0] // (k.F * k.C)

    def rows_of(self, s, core):
        return ds(self.k.block(s // self.k.H, s % self.k.H, core) * self.R, self.R)

    def piece(self, df, dh, half=None):
        s = df * self.k.H + dh
        if half is None:
            return self.twin.at[s]
        n = self.R // 2
        return self.twin.at[s, half * n:(half + 1) * n]

    def first(self):
        k = self.k

        @pl.loop(0, k.F * k.H)
        def _(s):
            x = self.xt[self.rows_of(s, 1 - k.core)]
            to = self.stage(s)
            for a, n in chunks(self.width, 256):
                to[:, a:a + n] = dot(x, self.y[:, a:a + n]).astype(BF)

        self.twins = [k.send(self.stage(s), self.twin.at[s], k.sib) for s in range(k.F * k.H)]

    def second(self, sem):
        k = self.k
        for copy in self.twins:
            copy.wait_recv()

        @pl.loop(0, k.F * k.H)
        def _(s):
            x = self.xt[self.rows_of(s, k.core)]
            for a, n in chunks(self.width, 256):
                total = dot(x, self.y[:, a:a + n]) + self.twin[s, :, a:a + n].astype(F32)
                self.twin[s, :, a:a + n] = total.astype(BF)

        self.diag = {}
        n = 0
        for df in range(1, k.F):
            for dh in range(1, k.H):
                for half, dev in ((0, k.chip(df, 0)), (1, k.chip(0, dh))):
                    self.diag[df, dh, half] = n, half, k.send(
                        self.piece(df, dh, half), self.relay.at[n, half], dev
                    )
                n += 1
        self.own = pltpu.make_async_copy(self.piece(0, 0), self.out.at[0], sem)
        self.own.start()

    def add(self, df, dh, half):
        piece = self.piece(df, dh, half)
        total = piece[...].astype(F32)
        for (ef, eh, other), (n, _, copy) in self.diag.items():
            if other == half and (ef == df or df == 0) and (eh == dh or dh == 0):
                copy.wait_recv()
                total = total + self.relay[n, half].astype(F32)
        piece[...] = total.astype(BF)

    def third(self):
        k = self.k
        self.far = []
        for dh in range(1, k.H):
            if k.F > 1:
                self.add(0, dh, 0)
            self.far.append(k.send(self.piece(0, dh), self.out.at[k.F - 1 + dh], k.chip(0, dh)))
        for df in range(1, k.F):
            if k.H > 1:
                self.add(df, 0, 1)
            self.far.append(k.send(self.piece(df, 0), self.out.at[df], k.chip(df, 0)))

    def done(self):
        for copy in self.far:
            copy.wait_recv()
        self.own.wait()


def n_semaphores(F, C, T):
    H = C // 2
    a, b, d = F - 1, H - 1, (F - 1) * (H - 1)
    gather = a + b + 1 + 2 * d + a + b + d
    grad = F * H + 2 * d + a + b
    return 4 * gather + 5 * grad + 2 * (F * C - 1) + 2 * (C - 1) + 9 * (T + 1)


def layer_kernel(
    sizes, hd,
    hidden_ref, seg_ref, pad_ref, ga_ref, gm_ref, wq_ref, wk_ref, wv_ref, wo_ref, wd_ref, cot_ref,
    wg_hbm, wu_hbm,
    out_ref, hid_ref, gg_ref, sum_down, sum_gate, sum_up, sum_out, sum_qkv,
    w_v, gate_v, up_v, down_v, n1_s, n2_s, gall, gm, xt_a, xt_b, inner, g_gate, g_up,
    q_s, attn_s, g_attn, g_qkv, lse_s, kv_s, k_s, v_s, g_kv, g_kvb, kv_slots, bias, cos_s, sin_s,
    padc, part_b, part2_b, slots, slots2, middle_a, middle_b, mid_s,
    twin_down, twin_gate, twin_up, twin_out, twin_qkv,
    relay_down, relay_gate, relay_up, relay_out, relay_qkv,
    gains_s, gz, gz_slots, gx, gx_slots, sends, recvs, local,
):
    k = Links(sizes, sends, recvs)
    T, F, C, H = k.T, k.F, k.C, k.H
    rows, D = hidden_ref.shape
    R, QW = wq_ref.shape
    FB = wg_hbm.shape[1]
    span, length = bias.shape[0], seg_ref.shape[1]
    nh = QW // hd
    QKV = QW + 2 * hd
    pair = 2 * hd
    scale = hd ** (-0.5)
    at_t = ds(k.t * rows, rows)
    at_c = ds(k.c * span, span)
    k.greet()

    aw, gw, uw, dw = (Gather(k, full, R) for full in (w_v, gate_v, up_v, down_v))
    mine = k.block(0, 0, k.core)
    own_w = aw.part()
    own_w[:, :QW] = wq_ref[...]
    kv_w = jnp.concatenate([wk_ref[...], wv_ref[...]], axis=0)
    own_w[:, QW:QKV] = kv_w.astype(F32).T.astype(BF)
    own_w[:, QKV:] = wo_ref[...].astype(F32).T.astype(BF)
    gains_s[mine, :, :R] = ga_ref[...].astype(F32).reshape(1, R)
    gains_s[mine, :, R:] = gm_ref[...].astype(F32).reshape(1, R)
    loads = [
        pltpu.make_async_copy(wg_hbm, gw.part(), local.at[0]),
        pltpu.make_async_copy(wu_hbm, uw.part(), local.at[1]),
    ]
    for copy in loads:
        copy.start()
    k.meet()
    h_gather = ZGather(k, gm, rows, hidden_ref)
    gm[at_t] = hidden_ref[...]
    own_gain = gains_s.at[mine]
    gain_copies = [k.send(own_gain, own_gain, dev) for dev in k.plane_peers()]
    aw.first(own_w)

    def gain_row(which):
        return jnp.concatenate(
            [gains_s[b][:, which * R:(which + 1) * R] for b in range(F * C)], axis=1
        )

    down_v[ds(mine * R, R)] = wd_ref[...].astype(F32).T.astype(BF)

    def column_of(row):
        return jnp.broadcast_to(row.astype(F32), (8, span)).T[:, :1]

    seg = seg_ref[...].astype(F32)
    seg_col = column_of(seg_ref[:, at_c])
    win = bias.shape[1]
    win_at = jnp.maximum(k.c * span + span - win, 0)
    at_w = pl.ds(pl.multiple_of(win_at, span), win)
    padc[...] = column_of(pad_ref[:, at_c])
    row_at = k.c * span + lax.broadcasted_iota(jnp.int32, (span, 1), 0)
    column = win_at + lax.broadcasted_iota(jnp.int32, (span, win), 1)
    first = jnp.sum(jnp.where(seg < seg_col, 1.0, 0.0), axis=1, keepdims=True)
    lane = lax.broadcasted_iota(jnp.int32, (1, pair), 1)
    frequency = jnp.exp(-((lane % (hd // 2)).astype(F32) * (2.0 / hd)) * math.log(10000.0))
    low = (lane % hd) < (hd // 2)
    angles = (row_at.astype(F32) - first) * frequency
    cos_s[...] = jnp.cos(angles)
    sin_s[...] = jnp.where(low, -1.0, 1.0) * jnp.sin(angles)
    allowed = (seg_ref[:, at_w].astype(F32) == seg_col) & (column <= row_at) & (
        (pad_ref[:, at_w] == 1) | (column == row_at)
    )
    bias[...] = jnp.where(allowed, 0.0, NEG)
    keep = padc[at_t]
    gall[at_t] = (cot_ref[...].astype(F32) * keep).astype(BF)

    def swap_halves(x):
        return jnp.where(low, pltpu.roll(x, pair - hd // 2, 1), pltpu.roll(x, hd // 2, 1))

    def turn(x):
        return x * cos_s[...] + swap_halves(x) * sin_s[...]

    def turn_back(x):
        return x * cos_s[...] - swap_halves(x) * sin_s[...]

    aw.second()
    gw.first(wg_hbm)
    h_gather.relay()
    aw.third()
    for copy in gain_copies:
        copy.wait_recv()
    gain_one_row = gain_row(0)
    h_gather.wait()

    @pl.loop(0, T)
    def _(n):
        at = ds(n * rows, rows)
        h = gm[at].astype(F32)
        inv = lax.rsqrt(jnp.mean(h * h, axis=-1, keepdims=True) + EPS)
        n1_s[at] = (h * inv * gain_one_row).astype(BF)

    g_gather = ZGather(k, gall, rows)
    aw.done()

    pre = dot(n1_s[...], w_v[:, QW:QKV])
    kv_s[at_c] = jnp.where(lane < hd, turn(pre), pre).astype(BF)
    own_kv = kv_s.at[at_c]
    kv_copies = [k.send(own_kv, own_kv, k.cpeer(i)) for i in range(1, C)]
    for at, n in chunks(QW, 256):
        pre = dot(n1_s[...], w_v[:, at:at + n])
        for b in range(0, n, pair):
            q_s[:, at + b:at + b + pair] = turn(pre[:, b:b + pair]).astype(BF)
    for copy in kv_copies:
        copy.wait_recv()
    k_s[...] = kv_s[at_w, :hd]
    v_s[...] = kv_s[at_w, hd:]
    gw.second()
    uw.first(wu_hbm)
    lse_s[...] = jnp.zeros_like(lse_s)

    @pl.loop(0, nh // 2)
    def _(n):
        at = ds(n * pair, pair)
        two = q_s[:, at] * BF(scale)
        outs = []
        for e in range(2):
            scores = dot(two[:, e * hd:(e + 1) * hd], k_s[...], 1, 1) + bias[...]
            top = jnp.max(scores, axis=-1, keepdims=True)
            weights = jnp.exp(scores - top)
            total = jnp.sum(weights, axis=-1, keepdims=True)
            outs.append(dot((weights * (1.0 / total)).astype(BF), v_s[...]))
            lse_s[...] = jnp.where(lane == 2 * n + e, top + jnp.log(total), lse_s[...])
        attn_s[:, at] = jnp.concatenate(outs, axis=1).astype(BF)

    g_gather.relay()

    @pl.loop(0, D // 256)
    def _(n):
        at = ds(n * 256, 256)
        part_b[:, at] = dot(attn_s[...], w_v[at, QKV:], 1, 1).astype(BF)

    h_gather.sent()
    one = ZScatter(k, part_b, slots, middle_a, rows)
    gw.third()
    one.relay()
    uw.second()
    dw.first(dw.part())

    def turn_over(src, dst):
        @pl.loop(0, D // 256)
        def _(n):
            at = ds(n * 256, 256)
            dst[at] = src[:, at].astype(F32).T.astype(BF)

    g_gather.wait()
    turn_over(gall, xt_a)
    mid = hidden_ref[...].astype(F32) + one.total()
    mid_s[...] = mid
    scale_two = lax.rsqrt(jnp.mean(mid * mid, axis=-1, keepdims=True) + EPS)
    n2_s[at_t] = (mid * scale_two * gain_row(1)).astype(BF)
    n2_gather = ZGather(k, n2_s, rows)
    uw.third()
    n2_gather.relay()
    gw.done()
    uw.done()
    for copy in loads:
        copy.wait()
    n2_gather.wait()

    for at, n in chunks(FB, 256):
        gate = dot(n2_s[...], gate_v[:, at:at + n])
        up = dot(n2_s[...], up_v[:, at:at + n])
        sig = jax.nn.sigmoid(gate)
        inner[:, at:at + n] = (gate * sig * up).astype(BF)
        g_gate[:, at:at + n] = (up * sig * (1.0 + gate * (1.0 - sig))).astype(BF)
        g_up[:, at:at + n] = (gate * sig).astype(BF)

    down_g = Grad(k, xt_a, inner, FB, lambda s: twin_up.at[s], twin_down, relay_down, sum_down)
    down_g.first()
    dw.second()
    turn_over(n2_s, xt_b)
    down_g.second(local.at[2])
    k.finish(down_g.twins)
    dw.third()
    dw.done()
    for at, n in chunks(FB, 256):
        g_in = dot(gall[...], down_v[:, at:at + n])
        g_gate[:, at:at + n] = (g_in * g_gate[:, at:at + n].astype(F32)).astype(BF)
        g_up[:, at:at + n] = (g_in * g_up[:, at:at + n].astype(F32)).astype(BF)

    k.finish([one.far] * one.line + list(one.copies.values()))

    @pl.loop(0, D // 256)
    def _(n):
        at = ds(n * 256, 256)
        part = dot(g_gate[...], gate_v[at], 1, 1) + dot(g_up[...], up_v[at], 1, 1)
        part_b[:, at] = part.astype(BF)

    two = ZScatter(k, part_b, slots, middle_a, rows)
    for weight in (aw, gw, uw, dw):
        weight.sent()

    def spare(room, lane, width):
        return lambda s: room.at[ds(s * R, R), lane:lane + width]

    gate_g = Grad(k, xt_b, g_gate, FB, spare(gate_v, 0, FB), twin_gate, relay_gate, sum_gate)
    up_g = Grad(k, xt_b, g_up, FB, spare(up_v, 0, FB), twin_up, relay_up, sum_up)
    gate_g.first()
    up_g.first()
    two.relay()
    gate_g.second(local.at[3])
    up_g.second(local.at[4])
    down_g.third()

    @pl.loop(0, D // 256)
    def _(n):
        at = ds(n * 256, 256)
        part2_b[:, at] = dot(inner[...], down_v[at], 1, 1).astype(BF)

    def norm_back(grad, vectors, gain):
        inv = lax.rsqrt(jnp.mean(vectors * vectors, axis=-1, keepdims=True) + EPS)
        unit = vectors * inv
        weighted = grad * gain
        g_gain = jnp.sum(grad * unit, axis=0, keepdims=True)
        return inv * (weighted - unit * jnp.mean(weighted * unit, axis=-1, keepdims=True)), g_gain

    d_mid, gain_two = norm_back(two.total(), mid_s[...], gain_row(1))
    g_mid = gall[at_t].astype(F32) + d_mid
    hid_ref[...] = g_mid
    gm[at_t] = g_mid.astype(BF)
    gm_gather = ZGather(k, gm, rows)
    gate_g.third()
    turn_over(n1_s, xt_b)
    gm_gather.relay()
    gm_gather.wait()
    branch = ZScatter(k, part2_b, slots2, middle_b, rows)
    for at, n in chunks(QW, 256):
        g_attn[:, at:at + n] = dot(gm[...], w_v[:, QKV + at:QKV + at + n]).astype(BF)
    g_kv[...] = jnp.zeros_like(g_kv)

    @pl.loop(0, nh // 2)
    def _(n):
        at = ds(n * pair, pair)
        two_q = q_s[:, at] * BF(scale)
        two_g = g_attn[:, at]
        g_qs, g_kvs = [], []
        for e in range(2):
            q_one, g_one = two_q[:, e * hd:(e + 1) * hd], two_g[:, e * hd:(e + 1) * hd]
            lse = jnp.sum(jnp.where(lane == 2 * n + e, lse_s[...], 0.0), axis=1, keepdims=True)
            p = jnp.exp(dot(q_one, k_s[...], 1, 1) + bias[...] - lse)
            dp = dot(g_one, v_s[...], 1, 1)
            delta = jnp.sum(p * dp, axis=-1, keepdims=True)
            d_scores = (p * (dp - delta)).astype(BF)
            g_qs.append(dot(d_scores, k_s[...]) * scale)
            g_kvs.append(
                jnp.concatenate([dot(d_scores, q_one, 0, 0), dot(p.astype(BF), g_one, 0, 0)], axis=1)
            )
        g_qkv[:, at] = turn_back(jnp.concatenate(g_qs, axis=1)).astype(BF)
        g_kv[at_w] += g_kvs[0] + g_kvs[1]

    g_kvb[...] = g_kv[...].astype(BF)
    kv_copies = []
    for i in range(1, C):
        piece = g_kvb.at[ds(((k.c + i) % C) * span, span)]
        kv_copies.append(k.send(piece, kv_slots.at[i - 1], k.cpeer(i)))
    branch.relay()
    up_g.third()
    turn_over(gm, xt_a)
    out_g = Grad(k, xt_a, attn_s, QW, spare(w_v, QKV, QW), twin_out, relay_out, sum_out)
    out_g.first()
    own_kv = g_kv[at_c]
    for i in range(1, C):
        kv_copies[i - 1].wait_recv()
        own_kv = own_kv + kv_slots[i - 1].astype(F32)
    g_qkv[:, QW:] = jnp.where(lane < hd, turn_back(own_kv), own_kv).astype(BF)
    k.finish([two.far] * two.line + list(two.copies.values()))

    @pl.loop(0, D // 256)
    def _(n):
        at = ds(n * 256, 256)
        part_b[:, at] = dot(g_qkv[...], w_v[at, :QKV], 1, 1).astype(BF)

    last = ZScatter(k, part_b, slots, middle_a, rows)
    out_g.second(local.at[5])
    qkv_g = Grad(k, xt_b, g_qkv, QKV, spare(w_v, 0, QKV), twin_qkv, relay_qkv, sum_qkv)
    qkv_g.first()
    last.relay()
    qkv_g.second(local.at[6])
    out_ref[...] = (padc[at_t] * (mid_s[...] + branch.total())).astype(BF)
    out_g.third()
    qkv_g.third()
    d_hid, gain_one = norm_back(last.total(), hidden_ref[...].astype(F32), gain_row(0))
    hid_ref[...] = hid_ref[...] + d_hid

    for b in range(F * C):
        gz[b] = jnp.concatenate(
            [gain_one[:, b * R:(b + 1) * R], gain_two[:, b * R:(b + 1) * R]], axis=1
        )
    z_copies = [k.send(gz, gz_slots.at[i - 1], k.zpeer(i)) for i in range(1, T)]
    both = gz[...]
    for i in range(1, T):
        z_copies[i - 1].wait_recv()
        both = both + gz_slots[i - 1]
    gx[...] = both
    x_copies = []
    for n, dev in enumerate(k.plane_peers()):
        x_copies.append(k.send(gx.at[dev[0] * C + dev[1]], gx_slots.at[n], dev))
    both = gx[mine]
    for n, copy in enumerate(x_copies):
        copy.wait_recv()
        both = both + gx_slots[n]
    gg_ref[...] = both
    for grad in (down_g, gate_g, up_g, out_g, qkv_g):
        grad.done()
    k.finish()


def layer(sizes, hd, hidden, seg, pad, ga, gm, wq, wk, wv, wo, wd, cot, wg, wu):
    F, C, T = sizes
    H = C // 2
    rows, D = hidden.shape
    R, QW = wq.shape
    FB = wg.shape[1]
    span, length, QKV = rows * T, seg.shape[1], QW + 2 * hd
    vm = pl.BlockSpec(memory_space=pltpu.VMEM)
    hbm = pl.BlockSpec(memory_space=pl.ANY)
    win = min(length, span + -(-DOC // span) * span)
    n_sems = n_semaphores(F, C, T)
    S = jax.ShapeDtypeStruct
    V = pltpu.VMEM
    FH, lines, diag = F * H, F + H - 1, max(1, (F - 1) * (H - 1))
    widths = (FB, FB, FB, QW, QKV)
    return pl.pallas_call(
        functools.partial(layer_kernel, sizes, hd),
        out_shape=(
            S((rows, D), BF), S((rows, D), F32), S((1, 2 * R), F32),
            *[S((lines, R, n), BF) for n in widths],
        ),
        in_specs=[vm] * 11 + [hbm] * 2,
        out_specs=[vm] * 3 + [hbm] * 5,
        scratch_shapes=[
            V((D, QW + QKV), BF), V((D, FB), BF), V((D, FB), BF), V((D, FB), BF),
            V((span, D), BF), V((span, D), BF), V((span, D), BF), V((span, D), BF),
            V((D, span), BF), V((D, span), BF),
            V((span, FB), BF), V((span, FB), BF), V((span, FB), BF),
            V((span, QW), BF), V((span, QW), BF), V((span, QW), BF), V((span, QKV), BF),
            V((span, 2 * hd), F32), V((length, 2 * hd), BF), V((win, hd), BF), V((win, hd), BF),
            V((length, 2 * hd), F32), V((length, 2 * hd), BF), V((C - 1, span, 2 * hd), BF),
            V((span, win), F32), V((span, 2 * hd), F32), V((span, 2 * hd), F32), V((span, 1), F32),
            V((span, D), BF), V((span, D), BF), V((T - 1, rows, D), BF), V((T - 1, rows, D), BF),
            V((rows, D), BF), V((rows, D), BF), V((rows, D), F32),
            *[V((FH, R, n), BF) for n in widths],
            *[V((diag, 2, R // 2, n), BF) for n in widths],
            V((F * C, 1, 2 * R), F32), V((F * C, 1, 2 * R), F32), V((T - 1, F * C, 1, 2 * R), F32),
            V((F * C, 1, 2 * R), F32), V((F * C - 1, 1, 2 * R), F32),
            pltpu.SemaphoreType.DMA((n_sems,)), pltpu.SemaphoreType.DMA((n_sems,)),
            pltpu.SemaphoreType.DMA((7,)),
        ],
        compiler_params=pltpu.CompilerParams(
            collective_id=0, has_side_effects=True, vmem_limit_bytes=62 * 2**20
        ),
        name="layer",
    )(hidden, seg, pad, ga, gm, wq, wk, wv, wo, wd, cot, wg, wu)


def final_kernel(
    hd, out_ref, hid_ref, down_ref, gate_ref, up_ref, wo_ref, qkv_ref,
    block_out, grad_hidden, g_query, g_key, g_value, g_out, g_gate, g_up, g_down,
):
    def total(ref):
        return sum(ref[i].astype(F32) for i in range(ref.shape[0]))

    QW = g_query.shape[1]
    block_out[...] = out_ref[...]
    grad_hidden[...] = hid_ref[...]
    qkv = total(qkv_ref)
    g_query[...] = qkv[:, :QW]
    kv = qkv[:, QW:].T
    g_key[...] = kv[:hd]
    g_value[...] = kv[hd:]
    g_out[...] = total(wo_ref).T
    g_gate[...] = total(gate_ref)
    g_up[...] = total(up_ref)
    g_down[...] = total(down_ref).T


def final(hd, block_out, grad_hidden, s_down, s_gate, s_up, s_out, s_qkv):
    L, R, FB = s_gate.shape
    QW = s_out.shape[2]
    rows, D = block_out.shape
    steps = R // 128 if R % 128 == 0 else 1
    r = R // steps
    S = jax.ShapeDtypeStruct

    def parts(x):
        return pl.BlockSpec((L, r, x.shape[2]), lambda i: (0, i, 0))

    def tall(n):
        return pl.BlockSpec((r, n), lambda i: (i, 0))

    def wide(n):
        return pl.BlockSpec((n, r), lambda i: (0, i))

    acts = pl.BlockSpec((rows // steps, D), lambda i: (i, 0))
    return pl.pallas_call(
        functools.partial(final_kernel, hd),
        grid=(steps,),
        out_shape=(
            S((rows, D), BF), S((rows, D), F32), S((R, QW), F32), S((hd, R), F32), S((hd, R), F32),
            S((QW, R), F32), S((R, FB), F32), S((R, FB), F32), S((FB, R), F32),
        ),
        in_specs=[acts, acts] + [parts(x) for x in (s_down, s_gate, s_up, s_out, s_qkv)],
        out_specs=[acts, acts, tall(QW), wide(hd), wide(hd), wide(QW), tall(FB), tall(FB), wide(FB)],
        compiler_params=pltpu.CompilerParams(vmem_limit_bytes=48 * 2**20),
        name="final",
    )(block_out, grad_hidden, s_down, s_gate, s_up, s_out, s_qkv)


def body(hidden_in, segment_ids, pad_mask, attn_gain, w_query, w_key, w_value, w_out,
         mlp_gain, w_gate, w_up, w_down, cotangent):
    sizes = tuple(lax.axis_size(n) for n in ("fsdp", "context", "tensor"))
    hd, R = w_key.shape[1], w_query.shape[0]
    block_out, grad_hidden, gg, *parts = layer(
        sizes, hd, hidden_in[0], segment_ids, pad_mask, attn_gain, mlp_gain,
        w_query, w_key.T, w_value.T, w_out, w_down, cotangent[0], w_gate, w_up,
    )
    block_out, grad_hidden, g_query, g_key, g_value, g_out, g_gate, g_up, g_down = final(
        hd, block_out, grad_hidden, *parts
    )
    return (
        block_out[None], grad_hidden[None], gg[0, :R], g_query, g_key.T, g_value.T, g_out, gg[0, R:],
        g_gate, g_up, g_down,
    )


def solution(mesh):
    rows = P("fsdp", ("context", "tensor"), None)
    tail = (P(FC), P(FC, "tensor"), P(FC, "tensor"), P(FC, "tensor"), P("tensor", FC),
            P(FC), P(FC, "tensor"), P(FC, "tensor"), P("tensor", FC))
    in_specs = (rows, P("fsdp", None), P("fsdp", None)) + tail + (rows,)
    out_specs = (rows, rows) + tail
    return jax.shard_map(body, mesh=mesh, in_specs=in_specs, out_specs=out_specs, check_vma=False)
```

```python
import functools
import math

import jax
import jax.numpy as jnp
from jax import lax
from jax.experimental import pallas as pl
from jax.experimental.pallas import tpu as pltpu
from jax.sharding import PartitionSpec as P

EPS = 1e-05
NEG = -1e30
DOC = 512
BF = jnp.bfloat16
F32 = jnp.float32
MESH = pl.DeviceIdType.MESH
FC = ("fsdp", "context")


def dot(a, b, ca=1, cb=0):
    return lax.dot_general(a, b, (((ca,), (cb,)), ((), ())), preferred_element_type=F32)


def chunks(total, step):
    return [(at, min(step, total - at)) for at in range(0, total, step)]


def ds(start, size):
    return pl.ds(pl.multiple_of(start, size), size)


class Links:
    def __init__(self, sizes, send_sems, recv_sems):
        self.F, self.C, self.T = sizes
        self.f = lax.axis_index("fsdp")
        self.c = lax.axis_index("context")
        self.t = lax.axis_index("tensor")
        self.h = self.c // 2
        self.core = self.c % 2
        self.H = self.C // 2
        self.send_sems, self.recv_sems = send_sems, recv_sems
        self.used = 0
        self.open = []
        self.sib = (self.f, self.h * 2 + 1 - self.core, self.t)

    def chip(self, df, dh):
        return ((self.f + df) % self.F, ((self.h + dh) % self.H) * 2 + self.core, self.t)

    def block(self, df, dh, core):
        return ((self.f + df) % self.F) * self.C + ((self.h + dh) % self.H) * 2 + core

    def zpeer(self, i):
        return (self.f, self.c, (self.t + i) % self.T)

    def cpeer(self, i):
        return (self.f, (self.c + i) % self.C, self.t)

    def new(self, src, dst, dev, recv=None):
        n = self.used
        self.used += 1
        copy = pltpu.make_async_remote_copy(
            src_ref=src, dst_ref=dst, send_sem=self.send_sems.at[n],
            recv_sem=self.recv_sems.at[n if recv is None else recv],
            device_id=dev, device_id_type=MESH,
        )
        return copy, n

    def start(self, copy, cond=None):
        if cond is None:
            copy.start()
        else:
            pl.when(cond)(copy.start)
        self.open.append((copy, cond))

    def send(self, src, dst, dev):
        copy, _ = self.new(src, dst, dev)
        self.start(copy)
        return copy

    def plane_peers(self):
        return [
            ((self.f + df) % self.F, (self.c + dc) % self.C, self.t)
            for df in range(self.F) for dc in range(self.C) if df or dc
        ]

    def peers(self):
        return self.plane_peers() + [self.zpeer(i) for i in range(1, self.T)]

    def greet(self):
        self.bar = pltpu.get_barrier_semaphore()
        for dev in self.peers():
            pl.semaphore_signal(self.bar, inc=1, device_id=dev, device_id_type=MESH)

    def meet(self):
        pl.semaphore_wait(self.bar, len(self.peers()))

    def finish(self, copies=None):
        wanted = None if copies is None else [id(c) for c in copies]
        left = []
        for copy, cond in self.open:
            if wanted is not None and id(copy) not in wanted:
                left.append((copy, cond))
            elif cond is None:
                copy.wait_send()
            else:
                pl.when(cond)(copy.wait_send)
        self.open = left


class Gather:
    def __init__(self, links, full, rows):
        self.k, self.full, self.rows, self.early = links, full, rows, []

    def part(self, df=0, dh=0, half=None, size=None, start=0):
        block = self.k.block(-df, -dh, self.k.core)
        if size is not None:
            at = pl.multiple_of(block * self.rows + start, self.rows // 4)
            return self.full.at[pl.ds(at, size)]
        if half is None:
            return self.full.at[ds(block * self.rows, self.rows)]
        n = self.rows // 2
        return self.full.at[ds(block * self.rows + half * n, n)]

    def first(self, own, along="fc"):
        k = self.k
        mine = self.part()
        if "f" in along:
            self.line = {}
            for df in range(1, k.F):
                self.line[df, 0] = k.send(own, mine, k.chip(df, 0))
            self.twin = [k.send(own, mine, k.sib)]
        if "c" in along:
            for dh in range(1, k.H):
                self.line[0, dh] = k.send(own, mine, k.chip(0, dh))
        n = self.rows // 4
        if "1" in along:
            self.early = [
                k.send(own.at[:n], self.part(0, 0, None, n, 0), k.chip(0, dh)) for dh in range(1, k.H)
            ]
        if "2" in along:
            for dh in range(1, k.H):
                self.line[0, dh] = k.send(own.at[n:], self.part(0, 0, None, 3 * n, n), k.chip(0, dh))

    def second(self):
        k = self.k
        self.diag = {}
        for copy in self.early:
            copy.wait_recv()
        for (df, dh), copy in self.line.items():
            copy.wait_recv()
            half = 0 if df else 1
            piece = self.part(df, dh, half)
            if df:
                for eh in range(1, k.H):
                    self.diag[df, eh, half] = k.send(piece, piece, k.chip(0, eh))
            else:
                for ef in range(1, k.F):
                    self.diag[ef, dh, half] = k.send(piece, piece, k.chip(ef, 0))
            whole = self.part(df, dh)
            self.twin.append(k.send(whole, whole, k.sib))

    def third(self):
        k = self.k
        for copy in self.diag.values():
            copy.wait_recv()
        for df in range(1, k.F):
            for dh in range(1, k.H):
                whole = self.part(df, dh)
                self.twin.append(k.send(whole, whole, k.sib))

    def done(self):
        for copy in self.twin:
            copy.wait_recv()

    def sent(self):
        self.k.finish(self.early + list(self.line.values()) + list(self.diag.values()) + self.twin)


class ZGather:
    def __init__(self, k, full, rows, own=None):
        self.k, self.full, self.rows = k, full, rows
        T = k.T
        piece = full.at[ds(k.t * rows, rows)]
        own = piece if own is None else own
        self.copies = {i: k.new(own, piece, k.zpeer(i)) for i in range(1, T)}
        for i in [2, 1, 3] if T == 4 else range(1, T):
            cond = None
            if T == 4 and i != 2:
                cond = (k.t < 3) if i == 1 else (k.t > 0)
            k.start(self.copies[i][0], cond)
        self.left = list(range(1, T))
        self.relays = []
        self.order = [2, 1, 3] if T == 4 else list(range(1, T))

    def relay(self):
        k = self.k
        if k.T != 4:
            return
        self.copies[2][0].wait_recv()
        self.left = [1, 3]
        for at, origin, i in ((2, 0, 3), (1, 3, 1)):
            piece = self.full.at[ds(origin * self.rows, self.rows)]
            copy, _ = k.new(piece, piece, (k.f, k.c, 3 - origin), recv=self.copies[i][1])
            k.start(copy, k.t == at)
            self.relays.append(copy)

    def sent(self):
        self.k.finish([c for c, _ in self.copies.values()] + self.relays)

    def wait(self):
        for i in self.left:
            self.copies[i][0].wait_recv()

    def arrival(self, i):
        if self.k.T != 4:
            self.copies[i][0].wait_recv()
            return i
        if i == 2:
            return i
        at_first = self.k.t == 0
        pl.when(at_first)(self.copies[4 - i][0].wait_recv)
        pl.when(jnp.logical_not(at_first))(self.copies[i][0].wait_recv)
        return jnp.where(at_first, 4 - i, i)


class ZScatter:
    def __init__(self, k, part, slots, middle, rows):
        self.k, self.part, self.slots, self.middle, self.rows = k, part, slots, middle, rows
        T = k.T
        self.line = T == 4
        self.end = (k.t == 0) | (k.t == T - 1)
        if self.line:
            src = part.at[ds((3 - k.t) * rows, rows)]
            self.far, _ = k.new(src, middle, (k.f, k.c, 1 + k.t // 3))
            k.start(self.far, self.end)
        self.copies = {}
        for i in range(1, T):
            src = part.at[ds(((k.t + i) % T) * rows, rows)]
            self.copies[i], _ = k.new(src, slots.at[i - 1], k.zpeer(i))
        if self.line:
            k.start(self.copies[2], self.end)
            k.start(self.copies[1], k.t < 3)
            k.start(self.copies[3], k.t > 0)
        else:
            for i in range(1, T):
                k.start(self.copies[i])

    def relay(self):
        k = self.k
        if not self.line:
            return
        inner = (k.t > 0) & (k.t < 3)

        @pl.when(inner)
        def _():
            self.far.wait_recv()
            at = ds(((k.t + 2) % 4) * self.rows, self.rows)
            both = self.part[at].astype(F32) + self.middle[...].astype(F32)
            self.part[at] = both.astype(BF)
            self.copies[2].start()

        k.open.append((self.copies[2], inner))

    def total(self):
        k = self.k
        for i in range(1, k.T):
            if not self.line or i == 2:
                self.copies[i].wait_recv()
                continue
            there = (k.t > 0) if i == 1 else (k.t < 3)
            pl.when(there)(self.copies[i].wait_recv)

            @pl.when(jnp.logical_not(there))
            def _():
                self.slots[i - 1] = jnp.zeros(self.slots.shape[1:], BF)

        total = self.part[ds(k.t * self.rows, self.rows)].astype(F32)
        for i in range(1, k.T):
            total = total + self.slots[i - 1].astype(F32)
        return total


class Grad:
    def __init__(self, k, xt, y, width, stage, twin, relay, out):
        self.k, self.xt, self.y, self.width, self.stage = k, xt, y, width, stage
        self.twin, self.relay, self.out = twin, relay, out
        self.R = xt.shape[0] // (k.F * k.C)

    def rows_of(self, s, core):
        return ds(self.k.block(s // self.k.H, s % self.k.H, core) * self.R, self.R)

    def piece(self, df, dh, half=None):
        s = df * self.k.H + dh
        if half is None:
            return self.twin.at[s]
        n = self.R // 2
        return self.twin.at[s, half * n:(half + 1) * n]

    def first(self):
        k = self.k

        @pl.loop(0, k.F * k.H)
        def _(s):
            x = self.xt[self.rows_of(s, 1 - k.core)]
            to = self.stage(s)
            for a, n in chunks(self.width, 256):
                to[:, a:a + n] = dot(x, self.y[:, a:a + n]).astype(BF)

        self.twins = [k.send(self.stage(s), self.twin.at[s], k.sib) for s in range(k.F * k.H)]

    def second(self, sem):
        k = self.k
        for copy in self.twins:
            copy.wait_recv()

        @pl.loop(0, k.F * k.H)
        def _(s):
            x = self.xt[self.rows_of(s, k.core)]
            for a, n in chunks(self.width, 256):
                total = dot(x, self.y[:, a:a + n]) + self.twin[s, :, a:a + n].astype(F32)
                self.twin[s, :, a:a + n] = total.astype(BF)

        self.diag, self.far = {}, []
        n = 0
        for df in range(1, k.F):
            for dh in range(1, k.H):
                for half, dev in ((0, k.chip(df, 0)), (1, k.chip(0, dh))):
                    self.diag[df, dh, half] = n, half, k.send(
                        self.piece(df, dh, half), self.relay.at[n, half], dev
                    )
                n += 1
        self.own = pltpu.make_async_copy(self.piece(0, 0), self.out.at[0], sem)
        self.own.start()

    def direct(self, along, half):
        k = self.k
        n = self.R // 2
        at = slice(half * n, half * n + n)
        if along == "c":
            for dh in range(1, k.H):
                to = self.out.at[k.F - 1 + dh, at]
                self.far.append(k.send(self.piece(0, dh, half), to, k.chip(0, dh)))
        else:
            for df in range(1, k.F):
                self.far.append(k.send(self.piece(df, 0, half), self.out.at[df, at], k.chip(df, 0)))

    def add(self, df, dh, half):
        piece = self.piece(df, dh, half)
        total = piece[...].astype(F32)
        for (ef, eh, other), (n, _, copy) in self.diag.items():
            if other == half and (ef == df or df == 0) and (eh == dh or dh == 0):
                copy.wait_recv()
                total = total + self.relay[n, half].astype(F32)
        piece[...] = total.astype(BF)

    def third(self, along="fc"):
        k = self.k
        if "f" in along:
            for df in range(1, k.F):
                if k.H > 1:
                    self.add(df, 0, 1)
            self.direct("f", 1)
        if "c" in along:
            for dh in range(1, k.H):
                if k.F > 1:
                    self.add(0, dh, 0)
            self.direct("c", 0)

    def done(self):
        for copy in self.far:
            copy.wait_recv()
        self.own.wait()


def n_semaphores(F, C, T):
    H = C // 2
    a, b, d = F - 1, H - 1, (F - 1) * (H - 1)
    gather = a + b + 1 + 2 * d + a + b + d
    grad = F * H + 2 * d + 2 * (a + b)
    return 5 * gather + b + 5 * grad + 2 * (F * C - 1) + 2 * (C - 1) + 9 * (T + 1)


def layer_kernel(
    sizes, hd,
    seg_ref, pad_ref, ga_ref, gm_ref,
    hidden_hbm, wq_hbm, wk_hbm, wv_hbm, wo_hbm, wd_hbm, cot_hbm, wg_hbm, wu_hbm,
    out_ref, hid_ref, gg_ref, sum_down, sum_gate, sum_up, sum_out, sum_qkv,
    w_v, wo_v, gate_v, up_v, down_v, h_s, n1_s, n2_s, gall, gm, xt_a, xt_b, inner, g_gate, g_up,
    qt_s, attn_s, g_qkv, lse_s, kv_s, k_s, v_s, kt_s, vt_s, g_kv, g_kvb, kv_slots, bias, cos_s, sin_s,
    inv_s, gain_s,
    padc, part_b, part2_b, slots, slots2, middle_a, middle_b, mid_s,
    twin_down, twin_gate, twin_up, twin_out, twin_qkv,
    relay_down, relay_gate, relay_up, relay_out, relay_qkv,
    gains_s, gz, gz_slots, gx, gx_slots, hidden_ref, kvw_ref, wo_ref, wd_ref, cot_ref, sends, recvs, local,
):
    k = Links(sizes, sends, recvs)
    T, F, C, H = k.T, k.F, k.C, k.H
    rows, D = hidden_ref.shape
    R, QW = wq_hbm.shape
    FB = wg_hbm.shape[1]
    span, length = gall.shape[0], seg_ref.shape[1]
    nh = QW // hd
    QKV = QW + 2 * hd
    pair = 2 * hd
    scale = hd ** (-0.5)
    at_t = ds(k.t * rows, rows)
    at_c = ds(k.c * span, span)
    k.greet()

    aw, ow, gw, uw, dw = (Gather(k, full, R) for full in (w_v, wo_v, gate_v, up_v, down_v))
    mine = k.block(0, 0, k.core)
    own_w, own_o = aw.part(), ow.part()
    loads = [
        pltpu.make_async_copy(src, dst, local.at[n])
        for n, (src, dst) in enumerate((
            (wk_hbm, kvw_ref.at[:hd]), (wv_hbm, kvw_ref.at[hd:]), (wo_hbm, wo_ref),
            (wq_hbm, own_w.at[:, :QW]), (hidden_hbm, hidden_ref), (hidden_hbm, h_s.at[at_t]),
            (wd_hbm, wd_ref), (cot_hbm, cot_ref), (wg_hbm, gw.part()), (wu_hbm, uw.part()),
        ))
    ]
    for copy in loads:
        copy.start()
    gains_s[mine, :, :R] = ga_ref[...].astype(F32).reshape(1, R)
    gains_s[mine, :, R:] = gm_ref[...].astype(F32).reshape(1, R)
    for copy in loads[:4]:
        copy.wait()
    own_w[:, QW:] = kvw_ref[...].astype(F32).T.astype(BF)
    own_o[...] = wo_ref[...].astype(F32).T.astype(BF)
    k.meet()
    h_gather = ZGather(k, h_s, rows, hidden_hbm)
    own_gain = gains_s.at[mine]
    gain_copies = [k.send(own_gain, own_gain, dev) for dev in k.plane_peers()]
    aw.first(own_w)
    ow.first(own_o)

    def gain_row(which):
        return jnp.concatenate(
            [gains_s[b][:, which * R:(which + 1) * R] for b in range(F * C)], axis=1
        )

    for copy in loads[4:8]:
        copy.wait()
    down_v[ds(mine * R, R)] = wd_ref[...].astype(F32).T.astype(BF)

    def column_of(row):
        return jnp.broadcast_to(row.astype(F32), (8, span)).T[:, :1]

    seg = seg_ref[...].astype(F32)
    seg_row = seg_ref[:, at_c].astype(F32)
    seg_col = column_of(seg_row)
    padc[...] = column_of(pad_ref[:, at_c])
    win = k_s.shape[0]
    win_at = jnp.maximum(k.c * span + span - win, 0)
    at_w = pl.ds(pl.multiple_of(win_at, span), win)
    row_at = k.c * span + lax.broadcasted_iota(jnp.int32, (span, 1), 0)
    first = jnp.sum(jnp.where(seg < seg_col, 1.0, 0.0), axis=1, keepdims=True)
    lane = lax.broadcasted_iota(jnp.int32, (1, pair), 1)
    frequency = jnp.exp(-((lane % (hd // 2)).astype(F32) * (2.0 / hd)) * math.log(10000.0))
    low = (lane % hd) < (hd // 2)
    angles = (row_at.astype(F32) - first) * frequency
    cos_s[...] = jnp.cos(angles)
    sin_s[...] = jnp.where(low, -1.0, 1.0) * jnp.sin(angles)

    def tall_column(row):
        return jnp.broadcast_to(row.astype(F32), (8, win)).T[:, :1]

    key_at = win_at + lax.broadcasted_iota(jnp.int32, (win, span), 0)
    token_at = k.c * span + lax.broadcasted_iota(jnp.int32, (win, span), 1)
    allowed = (tall_column(seg_ref[:, at_w]) == seg_row) & (key_at <= token_at) & (
        (tall_column(pad_ref[:, at_w]) == 1.0) | (key_at == token_at)
    )
    terms = jnp.where(allowed, 0.0, NEG)
    for b in range(T):
        one = terms[:, b * rows:(b + 1) * rows]
        bias[b] = jnp.concatenate([one] * (128 // rows), axis=1)
    keep = padc[at_t]
    gall[at_t] = (cot_ref[...].astype(F32) * keep).astype(BF)

    def swap_halves(x):
        return jnp.where(low, pltpu.roll(x, pair - hd // 2, 1), pltpu.roll(x, hd // 2, 1))

    def turn(x):
        return x * cos_s[...] + swap_halves(x) * sin_s[...]

    def turn_back(x):
        return x * cos_s[...] - swap_halves(x) * sin_s[...]

    h_gather.relay()
    aw.second()
    ow.second()
    gw.first(wg_hbm, "f1")
    aw.third()
    for copy in gain_copies:
        copy.wait_recv()
    gain_one_row = gain_row(0)
    h_gather.wait()

    @pl.loop(0, T)
    def _(n):
        at = ds(n * rows, rows)
        h = h_s[at].astype(F32)
        inv = lax.rsqrt(jnp.mean(h * h, axis=-1, keepdims=True) + EPS)
        inv_s[at] = inv
        n1_s[at] = (h * inv * gain_one_row).astype(BF)

    g_gather = ZGather(k, gall, rows)
    aw.done()

    def down_rows(x):
        t = x.T
        return jnp.concatenate([t[n * hd:(n + 1) * hd] for n in range(nh)], axis=1)

    def across(x):
        t = x.T
        return jnp.concatenate([t[n * rows:(n + 1) * rows] for n in range(nh)], axis=1)

    pre = dot(n1_s[...], w_v[:, QW:])
    kv_s[at_c] = jnp.where(lane < hd, turn(pre), pre).astype(BF)
    own_kv = kv_s.at[at_c]
    kv_copies = [k.send(own_kv, own_kv, k.cpeer(i)) for i in range(1, C)]
    gw.first(wg_hbm, "2")
    turned = []
    for at, n in chunks(QW, 256):
        pre = dot(n1_s[...], w_v[:, at:at + n])
        turned += [turn(pre[:, b:b + pair]) * scale for b in range(0, n, pair)]
    turned = jnp.concatenate(turned, axis=1)
    for b in range(T):
        qt_s[b] = down_rows(turned[b * rows:(b + 1) * rows]).astype(BF)
    ow.third()
    for copy in kv_copies:
        copy.wait_recv()
    k_s[...] = kv_s[at_w, :hd]
    v_s[...] = kv_s[at_w, hd:]
    kvt = kv_s[at_w].astype(F32).T.astype(BF)
    kt_s[...] = kvt[:hd]
    vt_s[...] = kvt[hd:]
    g_gather.relay()
    wide = nh * rows
    group = min(256, wide)

    @pl.loop(0, T)
    def _(b):
        mask = jnp.concatenate([bias[b]] * (group // 128), axis=1)
        outs = []
        for a in range(0, wide, group):
            scores = dot(k_s[...], qt_s[b, :, a:a + group]) + mask
            top = jnp.max(scores, axis=0, keepdims=True)
            weights = jnp.exp(scores - top)
            total = jnp.sum(weights, axis=0, keepdims=True)
            outs.append(dot(vt_s[...], (weights * (1.0 / total)).astype(BF)))
            lse_s[b, :, a:a + group] = top + jnp.log(total)
        attn_s[ds(b * rows, rows)] = across(jnp.concatenate(outs, axis=1)).astype(BF)

    uw.first(wu_hbm)
    ow.done()

    @pl.loop(0, D // 256)
    def _(n):
        at = ds(n * 256, 256)
        part_b[:, at] = dot(attn_s[...], wo_v[at], 1, 1).astype(BF)

    h_gather.sent()
    one = ZScatter(k, part_b, slots, middle_a, rows)
    gw.second()
    one.relay()

    def turn_over(src, dst):
        @pl.loop(0, D // 256)
        def _(n):
            at = ds(n * 256, 256)
            dst[at] = src[:, at].astype(F32).T.astype(BF)

    g_gather.wait()
    turn_over(gall, xt_a)
    mid = hidden_ref[...].astype(F32) + one.total()
    mid_s[...] = mid
    scale_two = lax.rsqrt(jnp.mean(mid * mid, axis=-1, keepdims=True) + EPS)
    n2_s[at_t] = (mid * scale_two * gain_row(1)).astype(BF)
    n2_gather = ZGather(k, n2_s, rows)
    uw.second()
    dw.first(dw.part())
    n2_gather.relay()
    gw.third()
    uw.third()
    gw.done()
    uw.done()
    for copy in loads[8:]:
        copy.wait()
    n2_gather.wait()

    for at, n in chunks(FB, 256):
        gate = dot(n2_s[...], gate_v[:, at:at + n])
        up = dot(n2_s[...], up_v[:, at:at + n])
        sig = jax.nn.sigmoid(gate)
        inner[:, at:at + n] = (gate * sig * up).astype(BF)
        g_gate[:, at:at + n] = (up * sig * (1.0 + gate * (1.0 - sig))).astype(BF)
        g_up[:, at:at + n] = (gate * sig).astype(BF)

    down_g = Grad(k, xt_a, inner, FB, lambda s: twin_up.at[s], twin_down, relay_down, sum_down)
    down_g.first()
    dw.second()
    turn_over(n2_s, xt_b)
    down_g.second(local.at[10])
    down_g.direct("f", 0)
    down_g.direct("c", 1)
    k.finish(down_g.twins)
    dw.third()
    dw.done()
    for at, n in chunks(FB, 256):
        g_in = dot(gall[...], down_v[:, at:at + n])
        g_gate[:, at:at + n] = (g_in * g_gate[:, at:at + n].astype(F32)).astype(BF)
        g_up[:, at:at + n] = (g_in * g_up[:, at:at + n].astype(F32)).astype(BF)

    k.finish([one.far] * one.line + list(one.copies.values()))

    @pl.loop(0, D // 256)
    def _(n):
        at = ds(n * 256, 256)
        part = dot(g_gate[...], gate_v[at], 1, 1) + dot(g_up[...], up_v[at], 1, 1)
        part_b[:, at] = part.astype(BF)

    two = ZScatter(k, part_b, slots, middle_a, rows)
    for weight in (aw, ow, gw, uw, dw):
        weight.sent()

    def spare(room, lane, width):
        return lambda s: room.at[ds(s * R, R), lane:lane + width]

    gate_g = Grad(k, xt_b, g_gate, FB, spare(gate_v, 0, FB), twin_gate, relay_gate, sum_gate)
    up_g = Grad(k, xt_b, g_up, FB, spare(up_v, 0, FB), twin_up, relay_up, sum_up)
    down_g.third()
    gate_g.first()
    up_g.first()
    two.relay()
    gate_g.second(local.at[11])
    gate_g.direct("f", 0)
    gate_g.direct("c", 1)
    up_g.second(local.at[12])
    up_g.direct("f", 0)

    @pl.loop(0, D // 256)
    def _(n):
        at = ds(n * 256, 256)
        part2_b[:, at] = dot(inner[...], down_v[at], 1, 1).astype(BF)

    def norm_back(grad, vectors, gain):
        inv = lax.rsqrt(jnp.mean(vectors * vectors, axis=-1, keepdims=True) + EPS)
        unit = vectors * inv
        weighted = grad * gain
        g_gain = jnp.sum(grad * unit, axis=0, keepdims=True)
        return inv * (weighted - unit * jnp.mean(weighted * unit, axis=-1, keepdims=True)), g_gain

    d_mid, gain_two = norm_back(two.total(), mid_s[...], gain_row(1))
    g_mid = gall[at_t].astype(F32) + d_mid
    hid_ref[...] = g_mid
    gm[at_t] = g_mid.astype(BF)
    gm_gather = ZGather(k, gm, rows)
    turn_over(n1_s, xt_b)
    gate_g.third()
    g_kv[...] = jnp.zeros_like(g_kv)

    def attend_back(b):
        at_b = ds(b * rows, rows)
        mask = jnp.concatenate([bias[b]] * (group // 128), axis=1)
        g_block = dot(gm[at_b], wo_v[...])
        g_block = down_rows(g_block.astype(BF).astype(F32)).astype(BF)
        g_qs, g_keys, g_values = [], [], []
        for a in range(0, wide, group):
            q_one, g_one = qt_s[b, :, a:a + group], g_block[:, a:a + group]
            p = jnp.exp(dot(k_s[...], q_one) + mask - lse_s[b, :, a:a + group])
            dp = dot(v_s[...], g_one)
            delta = jnp.sum(p * dp, axis=0, keepdims=True)
            d_scores = (p * (dp - delta)).astype(BF)
            g_qs.append(dot(kt_s[...], d_scores))
            g_keys.append(dot(d_scores, q_one, 1, 1))
            g_values.append(dot(p.astype(BF), g_one, 1, 1))
        g_query = across(jnp.concatenate(g_qs, axis=1)) * scale
        cos, sin = cos_s[at_b], sin_s[at_b]
        for n in range(0, QW, pair):
            x = g_query[:, n:n + pair]
            g_qkv[at_b, n:n + pair] = (x * cos - swap_halves(x) * sin).astype(BF)
        g_kv[at_w] += jnp.concatenate([sum(g_keys), sum(g_values)], axis=1)

    attend_back(k.t)
    gm_gather.relay()
    branch = ZScatter(k, part2_b, slots2, middle_b, rows)
    for i in gm_gather.order:
        attend_back((k.t + T - gm_gather.arrival(i)) % T)
    g_kvb[...] = g_kv[...].astype(BF)
    kv_copies = []
    for i in range(1, C):
        piece = g_kvb.at[ds(((k.c + i) % C) * span, span)]
        kv_copies.append(k.send(piece, kv_slots.at[i - 1], k.cpeer(i)))
    branch.relay()
    up_g.direct("c", 1)
    up_g.third()
    turn_over(gm, xt_a)
    out_g = Grad(k, xt_a, attn_s, QW, spare(wo_v, 0, QW), twin_out, relay_out, sum_out)
    out_g.first()
    own_kv = g_kv[at_c]
    for i in range(1, C):
        kv_copies[i - 1].wait_recv()
        own_kv = own_kv + kv_slots[i - 1].astype(F32)
    g_qkv[:, QW:] = jnp.where(lane < hd, turn_back(own_kv), own_kv).astype(BF)
    k.finish([two.far] * two.line + list(two.copies.values()))

    @pl.loop(0, D // 256)
    def _(n):
        at = ds(n * 256, 256)
        part = dot(g_qkv[...], w_v[at], 1, 1)
        part_b[:, at] = part.astype(BF)
        gain_s[:, at] = jnp.sum(part * (h_s[:, at].astype(F32) * inv_s[...]), axis=0, keepdims=True)

    last = ZScatter(k, part_b, slots, middle_a, rows)
    out_g.second(local.at[13])
    out_g.direct("f", 0)
    out_g.direct("c", 1)
    qkv_g = Grad(k, xt_b, g_qkv, QKV, spare(w_v, 0, QKV), twin_qkv, relay_qkv, sum_qkv)
    qkv_g.first()
    last.relay()
    qkv_g.second(local.at[14])
    qkv_g.direct("f", 0)
    qkv_g.direct("c", 1)
    gain_one = gain_s[...]
    for b in range(F * C):
        gz[b] = jnp.concatenate(
            [gain_one[:, b * R:(b + 1) * R], gain_two[:, b * R:(b + 1) * R]], axis=1
        )
    z_copies = [k.send(gz, gz_slots.at[i - 1], k.zpeer(i)) for i in range(1, T)]
    out_ref[...] = (padc[at_t] * (mid_s[...] + branch.total())).astype(BF)
    out_g.third()
    both = gz[...]
    for i in range(1, T):
        z_copies[i - 1].wait_recv()
        both = both + gz_slots[i - 1]
    gx[...] = both
    x_copies = []
    for n, dev in enumerate(k.plane_peers()):
        x_copies.append(k.send(gx.at[dev[0] * C + dev[1]], gx_slots.at[n], dev))
    qkv_g.third()
    d_hid, _ = norm_back(last.total(), hidden_ref[...].astype(F32), gain_one_row)
    hid_ref[...] = hid_ref[...] + d_hid
    both = gx[mine]
    for n, copy in enumerate(x_copies):
        copy.wait_recv()
        both = both + gx_slots[n]
    gg_ref[...] = both
    for grad in (down_g, gate_g, up_g, out_g, qkv_g):
        grad.done()
    k.finish()


def layer(sizes, hd, hidden, seg, pad, ga, gm, wq, wk, wv, wo, wd, cot, wg, wu):
    F, C, T = sizes
    H = C // 2
    rows, D = hidden.shape
    R, QW = wq.shape
    FB = wg.shape[1]
    span, length, QKV = rows * T, seg.shape[1], QW + 2 * hd
    vm = pl.BlockSpec(memory_space=pltpu.VMEM)
    hbm = pl.BlockSpec(memory_space=pl.ANY)
    wide = QW // hd * rows
    win = min(length, span + -(-DOC // span) * span)
    n_sems = n_semaphores(F, C, T)
    S = jax.ShapeDtypeStruct
    V = pltpu.VMEM
    FH, lines, diag = F * H, F + H - 1, max(1, (F - 1) * (H - 1))
    widths = (FB, FB, FB, QW, QKV)
    return pl.pallas_call(
        functools.partial(layer_kernel, sizes, hd),
        out_shape=(
            S((rows, D), BF), S((rows, D), F32), S((1, 2 * R), F32),
            *[S((lines, R, n), BF) for n in widths],
        ),
        in_specs=[vm] * 4 + [hbm] * 9,
        out_specs=[vm] * 3 + [hbm] * 5,
        scratch_shapes=[
            V((D, QKV), BF), V((D, QW), BF), V((D, FB), BF), V((D, FB), BF), V((D, FB), BF),
            V((span, D), BF), V((span, D), BF), V((span, D), BF), V((span, D), BF), V((span, D), BF),
            V((D, span), BF), V((D, span), BF),
            V((span, FB), BF), V((span, FB), BF), V((span, FB), BF),
            V((T, hd, wide), BF), V((span, QW), BF), V((span, QKV), BF), V((T, 1, wide), F32),
            V((length, 2 * hd), BF), V((win, hd), BF), V((win, hd), BF), V((hd, win), BF), V((hd, win), BF),
            V((length, 2 * hd), F32), V((length, 2 * hd), BF), V((C - 1, span, 2 * hd), BF),
            V((T, win, 128), F32), V((span, 2 * hd), F32), V((span, 2 * hd), F32),
            V((span, 1), F32), V((1, D), F32), V((span, 1), F32),
            V((span, D), BF), V((span, D), BF), V((T - 1, rows, D), BF), V((T - 1, rows, D), BF),
            V((rows, D), BF), V((rows, D), BF), V((rows, D), F32),
            *[V((FH, R, n), BF) for n in widths],
            *[V((diag, 2, R // 2, n), BF) for n in widths],
            V((F * C, 1, 2 * R), F32), V((F * C, 1, 2 * R), F32), V((T - 1, F * C, 1, 2 * R), F32),
            V((F * C, 1, 2 * R), F32), V((F * C - 1, 1, 2 * R), F32),
            V((rows, D), BF), V((2 * hd, R), BF), V((QW, R), BF), V((FB, R), BF), V((rows, D), BF),
            pltpu.SemaphoreType.DMA((n_sems,)), pltpu.SemaphoreType.DMA((n_sems,)),
            pltpu.SemaphoreType.DMA((15,)),
        ],
        compiler_params=pltpu.CompilerParams(
            collective_id=0, has_side_effects=True, vmem_limit_bytes=62 * 2**20
        ),
        name="layer",
    )(seg, pad, ga, gm, hidden, wq, wk, wv, wo, wd, cot, wg, wu)


def final_kernel(
    hd, out_ref, hid_ref, down_ref, gate_ref, up_ref, wo_ref, qkv_ref,
    block_out, grad_hidden, g_query, g_key, g_value, g_out, g_gate, g_up, g_down,
):
    def total(ref):
        return sum(ref[i].astype(F32) for i in range(ref.shape[0]))

    QW = g_query.shape[1]
    block_out[...] = out_ref[...]
    grad_hidden[...] = hid_ref[...]
    qkv = total(qkv_ref)
    g_query[...] = qkv[:, :QW]
    kv = qkv[:, QW:].T
    g_key[...] = kv[:hd]
    g_value[...] = kv[hd:]
    g_out[...] = total(wo_ref).T
    g_gate[...] = total(gate_ref)
    g_up[...] = total(up_ref)
    g_down[...] = total(down_ref).T


def final(hd, block_out, grad_hidden, s_down, s_gate, s_up, s_out, s_qkv):
    L, R, FB = s_gate.shape
    QW = s_out.shape[2]
    rows, D = block_out.shape
    steps = R // 128 if R % 128 == 0 else 1
    r = R // steps
    S = jax.ShapeDtypeStruct

    def parts(x):
        return pl.BlockSpec((L, r, x.shape[2]), lambda i: (0, i, 0))

    def tall(n):
        return pl.BlockSpec((r, n), lambda i: (i, 0))

    def wide(n):
        return pl.BlockSpec((n, r), lambda i: (0, i))

    acts = pl.BlockSpec((rows // steps, D), lambda i: (i, 0))
    return pl.pallas_call(
        functools.partial(final_kernel, hd),
        grid=(steps,),
        out_shape=(
            S((rows, D), BF), S((rows, D), F32), S((R, QW), F32), S((hd, R), F32), S((hd, R), F32),
            S((QW, R), F32), S((R, FB), F32), S((R, FB), F32), S((FB, R), F32),
        ),
        in_specs=[acts, acts] + [parts(x) for x in (s_down, s_gate, s_up, s_out, s_qkv)],
        out_specs=[acts, acts, tall(QW), wide(hd), wide(hd), wide(QW), tall(FB), tall(FB), wide(FB)],
        compiler_params=pltpu.CompilerParams(vmem_limit_bytes=62 * 2**20),
        name="final",
    )(block_out, grad_hidden, s_down, s_gate, s_up, s_out, s_qkv)


def body(hidden_in, segment_ids, pad_mask, attn_gain, w_query, w_key, w_value, w_out,
         mlp_gain, w_gate, w_up, w_down, cotangent):
    sizes = tuple(lax.axis_size(n) for n in ("fsdp", "context", "tensor"))
    hd, R = w_key.shape[1], w_query.shape[0]
    block_out, grad_hidden, gg, *parts = layer(
        sizes, hd, hidden_in[0], segment_ids, pad_mask, attn_gain, mlp_gain,
        w_query, w_key.T, w_value.T, w_out, w_down, cotangent[0], w_gate, w_up,
    )
    block_out, grad_hidden, g_query, g_key, g_value, g_out, g_gate, g_up, g_down = final(
        hd, block_out, grad_hidden, *parts
    )
    return (
        block_out[None], grad_hidden[None], gg[0, :R], g_query, g_key.T, g_value.T, g_out, gg[0, R:],
        g_gate, g_up, g_down,
    )


def solution(mesh):
    rows = P("fsdp", ("context", "tensor"), None)
    tail = (P(FC), P(FC, "tensor"), P(FC, "tensor"), P(FC, "tensor"), P("tensor", FC),
            P(FC), P(FC, "tensor"), P(FC, "tensor"), P("tensor", FC))
    in_specs = (rows, P("fsdp", None), P("fsdp", None)) + tail + (rows,)
    out_specs = (rows, rows) + tail
    return jax.shard_map(body, mesh=mesh, in_specs=in_specs, out_specs=out_specs, check_vma=False)
```

```python
import functools
import math

import jax
import jax.numpy as jnp
from jax import lax
from jax.experimental import pallas as pl
from jax.experimental.pallas import tpu as pltpu
from jax.sharding import PartitionSpec as P

EPS = 1e-05
NEG = -1e30
DOC = 512
BF = jnp.bfloat16
F32 = jnp.float32
MESH = pl.DeviceIdType.MESH
FC = ("fsdp", "context")


def dot(a, b, ca=1, cb=0):
    return lax.dot_general(a, b, (((ca,), (cb,)), ((), ())), preferred_element_type=F32)


def chunks(total, step):
    return [(at, min(step, total - at)) for at in range(0, total, step)]


def ds(start, size):
    return pl.ds(pl.multiple_of(start, size), size)


class Links:
    def __init__(self, sizes, send_sems, recv_sems):
        self.F, self.C, self.T = sizes
        self.f = lax.axis_index("fsdp")
        self.c = lax.axis_index("context")
        self.t = lax.axis_index("tensor")
        self.h = self.c // 2
        self.core = self.c % 2
        self.H = self.C // 2
        self.send_sems, self.recv_sems = send_sems, recv_sems
        self.used = 0
        self.open = []
        self.sib = (self.f, self.h * 2 + 1 - self.core, self.t)

    def chip(self, df, dh):
        return ((self.f + df) % self.F, ((self.h + dh) % self.H) * 2 + self.core, self.t)

    def block(self, df, dh, core):
        return ((self.f + df) % self.F) * self.C + ((self.h + dh) % self.H) * 2 + core

    def zpeer(self, i):
        return (self.f, self.c, (self.t + i) % self.T)

    def cpeer(self, i):
        return (self.f, (self.c + i) % self.C, self.t)

    def new(self, src, dst, dev, recv=None):
        n = self.used
        self.used += 1
        copy = pltpu.make_async_remote_copy(
            src_ref=src, dst_ref=dst, send_sem=self.send_sems.at[n],
            recv_sem=self.recv_sems.at[n if recv is None else recv],
            device_id=dev, device_id_type=MESH,
        )
        return copy, n

    def start(self, copy, cond=None):
        if cond is None:
            copy.start()
        else:
            pl.when(cond)(copy.start)
        self.open.append((copy, cond))

    def send(self, src, dst, dev):
        copy, _ = self.new(src, dst, dev)
        self.start(copy)
        return copy

    def plane_peers(self):
        return [
            ((self.f + df) % self.F, (self.c + dc) % self.C, self.t)
            for df in range(self.F) for dc in range(self.C) if df or dc
        ]

    def peers(self):
        return self.plane_peers() + [self.zpeer(i) for i in range(1, self.T)]

    def greet(self):
        self.bar = pltpu.get_barrier_semaphore()
        for dev in self.peers():
            pl.semaphore_signal(self.bar, inc=1, device_id=dev, device_id_type=MESH)

    def meet(self):
        pl.semaphore_wait(self.bar, len(self.peers()))

    def finish(self, copies=None):
        wanted = None if copies is None else [id(c) for c in copies]
        left = []
        for copy, cond in self.open:
            if wanted is not None and id(copy) not in wanted:
                left.append((copy, cond))
            elif cond is None:
                copy.wait_send()
            else:
                pl.when(cond)(copy.wait_send)
        self.open = left


class Gather:
    def __init__(self, links, full, rows):
        self.k, self.full, self.rows = links, full, rows
        self.line, self.twin, self.diag, self.split = {}, [], {}, False

    def part(self, df=0, dh=0, start=0, size=None):
        n = self.rows // 4
        block = self.k.block(-df, -dh, self.k.core)
        if size is None:
            return self.full.at[ds(block * self.rows, self.rows)]
        return self.full.at[pl.ds(pl.multiple_of(block * self.rows + start * n, n), size * n)]

    def some(self, own, along, start, size):
        k, n = self.k, self.rows // 4
        src, to = own.at[start * n:(start + size) * n], self.part(0, 0, start, size)
        for df in range(1, k.F) if "f" in along else ():
            self.line.setdefault((df, 0), []).append(k.send(src, to, k.chip(df, 0)))
        for dh in range(1, k.H) if "c" in along else ():
            self.line.setdefault((0, dh), []).append(k.send(src, to, k.chip(0, dh)))

    def sibling(self, own):
        self.twin.append(self.k.send(own, self.part(), self.k.sib))

    def first(self, own):
        self.some(own, "fc", 0, 4)
        self.sibling(own)

    def first_split(self, own):
        self.split = True
        self.some(own, "f", 0, 2)
        self.some(own, "c", 2, 2)
        self.some(own, "f", 2, 2)
        self.some(own, "c", 0, 2)
        self.sibling(own)

    def second(self):
        k = self.k
        for df, dh in sorted(self.line, reverse=True):
            copies = self.line[df, dh]
            for copy in copies[:1] if self.split else copies:
                copy.wait_recv()
            half = 0 if df else 1
            piece = self.part(df, dh, 2 * half, 2)
            if df:
                for eh in range(1, k.H):
                    self.diag[df, eh, half] = k.send(piece, piece, k.chip(0, eh))
            else:
                for ef in range(1, k.F):
                    self.diag[ef, dh, half] = k.send(piece, piece, k.chip(ef, 0))
        if not self.split:
            self.pass_on()

    def pass_on(self):
        for df, dh in sorted(self.line, reverse=True):
            for copy in self.line[df, dh][1:] if self.split else ():
                copy.wait_recv()
            whole = self.part(df, dh)
            self.twin.append(self.k.send(whole, whole, self.k.sib))

    def third(self):
        k = self.k
        if self.split:
            self.pass_on()
        for copy in self.diag.values():
            copy.wait_recv()
        for df in range(1, k.F):
            for dh in range(1, k.H):
                whole = self.part(df, dh)
                self.twin.append(k.send(whole, whole, k.sib))

    def done(self):
        for copy in self.twin:
            copy.wait_recv()

    def sent(self):
        lines = [copy for copies in self.line.values() for copy in copies]
        self.k.finish(lines + list(self.diag.values()) + self.twin)


class ZGather:
    def __init__(self, k, full, rows, own=None):
        self.k, self.full, self.rows = k, full, rows
        T = k.T
        piece = full.at[ds(k.t * rows, rows)]
        own = piece if own is None else own
        self.copies = {i: k.new(own, piece, k.zpeer(i)) for i in range(1, T)}
        for i in [2, 1, 3] if T == 4 else range(1, T):
            cond = None
            if T == 4 and i != 2:
                cond = (k.t < 3) if i == 1 else (k.t > 0)
            k.start(self.copies[i][0], cond)
        self.left = list(range(1, T))
        self.relays = []
        self.order = [2, 1, 3] if T == 4 else list(range(1, T))

    def relay(self):
        k = self.k
        if k.T != 4:
            return
        self.copies[2][0].wait_recv()
        self.left = [1, 3]
        for at, origin, i in ((2, 0, 3), (1, 3, 1)):
            piece = self.full.at[ds(origin * self.rows, self.rows)]
            copy, _ = k.new(piece, piece, (k.f, k.c, 3 - origin), recv=self.copies[i][1])
            k.start(copy, k.t == at)
            self.relays.append(copy)

    def sent(self):
        self.k.finish([c for c, _ in self.copies.values()] + self.relays)

    def wait(self):
        for i in self.left:
            self.copies[i][0].wait_recv()

    def arrival(self, i):
        if self.k.T != 4:
            self.copies[i][0].wait_recv()
            return i
        if i == 2:
            return i
        at_first = self.k.t == 0
        pl.when(at_first)(self.copies[4 - i][0].wait_recv)
        pl.when(jnp.logical_not(at_first))(self.copies[i][0].wait_recv)
        return jnp.where(at_first, 4 - i, i)


class ZScatter:
    def __init__(self, k, part, slots, middle, rows):
        self.k, self.part, self.slots, self.middle, self.rows = k, part, slots, middle, rows
        T = k.T
        self.line = T == 4
        self.end = (k.t == 0) | (k.t == T - 1)
        if self.line:
            src = part.at[ds((3 - k.t) * rows, rows)]
            self.far, _ = k.new(src, middle, (k.f, k.c, 1 + k.t // 3))
            k.start(self.far, self.end)
        self.copies = {}
        for i in range(1, T):
            src = part.at[ds(((k.t + i) % T) * rows, rows)]
            self.copies[i], _ = k.new(src, slots.at[i - 1], k.zpeer(i))
        if self.line:
            k.start(self.copies[2], self.end)
            k.start(self.copies[1], k.t < 3)
            k.start(self.copies[3], k.t > 0)
        else:
            for i in range(1, T):
                k.start(self.copies[i])

    def relay(self):
        k = self.k
        if not self.line:
            return
        inner = (k.t > 0) & (k.t < 3)

        @pl.when(inner)
        def _():
            self.far.wait_recv()
            at = ds(((k.t + 2) % 4) * self.rows, self.rows)
            both = self.part[at].astype(F32) + self.middle[...].astype(F32)
            self.part[at] = both.astype(BF)
            self.copies[2].start()

        k.open.append((self.copies[2], inner))

    def total(self):
        k = self.k
        for i in range(1, k.T):
            if not self.line or i == 2:
                self.copies[i].wait_recv()
                continue
            there = (k.t > 0) if i == 1 else (k.t < 3)
            pl.when(there)(self.copies[i].wait_recv)

            @pl.when(jnp.logical_not(there))
            def _():
                self.slots[i - 1] = jnp.zeros(self.slots.shape[1:], BF)

        total = self.part[ds(k.t * self.rows, self.rows)].astype(F32)
        for i in range(1, k.T):
            total = total + self.slots[i - 1].astype(F32)
        return total


class Grad:
    def __init__(self, k, xt, y, width, stage, twin, relay, out):
        self.k, self.xt, self.y, self.width, self.stage = k, xt, y, width, stage
        self.twin, self.relay, self.out = twin, relay, out
        self.R = xt.shape[0] // (k.F * k.C)

    def rows_of(self, s, core):
        return ds(self.k.block(s // self.k.H, s % self.k.H, core) * self.R, self.R)

    def piece(self, df, dh, half=None):
        s = df * self.k.H + dh
        if half is None:
            return self.twin.at[s]
        n = self.R // 2
        return self.twin.at[s, half * n:(half + 1) * n]

    def first(self):
        k = self.k

        @pl.loop(0, k.F * k.H)
        def _(s):
            x = self.xt[self.rows_of(s, 1 - k.core)]
            to = self.stage(s)
            for a, n in chunks(self.width, 256):
                to[:, a:a + n] = dot(x, self.y[:, a:a + n]).astype(BF)

        self.twins = [k.send(self.stage(s), self.twin.at[s], k.sib) for s in range(k.F * k.H)]

    def second(self, sem):
        k = self.k
        for copy in self.twins:
            copy.wait_recv()

        @pl.loop(0, k.F * k.H)
        def _(s):
            x = self.xt[self.rows_of(s, k.core)]
            for a, n in chunks(self.width, 256):
                total = dot(x, self.y[:, a:a + n]) + self.twin[s, :, a:a + n].astype(F32)
                self.twin[s, :, a:a + n] = total.astype(BF)

        self.diag, self.far = {}, []
        n = 0
        for df in range(1, k.F):
            for dh in range(1, k.H):
                for half, dev in ((0, k.chip(df, 0)), (1, k.chip(0, dh))):
                    self.diag[df, dh, half] = n, half, k.send(
                        self.piece(df, dh, half), self.relay.at[n, half], dev
                    )
                n += 1
        self.own = None
        if sem is not None:
            self.own = pltpu.make_async_copy(self.piece(0, 0), self.out.at[0], sem)
            self.own.start()

    def direct(self, along, half):
        k = self.k
        n = self.R // 2
        at = slice(half * n, half * n + n)
        if along == "c":
            for dh in range(1, k.H):
                to = self.out.at[k.F - 1 + dh, at]
                self.far.append(k.send(self.piece(0, dh, half), to, k.chip(0, dh)))
        else:
            for df in range(1, k.F):
                self.far.append(k.send(self.piece(df, 0, half), self.out.at[df, at], k.chip(df, 0)))

    def add(self, df, dh, half):
        piece = self.piece(df, dh, half)
        total = piece[...].astype(F32)
        for (ef, eh, other), (n, _, copy) in self.diag.items():
            if other == half and (ef == df or df == 0) and (eh == dh or dh == 0):
                copy.wait_recv()
                total = total + self.relay[n, half].astype(F32)
        piece[...] = total.astype(BF)

    def third(self, along="fc"):
        k = self.k
        if "f" in along:
            for df in range(1, k.F):
                if k.H > 1:
                    self.add(df, 0, 1)
            self.direct("f", 1)
        if "c" in along:
            for dh in range(1, k.H):
                if k.F > 1:
                    self.add(0, dh, 0)
            self.direct("c", 0)

    def done(self):
        for copy in self.far:
            copy.wait_recv()
        if self.own is not None:
            self.own.wait()

    def collect(self, room, sems):
        self.done()
        lines = self.k.F + self.k.H - 1
        first = self.k.F * self.k.H * self.R
        self.room, self.first_row = room, first
        self.loads = [
            pltpu.make_async_copy(
                self.out.at[n], room.at[first + (n - 1) * self.R:first + n * self.R], sems.at[n - 1]
            )
            for n in range(1, lines)
        ]
        for copy in self.loads:
            copy.start()

    def add_up(self, result, sem):
        for copy in self.loads:
            copy.wait()
        step = min(self.R, 64)

        @pl.loop(0, self.R // step)
        def _(n):
            total = self.twin[0, ds(n * step, step)].astype(F32)
            for i in range(len(self.loads)):
                total = total + self.room[ds(self.first_row + i * self.R + n * step, step)].astype(F32)
            self.twin[0, ds(n * step, step)] = total.astype(BF)

        self.own = pltpu.make_async_copy(self.twin.at[0], result, sem)
        self.own.start()


def n_semaphores(F, C, T):
    H = C // 2
    a, b, d = F - 1, H - 1, (F - 1) * (H - 1)
    gather = a + b + 1 + 2 * d + a + b + d
    grad = F * H + 2 * d + 2 * (a + b)
    return 5 * gather + 4 * (a + b) + 5 * grad + 2 * (F * C - 1) + 2 * (C - 1) + 9 * (T + 1)


def layer_kernel(
    sizes, hd,
    seg_ref, pad_ref, ga_ref, gm_ref,
    hidden_hbm, wq_hbm, wk_hbm, wv_hbm, wo_hbm, wd_hbm, cot_hbm, wg_hbm, wu_hbm,
    out_ref, hid_ref, gg_ref, sum_down, sum_gate, sum_up, sum_out, sum_qkv, all_down, all_gate, all_up,
    w_v, wo_v, gate_v, up_v, down_v, h_s, n1_s, n2_s, gall, gm, xt_a, xt_b, inner, g_gate, g_up,
    qt_s, attn_s, g_qkv, lse_s, kv_s, k_s, v_s, kt_s, vt_s, g_kv, g_kvb, kv_slots, bias, cos_s, sin_s,
    inv_s, gain_s,
    padc, part_b, part2_b, slots, slots2, middle_a, middle_b, mid_s,
    twin_down, twin_gate, twin_up, twin_out, twin_qkv,
    relay_down, relay_gate, relay_up, relay_out, relay_qkv,
    gains_s, gz, gz_slots, gx, gx_slots, hidden_ref, kvw_ref, wo_ref, wd_ref, cot_ref, sends, recvs, local, many,
):
    k = Links(sizes, sends, recvs)
    T, F, C, H = k.T, k.F, k.C, k.H
    rows, D = hidden_ref.shape
    R, QW = wq_hbm.shape
    FB = wg_hbm.shape[1]
    span, length = gall.shape[0], seg_ref.shape[1]
    nh = QW // hd
    QKV = QW + 2 * hd
    pair = 2 * hd
    scale = hd ** (-0.5)
    at_t = ds(k.t * rows, rows)
    at_c = ds(k.c * span, span)
    back = k_s.shape[0] // span - 1
    kv_s[...] = jnp.zeros_like(kv_s)
    kv_slots[...] = jnp.zeros_like(kv_slots)
    k.greet()

    aw, ow, gw, uw, dw = (Gather(k, full, R) for full in (w_v, wo_v, gate_v, up_v, down_v))
    mine = k.block(0, 0, k.core)
    own_w, own_o = aw.part(), ow.part()
    loads = [
        pltpu.make_async_copy(src, dst, local.at[n])
        for n, (src, dst) in enumerate((
            (wk_hbm, kvw_ref.at[:hd]), (wv_hbm, kvw_ref.at[hd:]), (wo_hbm, wo_ref),
            (wq_hbm, own_w.at[:, :QW]), (hidden_hbm, hidden_ref), (hidden_hbm, h_s.at[at_t]),
            (wd_hbm, wd_ref), (cot_hbm, cot_ref), (wg_hbm, gw.part()), (wu_hbm, uw.part()),
        ))
    ]
    for copy in loads:
        copy.start()
    gains_s[mine, :, :R] = ga_ref[...].astype(F32).reshape(1, R)
    gains_s[mine, :, R:] = gm_ref[...].astype(F32).reshape(1, R)
    for copy in loads[:4]:
        copy.wait()
    own_w[:, QW:] = kvw_ref[...].astype(F32).T.astype(BF)
    own_o[...] = wo_ref[...].astype(F32).T.astype(BF)
    k.meet()
    h_gather = ZGather(k, h_s, rows, hidden_hbm)
    own_gain = gains_s.at[mine]
    gain_copies = [k.send(own_gain, own_gain, dev) for dev in k.plane_peers()]
    aw.first(own_w)
    ow.first(own_o)

    def gain_row(which):
        return jnp.concatenate(
            [gains_s[b][:, which * R:(which + 1) * R] for b in range(F * C)], axis=1
        )

    for copy in loads[4:8]:
        copy.wait()
    down_v[ds(mine * R, R)] = wd_ref[...].astype(F32).T.astype(BF)

    def column_of(row):
        return jnp.broadcast_to(row.astype(F32), (8, span)).T[:, :1]

    seg = seg_ref[...].astype(F32)
    seg_row = seg_ref[:, at_c].astype(F32)
    seg_col = column_of(seg_row)
    padc[...] = column_of(pad_ref[:, at_c])
    win = k_s.shape[0]
    win_at = jnp.maximum(k.c * span + span - win, 0)
    at_w = pl.ds(pl.multiple_of(win_at, span), win)
    row_at = k.c * span + lax.broadcasted_iota(jnp.int32, (span, 1), 0)
    first = jnp.sum(jnp.where(seg < seg_col, 1.0, 0.0), axis=1, keepdims=True)
    lane = lax.broadcasted_iota(jnp.int32, (1, pair), 1)
    frequency = jnp.exp(-((lane % (hd // 2)).astype(F32) * (2.0 / hd)) * math.log(10000.0))
    low = (lane % hd) < (hd // 2)
    angles = (row_at.astype(F32) - first) * frequency
    cos_s[...] = jnp.cos(angles)
    sin_s[...] = jnp.where(low, -1.0, 1.0) * jnp.sin(angles)

    def tall_column(row):
        return jnp.broadcast_to(row.astype(F32), (8, win)).T[:, :1]

    key_at = win_at + lax.broadcasted_iota(jnp.int32, (win, span), 0)
    token_at = k.c * span + lax.broadcasted_iota(jnp.int32, (win, span), 1)
    allowed = (tall_column(seg_ref[:, at_w]) == seg_row) & (key_at <= token_at) & (
        (tall_column(pad_ref[:, at_w]) == 1.0) | (key_at == token_at)
    )
    terms = jnp.where(allowed, 0.0, NEG)
    for b in range(T):
        one = terms[:, b * rows:(b + 1) * rows]
        bias[b] = jnp.concatenate([one] * (128 // rows), axis=1)
    keep = padc[at_t]
    gall[at_t] = (cot_ref[...].astype(F32) * keep).astype(BF)

    def swap_halves(x):
        return jnp.where(low, pltpu.roll(x, pair - hd // 2, 1), pltpu.roll(x, hd // 2, 1))

    def turn(x):
        return x * cos_s[...] + swap_halves(x) * sin_s[...]

    def turn_back(x):
        return x * cos_s[...] - swap_halves(x) * sin_s[...]

    h_gather.relay()
    aw.second()
    ow.second()
    gw.some(wg_hbm, "f", 0, 4)
    gw.some(wg_hbm, "c", 0, 1)
    gw.sibling(wg_hbm)
    aw.third()
    for copy in gain_copies:
        copy.wait_recv()
    gain_one_row = gain_row(0)
    h_gather.wait()

    @pl.loop(0, T)
    def _(n):
        at = ds(n * rows, rows)
        h = h_s[at].astype(F32)
        inv = lax.rsqrt(jnp.mean(h * h, axis=-1, keepdims=True) + EPS)
        inv_s[at] = inv
        n1_s[at] = (h * inv * gain_one_row).astype(BF)

    g_gather = ZGather(k, gall, rows)
    aw.done()

    def down_rows(x):
        t = x.T
        return jnp.concatenate([t[n * hd:(n + 1) * hd] for n in range(nh)], axis=1)

    def across(x):
        t = x.T
        return jnp.concatenate([t[n * rows:(n + 1) * rows] for n in range(nh)], axis=1)

    pre = dot(n1_s[...], w_v[:, QW:])
    kv_s[at_c] = jnp.where(lane < hd, turn(pre), pre).astype(BF)
    own_kv = kv_s.at[at_c]
    kv_copies = {}
    for i in range(1, back + 1):
        kv_copies[i], _ = k.new(own_kv, own_kv, k.cpeer(i))
        k.start(kv_copies[i], k.c + i < C)
    gw.some(wg_hbm, "c", 1, 3)
    turned = []
    for at, n in chunks(QW, 256):
        pre = dot(n1_s[...], w_v[:, at:at + n])
        turned += [turn(pre[:, b:b + pair]) * scale for b in range(0, n, pair)]
    turned = jnp.concatenate(turned, axis=1)
    for b in range(T):
        qt_s[b] = down_rows(turned[b * rows:(b + 1) * rows]).astype(BF)
    ow.third()
    for i, copy in kv_copies.items():
        pl.when(k.c >= i)(copy.wait_recv)
    k_s[...] = kv_s[at_w, :hd]
    v_s[...] = kv_s[at_w, hd:]
    kvt = kv_s[at_w].astype(F32).T.astype(BF)
    kt_s[...] = kvt[:hd]
    vt_s[...] = kvt[hd:]
    g_gather.relay()
    wide = nh * rows
    group = min(256, wide)

    @pl.loop(0, T)
    def _(b):
        mask = jnp.concatenate([bias[b]] * (group // 128), axis=1)
        outs = []
        for a in range(0, wide, group):
            scores = dot(k_s[...], qt_s[b, :, a:a + group]) + mask
            top = jnp.max(scores, axis=0, keepdims=True)
            weights = jnp.exp(scores - top)
            total = jnp.sum(weights, axis=0, keepdims=True)
            outs.append(dot(vt_s[...], (weights * (1.0 / total)).astype(BF)))
            lse_s[b, :, a:a + group] = top + jnp.log(total)
        attn_s[ds(b * rows, rows)] = across(jnp.concatenate(outs, axis=1)).astype(BF)

    uw.first(wu_hbm)
    ow.done()

    @pl.loop(0, D // 256)
    def _(n):
        at = ds(n * 256, 256)
        part_b[:, at] = dot(attn_s[...], wo_v[at], 1, 1).astype(BF)

    h_gather.sent()
    one = ZScatter(k, part_b, slots, middle_a, rows)
    gw.second()
    one.relay()

    def turn_over(src, dst):
        @pl.loop(0, D // 256)
        def _(n):
            at = ds(n * 256, 256)
            dst[at] = src[:, at].astype(F32).T.astype(BF)

    g_gather.wait()
    turn_over(gall, xt_a)
    mid = hidden_ref[...].astype(F32) + one.total()
    mid_s[...] = mid
    scale_two = lax.rsqrt(jnp.mean(mid * mid, axis=-1, keepdims=True) + EPS)
    n2_s[at_t] = (mid * scale_two * gain_row(1)).astype(BF)
    n2_gather = ZGather(k, n2_s, rows)
    uw.second()
    dw.first_split(dw.part())
    n2_gather.relay()
    gw.third()
    uw.third()
    gw.done()
    uw.done()
    for copy in loads[8:]:
        copy.wait()
    n2_gather.wait()

    for at, n in chunks(FB, 256):
        gate = dot(n2_s[...], gate_v[:, at:at + n])
        up = dot(n2_s[...], up_v[:, at:at + n])
        sig = jax.nn.sigmoid(gate)
        inner[:, at:at + n] = (gate * sig * up).astype(BF)
        g_gate[:, at:at + n] = (up * sig * (1.0 + gate * (1.0 - sig))).astype(BF)
        g_up[:, at:at + n] = (gate * sig).astype(BF)

    down_g = Grad(k, xt_a, inner, FB, lambda s: twin_up.at[s], twin_down, relay_down, sum_down)
    down_g.first()
    dw.second()
    turn_over(n2_s, xt_b)
    down_g.second(None)
    down_g.direct("f", 0)
    down_g.direct("c", 1)
    k.finish(down_g.twins)
    dw.third()
    dw.done()
    for at, n in chunks(FB, 256):
        g_in = dot(gall[...], down_v[:, at:at + n])
        g_gate[:, at:at + n] = (g_in * g_gate[:, at:at + n].astype(F32)).astype(BF)
        g_up[:, at:at + n] = (g_in * g_up[:, at:at + n].astype(F32)).astype(BF)

    k.finish([one.far] * one.line + list(one.copies.values()))

    @pl.loop(0, D // 256)
    def _(n):
        at = ds(n * 256, 256)
        part = dot(g_gate[...], gate_v[at], 1, 1) + dot(g_up[...], up_v[at], 1, 1)
        part_b[:, at] = part.astype(BF)

    two = ZScatter(k, part_b, slots, middle_a, rows)
    for weight in (aw, ow, gw, uw, dw):
        weight.sent()

    def spare(room, lane, width):
        return lambda s: room.at[ds(s * R, R), lane:lane + width]

    gate_g = Grad(k, xt_b, g_gate, FB, spare(gate_v, 0, FB), twin_gate, relay_gate, sum_gate)
    up_g = Grad(k, xt_b, g_up, FB, spare(up_v, 0, FB), twin_up, relay_up, sum_up)
    down_g.third()
    gate_g.first()
    up_g.first()
    two.relay()
    gate_g.second(None)
    gate_g.direct("f", 0)
    gate_g.direct("c", 1)
    up_g.second(None)
    up_g.direct("f", 0)

    @pl.loop(0, D // 256)
    def _(n):
        at = ds(n * 256, 256)
        part2_b[:, at] = dot(inner[...], down_v[at], 1, 1).astype(BF)

    def norm_back(grad, vectors, gain):
        inv = lax.rsqrt(jnp.mean(vectors * vectors, axis=-1, keepdims=True) + EPS)
        unit = vectors * inv
        weighted = grad * gain
        g_gain = jnp.sum(grad * unit, axis=0, keepdims=True)
        return inv * (weighted - unit * jnp.mean(weighted * unit, axis=-1, keepdims=True)), g_gain

    d_mid, gain_two = norm_back(two.total(), mid_s[...], gain_row(1))
    g_mid = gall[at_t].astype(F32) + d_mid
    hid_ref[...] = g_mid
    gm[at_t] = g_mid.astype(BF)
    gm_gather = ZGather(k, gm, rows)
    turn_over(n1_s, xt_b)
    gate_g.third()
    g_kv[...] = jnp.zeros_like(g_kv)

    def attend_back(b):
        at_b = ds(b * rows, rows)
        mask = jnp.concatenate([bias[b]] * (group // 128), axis=1)
        g_block = dot(gm[at_b], wo_v[...])
        g_block = down_rows(g_block.astype(BF).astype(F32)).astype(BF)
        g_qs, g_keys, g_values = [], [], []
        for a in range(0, wide, group):
            q_one, g_one = qt_s[b, :, a:a + group], g_block[:, a:a + group]
            p = jnp.exp(dot(k_s[...], q_one) + mask - lse_s[b, :, a:a + group])
            dp = dot(v_s[...], g_one)
            delta = jnp.sum(p * dp, axis=0, keepdims=True)
            d_scores = (p * (dp - delta)).astype(BF)
            g_qs.append(dot(kt_s[...], d_scores))
            g_keys.append(dot(d_scores, q_one, 1, 1))
            g_values.append(dot(p.astype(BF), g_one, 1, 1))
        g_query = across(jnp.concatenate(g_qs, axis=1)) * scale
        cos, sin = cos_s[at_b], sin_s[at_b]
        for n in range(0, QW, pair):
            x = g_query[:, n:n + pair]
            g_qkv[at_b, n:n + pair] = (x * cos - swap_halves(x) * sin).astype(BF)
        g_kv[at_w] += jnp.concatenate([sum(g_keys), sum(g_values)], axis=1)

    attend_back(k.t)
    gm_gather.relay()
    branch = ZScatter(k, part2_b, slots2, middle_b, rows)
    for i in gm_gather.order:
        attend_back((k.t + T - gm_gather.arrival(i)) % T)
    g_kvb[...] = g_kv[...].astype(BF)
    kv_copies = {}
    for i in range(1, back + 1):
        piece = g_kvb.at[ds(((k.c + C - i) % C) * span, span)]
        kv_copies[i], _ = k.new(piece, kv_slots.at[i - 1], k.cpeer(C - i))
        k.start(kv_copies[i], k.c >= i)
    branch.relay()
    up_g.direct("c", 1)
    up_g.third()
    turn_over(gm, xt_a)
    out_g = Grad(k, xt_a, attn_s, QW, spare(wo_v, 0, QW), twin_out, relay_out, sum_out)
    out_g.first()
    own_kv = g_kv[at_c]
    for i, copy in kv_copies.items():
        pl.when(k.c + i < C)(copy.wait_recv)
        own_kv = own_kv + kv_slots[i - 1].astype(F32)
    g_qkv[:, QW:] = jnp.where(lane < hd, turn_back(own_kv), own_kv).astype(BF)
    k.finish([two.far] * two.line + list(two.copies.values()))

    @pl.loop(0, D // 256)
    def _(n):
        at = ds(n * 256, 256)
        part = dot(g_qkv[...], w_v[at], 1, 1)
        part_b[:, at] = part.astype(BF)
        gain_s[:, at] = jnp.sum(part * (h_s[:, at].astype(F32) * inv_s[...]), axis=0, keepdims=True)

    gain_one = gain_s[...]
    for b in range(F * C):
        gz[b] = jnp.concatenate(
            [gain_one[:, b * R:(b + 1) * R], gain_two[:, b * R:(b + 1) * R]], axis=1
        )
    z_copies = [k.send(gz, gz_slots.at[i - 1], k.zpeer(i)) for i in range(1, T)]
    last = ZScatter(k, part_b, slots, middle_a, rows)
    qkv_g = Grad(k, xt_b, g_qkv, QKV, spare(w_v, 0, QKV), twin_qkv, relay_qkv, sum_qkv)
    qkv_g.first()
    out_g.second(local.at[13])
    out_g.direct("f", 0)
    out_g.direct("c", 1)
    qkv_g.second(local.at[14])
    qkv_g.direct("f", 0)
    qkv_g.direct("c", 1)
    last.relay()
    out_ref[...] = (padc[at_t] * (mid_s[...] + branch.total())).astype(BF)
    out_g.third()
    both = gz[...]
    for i in range(1, T):
        z_copies[i - 1].wait_recv()
        both = both + gz_slots[i - 1]
    gx[...] = both
    x_copies = []
    for n, dev in enumerate(k.plane_peers()):
        x_copies.append(k.send(gx.at[dev[0] * C + dev[1]], gx_slots.at[n], dev))
    qkv_g.third()
    adding = ((down_g, down_v, all_down), (gate_g, gate_v, all_gate), (up_g, up_v, all_up))
    for n, (grad, room, _) in enumerate(adding):
        grad.collect(room, many.at[n])
    for n, (grad, _, result) in enumerate(adding):
        grad.add_up(result, local.at[10 + n])
    d_hid, _ = norm_back(last.total(), hidden_ref[...].astype(F32), gain_one_row)
    hid_ref[...] = hid_ref[...] + d_hid
    both = gx[mine]
    for n, copy in enumerate(x_copies):
        copy.wait_recv()
        both = both + gx_slots[n]
    gg_ref[...] = both
    for grad in (out_g, qkv_g):
        grad.done()
    for grad, _, _ in adding:
        grad.own.wait()
    k.finish()


def layer(sizes, hd, hidden, seg, pad, ga, gm, wq, wk, wv, wo, wd, cot, wg, wu):
    F, C, T = sizes
    H = C // 2
    rows, D = hidden.shape
    R, QW = wq.shape
    FB = wg.shape[1]
    span, length, QKV = rows * T, seg.shape[1], QW + 2 * hd
    vm = pl.BlockSpec(memory_space=pltpu.VMEM)
    hbm = pl.BlockSpec(memory_space=pl.ANY)
    wide = QW // hd * rows
    win = min(length, span + -(-DOC // span) * span)
    n_sems = n_semaphores(F, C, T)
    S = jax.ShapeDtypeStruct
    V = pltpu.VMEM
    FH, lines, diag = F * H, F + H - 1, max(1, (F - 1) * (H - 1))
    widths = (FB, FB, FB, QW, QKV)
    return pl.pallas_call(
        functools.partial(layer_kernel, sizes, hd),
        out_shape=(
            S((rows, D), BF), S((rows, D), F32), S((1, 2 * R), F32),
            *[S((lines, R, n), BF) for n in widths], *[S((R, FB), BF)] * 3,
        ),
        in_specs=[vm] * 4 + [hbm] * 9,
        out_specs=[vm] * 3 + [hbm] * 8,
        scratch_shapes=[
            V((D, QKV), BF), V((D, QW), BF), V((D, FB), BF), V((D, FB), BF), V((D, FB), BF),
            V((span, D), BF), V((span, D), BF), V((span, D), BF), V((span, D), BF), V((span, D), BF),
            V((D, span), BF), V((D, span), BF),
            V((span, FB), BF), V((span, FB), BF), V((span, FB), BF),
            V((T, hd, wide), BF), V((span, QW), BF), V((span, QKV), BF), V((T, 1, wide), F32),
            V((length, 2 * hd), BF), V((win, hd), BF), V((win, hd), BF), V((hd, win), BF), V((hd, win), BF),
            V((length, 2 * hd), F32), V((length, 2 * hd), BF), V((win // span - 1, span, 2 * hd), BF),
            V((T, win, 128), F32), V((span, 2 * hd), F32), V((span, 2 * hd), F32),
            V((span, 1), F32), V((1, D), F32), V((span, 1), F32),
            V((span, D), BF), V((span, D), BF), V((T - 1, rows, D), BF), V((T - 1, rows, D), BF),
            V((rows, D), BF), V((rows, D), BF), V((rows, D), F32),
            *[V((FH, R, n), BF) for n in widths],
            *[V((diag, 2, R // 2, n), BF) for n in widths],
            V((F * C, 1, 2 * R), F32), V((F * C, 1, 2 * R), F32), V((T - 1, F * C, 1, 2 * R), F32),
            V((F * C, 1, 2 * R), F32), V((F * C - 1, 1, 2 * R), F32),
            V((rows, D), BF), V((2 * hd, R), BF), V((QW, R), BF), V((FB, R), BF), V((rows, D), BF),
            pltpu.SemaphoreType.DMA((n_sems,)), pltpu.SemaphoreType.DMA((n_sems,)),
            pltpu.SemaphoreType.DMA((15,)), pltpu.SemaphoreType.DMA((3, lines - 1)),
        ],
        compiler_params=pltpu.CompilerParams(
            collective_id=0, has_side_effects=True, vmem_limit_bytes=62 * 2**20
        ),
        name="layer",
    )(seg, pad, ga, gm, hidden, wq, wk, wv, wo, wd, cot, wg, wu)


def final_kernel(
    hd, out_ref, hid_ref, gg_ref, down_ref, gate_ref, up_ref, wo_ref, qkv_ref,
    block_out, grad_hidden, gain_one, gain_two, g_query, g_key, g_value, g_out, g_gate, g_up, g_down,
):
    def total(ref):
        return sum(ref[i].astype(F32) for i in range(ref.shape[0]))

    QW, R = g_query.shape[1], gain_one.shape[0]
    block_out[...] = out_ref[...]
    grad_hidden[...] = hid_ref[...]
    gain_one[...] = gg_ref[:, :R].reshape(R)
    gain_two[...] = gg_ref[:, R:].reshape(R)
    qkv = total(qkv_ref)
    g_query[...] = qkv[:, :QW]
    kv = qkv[:, QW:].T
    g_key[...] = kv[:hd]
    g_value[...] = kv[hd:]
    g_out[...] = total(wo_ref).T
    g_gate[...] = gate_ref[...].astype(F32)
    g_up[...] = up_ref[...].astype(F32)
    g_down[...] = down_ref[...].astype(F32).T


def final(hd, block_out, grad_hidden, gg, s_out, s_qkv, down, gate, up):
    L, R, QW = s_out.shape
    FB = gate.shape[1]
    rows, D = block_out.shape
    steps = R // 128 if R % 128 == 0 else 1
    r = R // steps
    S = jax.ShapeDtypeStruct

    def parts(x):
        return pl.BlockSpec((L, r, x.shape[2]), lambda i: (0, i, 0))

    def tall(n):
        return pl.BlockSpec((r, n), lambda i: (i, 0))

    def wide(n):
        return pl.BlockSpec((n, r), lambda i: (0, i))

    acts = pl.BlockSpec((rows // steps, D), lambda i: (i, 0))
    gain = pl.BlockSpec((R,), lambda i: (0,))
    return pl.pallas_call(
        functools.partial(final_kernel, hd),
        grid=(steps,),
        out_shape=(
            S((rows, D), BF), S((rows, D), F32), S((R,), F32), S((R,), F32), S((R, QW), F32),
            S((hd, R), F32), S((hd, R), F32), S((QW, R), F32), S((R, FB), F32), S((R, FB), F32),
            S((FB, R), F32),
        ),
        in_specs=[acts, acts, pl.BlockSpec((1, 2 * R), lambda i: (0, 0))]
        + [tall(FB)] * 3 + [parts(s_out), parts(s_qkv)],
        out_specs=[acts, acts, gain, gain, tall(QW), wide(hd), wide(hd), wide(QW), tall(FB), tall(FB),
                   wide(FB)],
        compiler_params=pltpu.CompilerParams(vmem_limit_bytes=62 * 2**20),
        name="final",
    )(block_out, grad_hidden, gg, down, gate, up, s_out, s_qkv)


def body(hidden_in, segment_ids, pad_mask, attn_gain, w_query, w_key, w_value, w_out,
         mlp_gain, w_gate, w_up, w_down, cotangent):
    sizes = tuple(lax.axis_size(n) for n in ("fsdp", "context", "tensor"))
    hd = w_key.shape[1]
    block_out, grad_hidden, gg, _, _, _, s_out, s_qkv, down, gate, up = layer(
        sizes, hd, hidden_in[0], segment_ids, pad_mask, attn_gain, mlp_gain,
        w_query, w_key.T, w_value.T, w_out, w_down, cotangent[0], w_gate, w_up,
    )
    (block_out, grad_hidden, gain_one, gain_two, g_query, g_key, g_value, g_out, g_gate, g_up,
     g_down) = final(hd, block_out, grad_hidden, gg, s_out, s_qkv, down, gate, up)
    return (
        block_out[None], grad_hidden[None], gain_one, g_query, g_key.T, g_value.T, g_out, gain_two,
        g_gate, g_up, g_down,
    )


def solution(mesh):
    rows = P("fsdp", ("context", "tensor"), None)
    tail = (P(FC), P(FC, "tensor"), P(FC, "tensor"), P(FC, "tensor"), P("tensor", FC),
            P(FC), P(FC, "tensor"), P(FC, "tensor"), P("tensor", FC))
    in_specs = (rows, P("fsdp", None), P("fsdp", None)) + tail + (rows,)
    out_specs = (rows, rows) + tail
    return jax.shard_map(body, mesh=mesh, in_specs=in_specs, out_specs=out_specs, check_vma=False)
```

```python
import functools
import math

import jax
import jax.numpy as jnp
from jax import lax
from jax.experimental import pallas as pl
from jax.experimental.pallas import tpu as pltpu
from jax.sharding import PartitionSpec as P

EPS = 1e-05
NEG = -1e30
DOC = 512
BF = jnp.bfloat16
F32 = jnp.float32
MESH = pl.DeviceIdType.MESH
FC = ("fsdp", "context")


def dot(a, b, ca=1, cb=0):
    return lax.dot_general(a, b, (((ca,), (cb,)), ((), ())), preferred_element_type=F32)


def chunks(total, step):
    return [(at, min(step, total - at)) for at in range(0, total, step)]


def ds(start, size):
    return pl.ds(pl.multiple_of(start, size), size)


class Links:
    def __init__(self, sizes, send_sems, recv_sems):
        self.F, self.C, self.T = sizes
        self.f = lax.axis_index("fsdp")
        self.c = lax.axis_index("context")
        self.t = lax.axis_index("tensor")
        self.h = self.c // 2
        self.core = self.c % 2
        self.H = self.C // 2
        self.send_sems, self.recv_sems = send_sems, recv_sems
        self.used = 0
        self.open = []
        self.sib = (self.f, self.h * 2 + 1 - self.core, self.t)

    def chip(self, df, dh):
        return ((self.f + df) % self.F, ((self.h + dh) % self.H) * 2 + self.core, self.t)

    def block(self, df, dh, core):
        return ((self.f + df) % self.F) * self.C + ((self.h + dh) % self.H) * 2 + core

    def zpeer(self, i):
        return (self.f, self.c, (self.t + i) % self.T)

    def cpeer(self, i):
        return (self.f, (self.c + i) % self.C, self.t)

    def new(self, src, dst, dev, recv=None):
        n = self.used
        self.used += 1
        copy = pltpu.make_async_remote_copy(
            src_ref=src, dst_ref=dst, send_sem=self.send_sems.at[n],
            recv_sem=self.recv_sems.at[n if recv is None else recv],
            device_id=dev, device_id_type=MESH,
        )
        return copy, n

    def start(self, copy, cond=None):
        if cond is None:
            copy.start()
        else:
            pl.when(cond)(copy.start)
        self.open.append((copy, cond))

    def send(self, src, dst, dev):
        copy, _ = self.new(src, dst, dev)
        self.start(copy)
        return copy

    def plane_peers(self):
        return [
            ((self.f + df) % self.F, (self.c + dc) % self.C, self.t)
            for df in range(self.F) for dc in range(self.C) if df or dc
        ]

    def peers(self):
        return self.plane_peers() + [self.zpeer(i) for i in range(1, self.T)]

    def greet(self):
        self.bar = pltpu.get_barrier_semaphore()
        for dev in self.peers():
            pl.semaphore_signal(self.bar, inc=1, device_id=dev, device_id_type=MESH)

    def meet(self):
        pl.semaphore_wait(self.bar, len(self.peers()))

    def finish(self, copies=None):
        wanted = None if copies is None else [id(c) for c in copies]
        left = []
        for copy, cond in self.open:
            if wanted is not None and id(copy) not in wanted:
                left.append((copy, cond))
            elif cond is None:
                copy.wait_send()
            else:
                pl.when(cond)(copy.wait_send)
        self.open = left


class Gather:
    def __init__(self, links, full, rows):
        self.k, self.full, self.rows = links, full, rows
        self.line, self.twin, self.diag, self.split = {}, [], {}, False

    def part(self, df=0, dh=0, start=0, size=None):
        n = self.rows // 4
        block = self.k.block(-df, -dh, self.k.core)
        if size is None:
            return self.full.at[ds(block * self.rows, self.rows)]
        return self.full.at[pl.ds(pl.multiple_of(block * self.rows + start * n, n), size * n)]

    def some(self, own, along, start, size):
        k, n = self.k, self.rows // 4
        src, to = own.at[start * n:(start + size) * n], self.part(0, 0, start, size)
        for df in range(1, k.F) if "f" in along else ():
            self.line.setdefault((df, 0), []).append(k.send(src, to, k.chip(df, 0)))
        for dh in range(1, k.H) if "c" in along else ():
            self.line.setdefault((0, dh), []).append(k.send(src, to, k.chip(0, dh)))

    def sibling(self, own):
        self.twin.append(self.k.send(own, self.part(), self.k.sib))

    def first(self, own):
        self.some(own, "fc", 0, 4)
        self.sibling(own)

    def first_split(self, own):
        self.split = True
        self.some(own, "f", 0, 2)
        self.some(own, "c", 2, 2)
        self.some(own, "f", 2, 2)
        self.some(own, "c", 0, 2)
        self.sibling(own)

    def second(self):
        k = self.k
        for df, dh in sorted(self.line, reverse=True):
            copies = self.line[df, dh]
            for copy in copies[:1] if self.split else copies:
                copy.wait_recv()
            half = 0 if df else 1
            piece = self.part(df, dh, 2 * half, 2)
            if df:
                for eh in range(1, k.H):
                    self.diag[df, eh, half] = k.send(piece, piece, k.chip(0, eh))
            else:
                for ef in range(1, k.F):
                    self.diag[ef, dh, half] = k.send(piece, piece, k.chip(ef, 0))
        if not self.split:
            self.pass_on()

    def pass_on(self):
        for df, dh in sorted(self.line, reverse=True):
            for copy in self.line[df, dh][1:] if self.split else ():
                copy.wait_recv()
            whole = self.part(df, dh)
            self.twin.append(self.k.send(whole, whole, self.k.sib))

    def third(self):
        k = self.k
        if self.split:
            self.pass_on()
        for copy in self.diag.values():
            copy.wait_recv()
        for df in range(1, k.F):
            for dh in range(1, k.H):
                whole = self.part(df, dh)
                self.twin.append(k.send(whole, whole, k.sib))

    def done(self):
        for copy in self.twin:
            copy.wait_recv()

    def sent(self):
        lines = [copy for copies in self.line.values() for copy in copies]
        self.k.finish(lines + list(self.diag.values()) + self.twin)


class ZGather:
    def __init__(self, k, full, rows, own=None):
        self.k, self.full, self.rows = k, full, rows
        T = k.T
        piece = full.at[ds(k.t * rows, rows)]
        own = piece if own is None else own
        self.copies = {i: k.new(own, piece, k.zpeer(i)) for i in range(1, T)}
        for i in [2, 1, 3] if T == 4 else range(1, T):
            cond = None
            if T == 4 and i != 2:
                cond = (k.t < 3) if i == 1 else (k.t > 0)
            k.start(self.copies[i][0], cond)
        self.left = list(range(1, T))
        self.relays = []
        self.order = [2, 1, 3] if T == 4 else list(range(1, T))

    def relay(self):
        k = self.k
        if k.T != 4:
            return
        self.copies[2][0].wait_recv()
        self.left = [1, 3]
        for at, origin, i in ((2, 0, 3), (1, 3, 1)):
            piece = self.full.at[ds(origin * self.rows, self.rows)]
            copy, _ = k.new(piece, piece, (k.f, k.c, 3 - origin), recv=self.copies[i][1])
            k.start(copy, k.t == at)
            self.relays.append(copy)

    def sent(self):
        self.k.finish([c for c, _ in self.copies.values()] + self.relays)

    def wait(self):
        for i in self.left:
            self.copies[i][0].wait_recv()

    def arrival(self, i):
        if self.k.T != 4:
            self.copies[i][0].wait_recv()
            return i
        if i == 2:
            return i
        at_first = self.k.t == 0
        pl.when(at_first)(self.copies[4 - i][0].wait_recv)
        pl.when(jnp.logical_not(at_first))(self.copies[i][0].wait_recv)
        return jnp.where(at_first, 4 - i, i)


class ZScatter:
    def __init__(self, k, part, slots, middle, rows):
        self.k, self.part, self.slots, self.middle, self.rows = k, part, slots, middle, rows
        T = k.T
        self.line = T == 4
        self.end = (k.t == 0) | (k.t == T - 1)
        if self.line:
            src = part.at[ds((3 - k.t) * rows, rows)]
            self.far, _ = k.new(src, middle, (k.f, k.c, 1 + k.t // 3))
            k.start(self.far, self.end)
        self.copies = {}
        for i in range(1, T):
            src = part.at[ds(((k.t + i) % T) * rows, rows)]
            self.copies[i], _ = k.new(src, slots.at[i - 1], k.zpeer(i))
        if self.line:
            k.start(self.copies[2], self.end)
            k.start(self.copies[1], k.t < 3)
            k.start(self.copies[3], k.t > 0)
        else:
            for i in range(1, T):
                k.start(self.copies[i])

    def relay(self):
        k = self.k
        if not self.line:
            return
        inner = (k.t > 0) & (k.t < 3)

        @pl.when(inner)
        def _():
            self.far.wait_recv()
            at = ds(((k.t + 2) % 4) * self.rows, self.rows)
            both = self.part[at].astype(F32) + self.middle[...].astype(F32)
            self.part[at] = both.astype(BF)
            self.copies[2].start()

        k.open.append((self.copies[2], inner))

    def total(self):
        k = self.k
        for i in range(1, k.T):
            if not self.line or i == 2:
                self.copies[i].wait_recv()
                continue
            there = (k.t > 0) if i == 1 else (k.t < 3)
            pl.when(there)(self.copies[i].wait_recv)

            @pl.when(jnp.logical_not(there))
            def _():
                self.slots[i - 1] = jnp.zeros(self.slots.shape[1:], BF)

        total = self.part[ds(k.t * self.rows, self.rows)].astype(F32)
        for i in range(1, k.T):
            total = total + self.slots[i - 1].astype(F32)
        return total


class Grad:
    def __init__(self, k, xt, y, width, stage, twin, relay, out):
        self.k, self.xt, self.y, self.width, self.stage = k, xt, y, width, stage
        self.twin, self.relay, self.out = twin, relay, out
        self.R = xt.shape[0] // (k.F * k.C)

    def rows_of(self, s, core):
        return ds(self.k.block(s // self.k.H, s % self.k.H, core) * self.R, self.R)

    def piece(self, df, dh, half=None):
        s = df * self.k.H + dh
        if half is None:
            return self.twin.at[s]
        n = self.R // 2
        return self.twin.at[s, half * n:(half + 1) * n]

    def first(self):
        k = self.k

        @pl.loop(0, k.F * k.H)
        def _(s):
            x = self.xt[self.rows_of(s, 1 - k.core)]
            to = self.stage(s)
            for a, n in chunks(self.width, 256):
                to[:, a:a + n] = dot(x, self.y[:, a:a + n]).astype(BF)

        self.twins = [k.send(self.stage(s), self.twin.at[s], k.sib) for s in range(k.F * k.H)]

    def second(self, sem):
        k = self.k
        for copy in self.twins:
            copy.wait_recv()

        @pl.loop(0, k.F * k.H)
        def _(s):
            x = self.xt[self.rows_of(s, k.core)]
            for a, n in chunks(self.width, 256):
                total = dot(x, self.y[:, a:a + n]) + self.twin[s, :, a:a + n].astype(F32)
                self.twin[s, :, a:a + n] = total.astype(BF)

        self.diag, self.far = {}, []
        n = 0
        for df in range(1, k.F):
            for dh in range(1, k.H):
                for half, dev in ((0, k.chip(df, 0)), (1, k.chip(0, dh))):
                    self.diag[df, dh, half] = n, half, k.send(
                        self.piece(df, dh, half), self.relay.at[n, half], dev
                    )
                n += 1
        self.own = None
        if sem is not None:
            self.own = pltpu.make_async_copy(self.piece(0, 0), self.out.at[0], sem)
            self.own.start()

    def direct(self, along, half):
        k = self.k
        n = self.R // 2
        at = slice(half * n, half * n + n)
        if along == "c":
            for dh in range(1, k.H):
                to = self.out.at[k.F - 1 + dh, at]
                self.far.append(k.send(self.piece(0, dh, half), to, k.chip(0, dh)))
        else:
            for df in range(1, k.F):
                self.far.append(k.send(self.piece(df, 0, half), self.out.at[df, at], k.chip(df, 0)))

    def add(self, df, dh, half):
        piece = self.piece(df, dh, half)
        total = piece[...].astype(F32)
        for (ef, eh, other), (n, _, copy) in self.diag.items():
            if other == half and (ef == df or df == 0) and (eh == dh or dh == 0):
                copy.wait_recv()
                total = total + self.relay[n, half].astype(F32)
        piece[...] = total.astype(BF)

    def third(self, along="fc"):
        k = self.k
        if "f" in along:
            for df in range(1, k.F):
                if k.H > 1:
                    self.add(df, 0, 1)
            self.direct("f", 1)
        if "c" in along:
            for dh in range(1, k.H):
                if k.F > 1:
                    self.add(0, dh, 0)
            self.direct("c", 0)

    def done(self):
        for copy in self.far:
            copy.wait_recv()
        if self.own is not None:
            self.own.wait()

    def collect(self, room, sems):
        self.done()
        lines = self.k.F + self.k.H - 1
        first = self.k.F * self.k.H * self.R
        self.room, self.first_row = room, first
        self.loads = [
            pltpu.make_async_copy(
                self.out.at[n], room.at[first + (n - 1) * self.R:first + n * self.R], sems.at[n - 1]
            )
            for n in range(1, lines)
        ]
        for copy in self.loads:
            copy.start()

    def add_up(self, result, sem):
        for copy in self.loads:
            copy.wait()
        step = min(self.R, 64)

        @pl.loop(0, self.R // step)
        def _(n):
            total = self.twin[0, ds(n * step, step)].astype(F32)
            for i in range(len(self.loads)):
                total = total + self.room[ds(self.first_row + i * self.R + n * step, step)].astype(F32)
            self.twin[0, ds(n * step, step)] = total.astype(BF)

        self.own = pltpu.make_async_copy(self.twin.at[0], result, sem)
        self.own.start()


def n_semaphores(F, C, T):
    H = C // 2
    a, b, d = F - 1, H - 1, (F - 1) * (H - 1)
    gather = a + b + 1 + 2 * d + a + b + d
    grad = F * H + 2 * d + 2 * (a + b)
    return 5 * gather + 4 * (a + b) + 5 * grad + 2 * (F * C - 1) + 2 * (C - 1) + 9 * (T + 1)


def layer_kernel(
    sizes, hd,
    seg_hbm, pad_hbm, ga_hbm, gm_hbm,
    hidden_hbm, wq_hbm, wk_hbm, wv_hbm, wo_hbm, wd_hbm, cot_hbm, wg_hbm, wu_hbm,
    out_ref, hid_ref, gg_ref, sum_down, sum_gate, sum_up, sum_out, sum_qkv, all_down, all_gate, all_up,
    w_v, wo_v, gate_v, up_v, down_v, h_s, n1_s, n2_s, gall, gm, xt_a, xt_b, inner, g_gate, g_up,
    qt_s, attn_s, g_qkv, lse_s, kv_s, k_s, v_s, kt_s, vt_s, g_kv, g_kvb, kv_slots, bias, cos_s, sin_s,
    inv_s, gain_s,
    padc, part_b, part2_b, slots, slots2, middle_a, middle_b, mid_s,
    twin_down, twin_gate, twin_up, twin_out, twin_qkv,
    relay_down, relay_gate, relay_up, relay_out, relay_qkv,
    gains_s, gz, gz_slots, gx, gx_slots, hidden_ref, kvw_ref, wo_ref, wd_ref, cot_ref, seg_ref, pad_ref, ga_ref, gm_ref, sends, recvs, local, many,
):
    k = Links(sizes, sends, recvs)
    T, F, C, H = k.T, k.F, k.C, k.H
    rows, D = hidden_ref.shape
    R, QW = wq_hbm.shape
    FB = wg_hbm.shape[1]
    span, length = gall.shape[0], seg_hbm.shape[1]
    nh = QW // hd
    QKV = QW + 2 * hd
    pair = 2 * hd
    scale = hd ** (-0.5)
    at_t = ds(k.t * rows, rows)
    at_c = ds(k.c * span, span)
    back = k_s.shape[0] // span - 1
    kv_s[...] = jnp.zeros_like(kv_s)
    kv_slots[...] = jnp.zeros_like(kv_slots)
    k.greet()

    aw, ow, gw, uw, dw = (Gather(k, full, R) for full in (w_v, wo_v, gate_v, up_v, down_v))
    mine = k.block(0, 0, k.core)
    own_w, own_o = aw.part(), ow.part()
    loads = [
        pltpu.make_async_copy(src, dst, local.at[n])
        for n, (src, dst) in enumerate((
            (wk_hbm, kvw_ref.at[:hd]), (wv_hbm, kvw_ref.at[hd:]), (wo_hbm, wo_ref),
            (wq_hbm, own_w.at[:, :QW]), (hidden_hbm, hidden_ref), (hidden_hbm, h_s.at[at_t]),
            (wd_hbm, wd_ref), (cot_hbm, cot_ref), (seg_hbm, seg_ref), (pad_hbm, pad_ref),
            (ga_hbm, ga_ref), (gm_hbm, gm_ref), (wg_hbm, gw.part()), (wu_hbm, uw.part()),
        ))
    ]
    for copy in loads:
        copy.start()
    for copy in loads[10:12]:
        copy.wait()
    gains_s[mine, :, :R] = ga_ref[...].astype(F32).reshape(1, R)
    gains_s[mine, :, R:] = gm_ref[...].astype(F32).reshape(1, R)
    for copy in loads[:4]:
        copy.wait()
    own_w[:, QW:] = kvw_ref[...].astype(F32).T.astype(BF)
    own_o[...] = wo_ref[...].astype(F32).T.astype(BF)
    k.meet()
    h_gather = ZGather(k, h_s, rows, hidden_hbm)
    own_gain = gains_s.at[mine]
    gain_copies = [k.send(own_gain, own_gain, dev) for dev in k.plane_peers()]
    aw.first(own_w)
    ow.first(own_o)

    def gain_row(which):
        return jnp.concatenate(
            [gains_s[b][:, which * R:(which + 1) * R] for b in range(F * C)], axis=1
        )

    for copy in loads[4:10]:
        copy.wait()
    down_v[ds(mine * R, R)] = wd_ref[...].astype(F32).T.astype(BF)

    def column_of(row):
        return jnp.broadcast_to(row.astype(F32), (8, span)).T[:, :1]

    seg = seg_ref[...].astype(F32)
    seg_row = seg_ref[:, at_c].astype(F32)
    seg_col = column_of(seg_row)
    padc[...] = column_of(pad_ref[:, at_c])
    win = k_s.shape[0]
    win_at = jnp.maximum(k.c * span + span - win, 0)
    at_w = pl.ds(pl.multiple_of(win_at, span), win)
    row_at = k.c * span + lax.broadcasted_iota(jnp.int32, (span, 1), 0)
    first = jnp.sum(jnp.where(seg < seg_col, 1.0, 0.0), axis=1, keepdims=True)
    lane = lax.broadcasted_iota(jnp.int32, (1, pair), 1)
    frequency = jnp.exp(-((lane % (hd // 2)).astype(F32) * (2.0 / hd)) * math.log(10000.0))
    low = (lane % hd) < (hd // 2)
    angles = (row_at.astype(F32) - first) * frequency
    cos_s[...] = jnp.cos(angles)
    sin_s[...] = jnp.where(low, -1.0, 1.0) * jnp.sin(angles)

    def tall_column(row):
        return jnp.broadcast_to(row.astype(F32), (8, win)).T[:, :1]

    key_at = win_at + lax.broadcasted_iota(jnp.int32, (win, span), 0)
    token_at = k.c * span + lax.broadcasted_iota(jnp.int32, (win, span), 1)
    allowed = (tall_column(seg_ref[:, at_w]) == seg_row) & (key_at <= token_at) & (
        (tall_column(pad_ref[:, at_w]) == 1.0) | (key_at == token_at)
    )
    terms = jnp.where(allowed, 0.0, NEG)
    for b in range(T):
        one = terms[:, b * rows:(b + 1) * rows]
        bias[b] = jnp.concatenate([one] * (128 // rows), axis=1)
    keep = padc[at_t]
    gall[at_t] = (cot_ref[...].astype(F32) * keep).astype(BF)

    def swap_halves(x):
        return jnp.where(low, pltpu.roll(x, pair - hd // 2, 1), pltpu.roll(x, hd // 2, 1))

    def turn(x):
        return x * cos_s[...] + swap_halves(x) * sin_s[...]

    def turn_back(x):
        return x * cos_s[...] - swap_halves(x) * sin_s[...]

    h_gather.relay()
    aw.second()
    ow.second()
    gw.some(wg_hbm, "f", 0, 4)
    gw.some(wg_hbm, "c", 0, 2)
    gw.sibling(wg_hbm)
    aw.third()
    for copy in gain_copies:
        copy.wait_recv()
    gain_one_row = gain_row(0)
    h_gather.wait()

    @pl.loop(0, T)
    def _(n):
        at = ds(n * rows, rows)
        h = h_s[at].astype(F32)
        inv = lax.rsqrt(jnp.mean(h * h, axis=-1, keepdims=True) + EPS)
        inv_s[at] = inv
        n1_s[at] = (h * inv * gain_one_row).astype(BF)

    g_gather = ZGather(k, gall, rows)
    aw.done()

    def down_rows(x):
        t = x.T
        return jnp.concatenate([t[n * hd:(n + 1) * hd] for n in range(nh)], axis=1)

    def across(x):
        t = x.T
        return jnp.concatenate([t[n * rows:(n + 1) * rows] for n in range(nh)], axis=1)

    pre = dot(n1_s[...], w_v[:, QW:])
    kv_s[at_c] = jnp.where(lane < hd, turn(pre), pre).astype(BF)
    own_kv = kv_s.at[at_c]
    kv_copies = {}
    for i in range(1, back + 1):
        kv_copies[i], _ = k.new(own_kv, own_kv, k.cpeer(i))
        k.start(kv_copies[i], k.c + i < C)
    gw.some(wg_hbm, "c", 2, 2)
    turned = []
    for at, n in chunks(QW, 256):
        pre = dot(n1_s[...], w_v[:, at:at + n])
        turned += [turn(pre[:, b:b + pair]) * scale for b in range(0, n, pair)]
    turned = jnp.concatenate(turned, axis=1)
    for b in range(T):
        qt_s[b] = down_rows(turned[b * rows:(b + 1) * rows]).astype(BF)
    ow.third()
    for i, copy in kv_copies.items():
        pl.when(k.c >= i)(copy.wait_recv)
    k_s[...] = kv_s[at_w, :hd]
    v_s[...] = kv_s[at_w, hd:]
    kvt = kv_s[at_w].astype(F32).T.astype(BF)
    kt_s[...] = kvt[:hd]
    vt_s[...] = kvt[hd:]
    uw.first(wu_hbm)
    g_gather.relay()
    wide = nh * rows
    group = min(256, wide)

    @pl.loop(0, T)
    def _(b):
        mask = jnp.concatenate([bias[b]] * (group // 128), axis=1)
        outs = []
        for a in range(0, wide, group):
            scores = dot(k_s[...], qt_s[b, :, a:a + group]) + mask
            top = jnp.max(scores, axis=0, keepdims=True)
            weights = jnp.exp(scores - top)
            total = jnp.sum(weights, axis=0, keepdims=True)
            outs.append(dot(vt_s[...], (weights * (1.0 / total)).astype(BF)))
            lse_s[b, :, a:a + group] = top + jnp.log(total)
        attn_s[ds(b * rows, rows)] = across(jnp.concatenate(outs, axis=1)).astype(BF)

    ow.done()

    @pl.loop(0, D // 256)
    def _(n):
        at = ds(n * 256, 256)
        part_b[:, at] = dot(attn_s[...], wo_v[at], 1, 1).astype(BF)

    h_gather.sent()
    one = ZScatter(k, part_b, slots, middle_a, rows)
    gw.second()
    one.relay()

    def turn_over(src, dst):
        @pl.loop(0, D // 256)
        def _(n):
            at = ds(n * 256, 256)
            dst[at] = src[:, at].astype(F32).T.astype(BF)

    g_gather.wait()
    turn_over(gall, xt_a)
    uw.second()
    dw.first_split(dw.part())
    mid = hidden_ref[...].astype(F32) + one.total()
    mid_s[...] = mid
    scale_two = lax.rsqrt(jnp.mean(mid * mid, axis=-1, keepdims=True) + EPS)
    n2_s[at_t] = (mid * scale_two * gain_row(1)).astype(BF)
    n2_gather = ZGather(k, n2_s, rows)
    n2_gather.relay()
    gw.third()
    uw.third()
    gw.done()
    uw.done()
    for copy in loads[12:]:
        copy.wait()
    n2_gather.wait()

    for at, n in chunks(FB, 256):
        gate = dot(n2_s[...], gate_v[:, at:at + n])
        up = dot(n2_s[...], up_v[:, at:at + n])
        sig = jax.nn.sigmoid(gate)
        inner[:, at:at + n] = (gate * sig * up).astype(BF)
        g_gate[:, at:at + n] = (up * sig * (1.0 + gate * (1.0 - sig))).astype(BF)
        g_up[:, at:at + n] = (gate * sig).astype(BF)

    down_g = Grad(k, xt_a, inner, FB, lambda s: twin_up.at[s], twin_down, relay_down, sum_down)
    down_g.first()
    dw.second()
    turn_over(n2_s, xt_b)
    down_g.second(None)
    down_g.direct("f", 0)
    down_g.direct("c", 1)
    k.finish(down_g.twins)
    dw.third()
    dw.done()
    for at, n in chunks(FB, 256):
        g_in = dot(gall[...], down_v[:, at:at + n])
        g_gate[:, at:at + n] = (g_in * g_gate[:, at:at + n].astype(F32)).astype(BF)
        g_up[:, at:at + n] = (g_in * g_up[:, at:at + n].astype(F32)).astype(BF)

    k.finish([one.far] * one.line + list(one.copies.values()))

    @pl.loop(0, D // 256)
    def _(n):
        at = ds(n * 256, 256)
        part = dot(g_gate[...], gate_v[at], 1, 1) + dot(g_up[...], up_v[at], 1, 1)
        part_b[:, at] = part.astype(BF)

    two = ZScatter(k, part_b, slots, middle_a, rows)
    for weight in (aw, ow, gw, uw, dw):
        weight.sent()

    def spare(room, lane, width):
        return lambda s: room.at[ds(s * R, R), lane:lane + width]

    gate_g = Grad(k, xt_b, g_gate, FB, spare(gate_v, 0, FB), twin_gate, relay_gate, sum_gate)
    up_g = Grad(k, xt_b, g_up, FB, spare(up_v, 0, FB), twin_up, relay_up, sum_up)
    down_g.third()
    gate_g.first()
    up_g.first()
    two.relay()
    gate_g.second(None)
    gate_g.direct("f", 0)
    gate_g.direct("c", 1)
    up_g.second(None)
    up_g.direct("f", 0)

    @pl.loop(0, D // 256)
    def _(n):
        at = ds(n * 256, 256)
        part2_b[:, at] = dot(inner[...], down_v[at], 1, 1).astype(BF)

    def norm_back(grad, vectors, gain):
        inv = lax.rsqrt(jnp.mean(vectors * vectors, axis=-1, keepdims=True) + EPS)
        unit = vectors * inv
        weighted = grad * gain
        g_gain = jnp.sum(grad * unit, axis=0, keepdims=True)
        return inv * (weighted - unit * jnp.mean(weighted * unit, axis=-1, keepdims=True)), g_gain

    d_mid, gain_two = norm_back(two.total(), mid_s[...], gain_row(1))
    g_mid = gall[at_t].astype(F32) + d_mid
    hid_ref[...] = g_mid
    gm[at_t] = g_mid.astype(BF)
    gm_gather = ZGather(k, gm, rows)
    turn_over(n1_s, xt_b)
    gate_g.third()
    g_kv[...] = jnp.zeros_like(g_kv)

    def attend_back(b):
        at_b = ds(b * rows, rows)
        mask = jnp.concatenate([bias[b]] * (group // 128), axis=1)
        g_block = dot(gm[at_b], wo_v[...])
        g_block = down_rows(g_block.astype(BF).astype(F32)).astype(BF)
        g_qs, g_keys, g_values = [], [], []
        for a in range(0, wide, group):
            q_one, g_one = qt_s[b, :, a:a + group], g_block[:, a:a + group]
            p = jnp.exp(dot(k_s[...], q_one) + mask - lse_s[b, :, a:a + group])
            dp = dot(v_s[...], g_one)
            delta = jnp.sum(p * dp, axis=0, keepdims=True)
            d_scores = (p * (dp - delta)).astype(BF)
            g_qs.append(dot(kt_s[...], d_scores))
            g_keys.append(dot(d_scores, q_one, 1, 1))
            g_values.append(dot(p.astype(BF), g_one, 1, 1))
        g_query = across(jnp.concatenate(g_qs, axis=1)) * scale
        cos, sin = cos_s[at_b], sin_s[at_b]
        for n in range(0, QW, pair):
            x = g_query[:, n:n + pair]
            g_qkv[at_b, n:n + pair] = (x * cos - swap_halves(x) * sin).astype(BF)
        g_kv[at_w] += jnp.concatenate([sum(g_keys), sum(g_values)], axis=1)

    attend_back(k.t)
    gm_gather.relay()
    branch = ZScatter(k, part2_b, slots2, middle_b, rows)
    for i in gm_gather.order:
        attend_back((k.t + T - gm_gather.arrival(i)) % T)
    g_kvb[...] = g_kv[...].astype(BF)
    kv_copies = {}
    for i in range(1, back + 1):
        piece = g_kvb.at[ds(((k.c + C - i) % C) * span, span)]
        kv_copies[i], _ = k.new(piece, kv_slots.at[i - 1], k.cpeer(C - i))
        k.start(kv_copies[i], k.c >= i)
    branch.relay()
    up_g.direct("c", 1)
    up_g.third()
    turn_over(gm, xt_a)
    out_g = Grad(k, xt_a, attn_s, QW, spare(wo_v, 0, QW), twin_out, relay_out, sum_out)
    out_g.first()
    own_kv = g_kv[at_c]
    for i, copy in kv_copies.items():
        pl.when(k.c + i < C)(copy.wait_recv)
        own_kv = own_kv + kv_slots[i - 1].astype(F32)
    g_qkv[:, QW:] = jnp.where(lane < hd, turn_back(own_kv), own_kv).astype(BF)
    k.finish([two.far] * two.line + list(two.copies.values()))

    @pl.loop(0, D // 256)
    def _(n):
        at = ds(n * 256, 256)
        part = dot(g_qkv[...], w_v[at], 1, 1)
        part_b[:, at] = part.astype(BF)
        gain_s[:, at] = jnp.sum(part * (h_s[:, at].astype(F32) * inv_s[...]), axis=0, keepdims=True)

    gain_one = gain_s[...]
    for b in range(F * C):
        gz[b] = jnp.concatenate(
            [gain_one[:, b * R:(b + 1) * R], gain_two[:, b * R:(b + 1) * R]], axis=1
        )
    z_copies = [k.send(gz, gz_slots.at[i - 1], k.zpeer(i)) for i in range(1, T)]
    last = ZScatter(k, part_b, slots, middle_a, rows)
    qkv_g = Grad(k, xt_b, g_qkv, QKV, spare(w_v, 0, QKV), twin_qkv, relay_qkv, sum_qkv)
    qkv_g.first()
    out_g.second(local.at[17])
    out_g.direct("f", 0)
    out_g.direct("c", 1)
    qkv_g.second(local.at[18])
    qkv_g.direct("f", 0)
    qkv_g.direct("c", 1)
    last.relay()
    out_ref[...] = (padc[at_t] * (mid_s[...] + branch.total())).astype(BF)
    out_g.third()
    both = gz[...]
    for i in range(1, T):
        z_copies[i - 1].wait_recv()
        both = both + gz_slots[i - 1]
    gx[...] = both
    x_copies = []
    for n, dev in enumerate(k.plane_peers()):
        x_copies.append(k.send(gx.at[dev[0] * C + dev[1]], gx_slots.at[n], dev))
    qkv_g.third()
    adding = ((down_g, down_v, all_down), (gate_g, gate_v, all_gate), (up_g, up_v, all_up))
    for n, (grad, room, _) in enumerate(adding):
        grad.collect(room, many.at[n])
    for n, (grad, _, result) in enumerate(adding):
        grad.add_up(result, local.at[14 + n])
    d_hid, _ = norm_back(last.total(), hidden_ref[...].astype(F32), gain_one_row)
    hid_ref[...] = hid_ref[...] + d_hid
    both = gx[mine]
    for n, copy in enumerate(x_copies):
        copy.wait_recv()
        both = both + gx_slots[n]
    gg_ref[...] = both
    for grad in (out_g, qkv_g):
        grad.done()
    for grad, _, _ in adding:
        grad.own.wait()
    k.finish()


def layer(sizes, hd, hidden, seg, pad, ga, gm, wq, wk, wv, wo, wd, cot, wg, wu):
    F, C, T = sizes
    H = C // 2
    rows, D = hidden.shape
    R, QW = wq.shape
    FB = wg.shape[1]
    span, length, QKV = rows * T, seg.shape[1], QW + 2 * hd
    vm = pl.BlockSpec(memory_space=pltpu.VMEM)
    hbm = pl.BlockSpec(memory_space=pl.ANY)
    wide = QW // hd * rows
    win = min(length, span + -(-DOC // span) * span)
    n_sems = n_semaphores(F, C, T)
    S = jax.ShapeDtypeStruct
    V = pltpu.VMEM
    FH, lines, diag = F * H, F + H - 1, max(1, (F - 1) * (H - 1))
    widths = (FB, FB, FB, QW, QKV)
    return pl.pallas_call(
        functools.partial(layer_kernel, sizes, hd),
        out_shape=(
            S((rows, D), BF), S((rows, D), F32), S((1, 2 * R), F32),
            *[S((lines, R, n), BF) for n in widths], *[S((R, FB), BF)] * 3,
        ),
        in_specs=[hbm] * 13,
        out_specs=[vm] * 3 + [hbm] * 8,
        scratch_shapes=[
            V((D, QKV), BF), V((D, QW), BF), V((D, FB), BF), V((D, FB), BF), V((D, FB), BF),
            V((span, D), BF), V((span, D), BF), V((span, D), BF), V((span, D), BF), V((span, D), BF),
            V((D, span), BF), V((D, span), BF),
            V((span, FB), BF), V((span, FB), BF), V((span, FB), BF),
            V((T, hd, wide), BF), V((span, QW), BF), V((span, QKV), BF), V((T, 1, wide), F32),
            V((length, 2 * hd), BF), V((win, hd), BF), V((win, hd), BF), V((hd, win), BF), V((hd, win), BF),
            V((length, 2 * hd), F32), V((length, 2 * hd), BF), V((win // span - 1, span, 2 * hd), BF),
            V((T, win, 128), F32), V((span, 2 * hd), F32), V((span, 2 * hd), F32),
            V((span, 1), F32), V((1, D), F32), V((span, 1), F32),
            V((span, D), BF), V((span, D), BF), V((T - 1, rows, D), BF), V((T - 1, rows, D), BF),
            V((rows, D), BF), V((rows, D), BF), V((rows, D), F32),
            *[V((FH, R, n), BF) for n in widths],
            *[V((diag, 2, R // 2, n), BF) for n in widths],
            V((F * C, 1, 2 * R), F32), V((F * C, 1, 2 * R), F32), V((T - 1, F * C, 1, 2 * R), F32),
            V((F * C, 1, 2 * R), F32), V((F * C - 1, 1, 2 * R), F32),
            V((rows, D), BF), V((2 * hd, R), BF), V((QW, R), BF), V((FB, R), BF), V((rows, D), BF),
            V((1, length), jnp.int32), V((1, length), jnp.int32), V((R,), BF), V((R,), BF),
            pltpu.SemaphoreType.DMA((n_sems,)), pltpu.SemaphoreType.DMA((n_sems,)),
            pltpu.SemaphoreType.DMA((19,)), pltpu.SemaphoreType.DMA((3, lines - 1)),
        ],
        compiler_params=pltpu.CompilerParams(
            collective_id=0, has_side_effects=True, vmem_limit_bytes=62 * 2**20
        ),
        name="layer",
    )(seg, pad, ga, gm, hidden, wq, wk, wv, wo, wd, cot, wg, wu)


def final_kernel(
    hd, out_ref, hid_ref, gg_ref, down_ref, gate_ref, up_ref, wo_ref, qkv_ref,
    block_out, grad_hidden, gain_one, gain_two, g_query, g_key, g_value, g_out, g_gate, g_up, g_down,
):
    def total(ref):
        return sum(ref[i].astype(F32) for i in range(ref.shape[0]))

    QW, R = g_query.shape[1], gain_one.shape[0]
    block_out[...] = out_ref[...]
    grad_hidden[...] = hid_ref[...]
    gain_one[...] = gg_ref[:, :R].reshape(R)
    gain_two[...] = gg_ref[:, R:].reshape(R)
    qkv = total(qkv_ref)
    g_query[...] = qkv[:, :QW]
    kv = qkv[:, QW:].T
    g_key[...] = kv[:hd]
    g_value[...] = kv[hd:]
    g_out[...] = total(wo_ref).T
    g_gate[...] = gate_ref[...].astype(F32)
    g_up[...] = up_ref[...].astype(F32)
    g_down[...] = down_ref[...].astype(F32).T


def final(hd, block_out, grad_hidden, gg, s_out, s_qkv, down, gate, up):
    L, R, QW = s_out.shape
    FB = gate.shape[1]
    rows, D = block_out.shape
    steps = R // 128 if R % 128 == 0 else 1
    r = R // steps
    S = jax.ShapeDtypeStruct

    def parts(x):
        return pl.BlockSpec((L, r, x.shape[2]), lambda i: (0, i, 0))

    def tall(n):
        return pl.BlockSpec((r, n), lambda i: (i, 0))

    def wide(n):
        return pl.BlockSpec((n, r), lambda i: (0, i))

    acts = pl.BlockSpec((rows // steps, D), lambda i: (i, 0))
    gain = pl.BlockSpec((R,), lambda i: (0,))
    return pl.pallas_call(
        functools.partial(final_kernel, hd),
        grid=(steps,),
        out_shape=(
            S((rows, D), BF), S((rows, D), F32), S((R,), F32), S((R,), F32), S((R, QW), F32),
            S((hd, R), F32), S((hd, R), F32), S((QW, R), F32), S((R, FB), F32), S((R, FB), F32),
            S((FB, R), F32),
        ),
        in_specs=[acts, acts, pl.BlockSpec((1, 2 * R), lambda i: (0, 0))]
        + [tall(FB)] * 3 + [parts(s_out), parts(s_qkv)],
        out_specs=[acts, acts, gain, gain, tall(QW), wide(hd), wide(hd), wide(QW), tall(FB), tall(FB),
                   wide(FB)],
        compiler_params=pltpu.CompilerParams(vmem_limit_bytes=62 * 2**20),
        name="final",
    )(block_out, grad_hidden, gg, down, gate, up, s_out, s_qkv)


def body(hidden_in, segment_ids, pad_mask, attn_gain, w_query, w_key, w_value, w_out,
         mlp_gain, w_gate, w_up, w_down, cotangent):
    sizes = tuple(lax.axis_size(n) for n in ("fsdp", "context", "tensor"))
    hd = w_key.shape[1]
    block_out, grad_hidden, gg, _, _, _, s_out, s_qkv, down, gate, up = layer(
        sizes, hd, hidden_in[0], segment_ids, pad_mask, attn_gain, mlp_gain,
        w_query, w_key.T, w_value.T, w_out, w_down, cotangent[0], w_gate, w_up,
    )
    (block_out, grad_hidden, gain_one, gain_two, g_query, g_key, g_value, g_out, g_gate, g_up,
     g_down) = final(hd, block_out, grad_hidden, gg, s_out, s_qkv, down, gate, up)
    return (
        block_out[None], grad_hidden[None], gain_one, g_query, g_key.T, g_value.T, g_out, gain_two,
        g_gate, g_up, g_down,
    )


def solution(mesh):
    rows = P("fsdp", ("context", "tensor"), None)
    tail = (P(FC), P(FC, "tensor"), P(FC, "tensor"), P(FC, "tensor"), P("tensor", FC),
            P(FC), P(FC, "tensor"), P(FC, "tensor"), P("tensor", FC))
    in_specs = (rows, P("fsdp", None), P("fsdp", None)) + tail + (rows,)
    out_specs = (rows, rows) + tail
    return jax.shard_map(body, mesh=mesh, in_specs=in_specs, out_specs=out_specs, check_vma=False)
```

```python
import functools
import math

import jax
import jax.numpy as jnp
from jax import lax
from jax.experimental import pallas as pl
from jax.experimental.pallas import tpu as pltpu
from jax.sharding import PartitionSpec as P

EPS = 1e-05
NEG = -1e30
DOC = 512
BF = jnp.bfloat16
F32 = jnp.float32
MESH = pl.DeviceIdType.MESH
FC = ("fsdp", "context")


def dot(a, b, ca=1, cb=0):
    return lax.dot_general(a, b, (((ca,), (cb,)), ((), ())), preferred_element_type=F32)


def chunks(total, step):
    return [(at, min(step, total - at)) for at in range(0, total, step)]


def ds(start, size):
    return pl.ds(pl.multiple_of(start, size), size)


class Links:
    def __init__(self, sizes, send_sems, recv_sems):
        self.F, self.C, self.T = sizes
        self.f = lax.axis_index("fsdp")
        self.c = lax.axis_index("context")
        self.t = lax.axis_index("tensor")
        self.h = self.c // 2
        self.core = self.c % 2
        self.H = self.C // 2
        self.send_sems, self.recv_sems = send_sems, recv_sems
        self.used = 0
        self.open = []
        self.sib = (self.f, self.h * 2 + 1 - self.core, self.t)

    def chip(self, df, dh):
        return ((self.f + df) % self.F, ((self.h + dh) % self.H) * 2 + self.core, self.t)

    def block(self, df, dh, core):
        return ((self.f + df) % self.F) * self.C + ((self.h + dh) % self.H) * 2 + core

    def zpeer(self, i):
        return (self.f, self.c, (self.t + i) % self.T)

    def cpeer(self, i):
        return (self.f, (self.c + i) % self.C, self.t)

    def new(self, src, dst, dev, recv=None):
        n = self.used
        self.used += 1
        copy = pltpu.make_async_remote_copy(
            src_ref=src, dst_ref=dst, send_sem=self.send_sems.at[n],
            recv_sem=self.recv_sems.at[n if recv is None else recv],
            device_id=dev, device_id_type=MESH,
        )
        return copy, n

    def start(self, copy, cond=None):
        if cond is None:
            copy.start()
        else:
            pl.when(cond)(copy.start)
        self.open.append((copy, cond))

    def send(self, src, dst, dev):
        copy, _ = self.new(src, dst, dev)
        self.start(copy)
        return copy

    def plane_peers(self):
        return [
            ((self.f + df) % self.F, (self.c + dc) % self.C, self.t)
            for df in range(self.F) for dc in range(self.C) if df or dc
        ]

    def peers(self):
        return self.plane_peers() + [self.zpeer(i) for i in range(1, self.T)]

    def greet(self):
        self.bar = pltpu.get_barrier_semaphore()
        for dev in self.peers():
            pl.semaphore_signal(self.bar, inc=1, device_id=dev, device_id_type=MESH)

    def meet(self):
        pl.semaphore_wait(self.bar, len(self.peers()))

    def finish(self, copies=None):
        wanted = None if copies is None else [id(c) for c in copies]
        left = []
        for copy, cond in self.open:
            if wanted is not None and id(copy) not in wanted:
                left.append((copy, cond))
            elif cond is None:
                copy.wait_send()
            else:
                pl.when(cond)(copy.wait_send)
        self.open = left


class Gather:
    def __init__(self, links, full, rows):
        self.k, self.full, self.rows = links, full, rows
        self.line, self.twin, self.diag, self.split = {}, [], {}, False

    def part(self, df=0, dh=0, start=0, size=None):
        n = self.rows // 4
        block = self.k.block(-df, -dh, self.k.core)
        if size is None:
            return self.full.at[ds(block * self.rows, self.rows)]
        return self.full.at[pl.ds(pl.multiple_of(block * self.rows + start * n, n), size * n)]

    def some(self, own, along, start, size):
        k, n = self.k, self.rows // 4
        src, to = own.at[start * n:(start + size) * n], self.part(0, 0, start, size)
        for df in range(1, k.F) if "f" in along else ():
            self.line.setdefault((df, 0), []).append(k.send(src, to, k.chip(df, 0)))
        for dh in range(1, k.H) if "c" in along else ():
            self.line.setdefault((0, dh), []).append(k.send(src, to, k.chip(0, dh)))

    def lanes(self, own, lanes):
        k = self.k
        to = self.part().at[:, lanes]
        for df in range(1, k.F):
            self.line.setdefault((df, 0), []).append(k.send(own, to, k.chip(df, 0)))
        for dh in range(1, k.H):
            self.line.setdefault((0, dh), []).append(k.send(own, to, k.chip(0, dh)))

    def sibling(self, own):
        self.twin.append(self.k.send(own, self.part(), self.k.sib))

    def first(self, own):
        self.some(own, "fc", 0, 4)
        self.sibling(own)

    def first_split(self, own):
        self.split = True
        self.some(own, "f", 0, 2)
        self.some(own, "c", 2, 2)
        self.some(own, "f", 2, 2)
        self.some(own, "c", 0, 2)
        self.sibling(own)

    def second(self):
        k = self.k
        for df, dh in sorted(self.line, reverse=True):
            copies = self.line[df, dh]
            for copy in copies[:1] if self.split else copies:
                copy.wait_recv()
            half = 0 if df else 1
            piece = self.part(df, dh, 2 * half, 2)
            if df:
                for eh in range(1, k.H):
                    self.diag[df, eh, half] = k.send(piece, piece, k.chip(0, eh))
            else:
                for ef in range(1, k.F):
                    self.diag[ef, dh, half] = k.send(piece, piece, k.chip(ef, 0))
        if not self.split:
            self.pass_on()

    def pass_on(self):
        for df, dh in sorted(self.line, reverse=True):
            for copy in self.line[df, dh][1:] if self.split else ():
                copy.wait_recv()
            whole = self.part(df, dh)
            self.twin.append(self.k.send(whole, whole, self.k.sib))

    def third(self):
        k = self.k
        if self.split:
            self.pass_on()
        for copy in self.diag.values():
            copy.wait_recv()
        for df in range(1, k.F):
            for dh in range(1, k.H):
                whole = self.part(df, dh)
                self.twin.append(k.send(whole, whole, k.sib))

    def done(self):
        for copy in self.twin:
            copy.wait_recv()

    def sent(self):
        lines = [copy for copies in self.line.values() for copy in copies]
        self.k.finish(lines + list(self.diag.values()) + self.twin)


class ZGather:
    def __init__(self, k, full, rows, own=None):
        self.k, self.full, self.rows = k, full, rows
        T = k.T
        piece = full.at[ds(k.t * rows, rows)]
        own = piece if own is None else own
        self.copies = {i: k.new(own, piece, k.zpeer(i)) for i in range(1, T)}
        for i in [2, 1, 3] if T == 4 else range(1, T):
            cond = None
            if T == 4 and i != 2:
                cond = (k.t < 3) if i == 1 else (k.t > 0)
            k.start(self.copies[i][0], cond)
        self.left = list(range(1, T))
        self.relays = []
        self.order = [2, 1, 3] if T == 4 else list(range(1, T))

    def relay(self):
        k = self.k
        if k.T != 4:
            return
        self.copies[2][0].wait_recv()
        self.left = [1, 3]
        for at, origin, i in ((2, 0, 3), (1, 3, 1)):
            piece = self.full.at[ds(origin * self.rows, self.rows)]
            copy, _ = k.new(piece, piece, (k.f, k.c, 3 - origin), recv=self.copies[i][1])
            k.start(copy, k.t == at)
            self.relays.append(copy)

    def sent(self):
        self.k.finish([c for c, _ in self.copies.values()] + self.relays)

    def wait(self):
        for i in self.left:
            self.copies[i][0].wait_recv()

    def arrival(self, i):
        if self.k.T != 4:
            self.copies[i][0].wait_recv()
            return i
        if i == 2:
            return i
        at_first = self.k.t == 0
        pl.when(at_first)(self.copies[4 - i][0].wait_recv)
        pl.when(jnp.logical_not(at_first))(self.copies[i][0].wait_recv)
        return jnp.where(at_first, 4 - i, i)


class ZScatter:
    def __init__(self, k, part, slots, middle, rows):
        self.k, self.part, self.slots, self.middle, self.rows = k, part, slots, middle, rows
        T = k.T
        self.line = T == 4
        self.end = (k.t == 0) | (k.t == T - 1)
        if self.line:
            src = part.at[ds((3 - k.t) * rows, rows)]
            self.far, _ = k.new(src, middle, (k.f, k.c, 1 + k.t // 3))
            k.start(self.far, self.end)
        self.copies = {}
        for i in range(1, T):
            src = part.at[ds(((k.t + i) % T) * rows, rows)]
            self.copies[i], _ = k.new(src, slots.at[i - 1], k.zpeer(i))
        if self.line:
            k.start(self.copies[2], self.end)
            k.start(self.copies[1], k.t < 3)
            k.start(self.copies[3], k.t > 0)
        else:
            for i in range(1, T):
                k.start(self.copies[i])

    def relay(self):
        k = self.k
        if not self.line:
            return
        inner = (k.t > 0) & (k.t < 3)

        @pl.when(inner)
        def _():
            self.far.wait_recv()
            at = ds(((k.t + 2) % 4) * self.rows, self.rows)
            both = self.part[at].astype(F32) + self.middle[...].astype(F32)
            self.part[at] = both.astype(BF)
            self.copies[2].start()

        k.open.append((self.copies[2], inner))

    def total(self):
        k = self.k
        for i in range(1, k.T):
            if not self.line or i == 2:
                self.copies[i].wait_recv()
                continue
            there = (k.t > 0) if i == 1 else (k.t < 3)
            pl.when(there)(self.copies[i].wait_recv)

            @pl.when(jnp.logical_not(there))
            def _():
                self.slots[i - 1] = jnp.zeros(self.slots.shape[1:], BF)

        total = self.part[ds(k.t * self.rows, self.rows)].astype(F32)
        for i in range(1, k.T):
            total = total + self.slots[i - 1].astype(F32)
        return total


class Grad:
    def __init__(self, k, xt, y, width, stage, twin, relay, out):
        self.k, self.xt, self.y, self.width, self.stage = k, xt, y, width, stage
        self.twin, self.relay, self.out = twin, relay, out
        self.R = xt.shape[0] // (k.F * k.C)

    def rows_of(self, s, core):
        return ds(self.k.block(s // self.k.H, s % self.k.H, core) * self.R, self.R)

    def piece(self, df, dh, half=None):
        s = df * self.k.H + dh
        if half is None:
            return self.twin.at[s]
        n = self.R // 2
        return self.twin.at[s, half * n:(half + 1) * n]

    def first(self):
        k = self.k

        @pl.loop(0, k.F * k.H)
        def _(s):
            x = self.xt[self.rows_of(s, 1 - k.core)]
            to = self.stage(s)
            for a, n in chunks(self.width, 256):
                to[:, a:a + n] = dot(x, self.y[:, a:a + n]).astype(BF)

        self.twins = [k.send(self.stage(s), self.twin.at[s], k.sib) for s in range(k.F * k.H)]

    def second(self, sem):
        k = self.k
        for copy in self.twins:
            copy.wait_recv()

        @pl.loop(0, k.F * k.H)
        def _(s):
            x = self.xt[self.rows_of(s, k.core)]
            for a, n in chunks(self.width, 256):
                total = dot(x, self.y[:, a:a + n]) + self.twin[s, :, a:a + n].astype(F32)
                self.twin[s, :, a:a + n] = total.astype(BF)

        self.diag, self.far = {}, []
        n = 0
        for df in range(1, k.F):
            for dh in range(1, k.H):
                for half, dev in ((0, k.chip(df, 0)), (1, k.chip(0, dh))):
                    self.diag[df, dh, half] = n, half, k.send(
                        self.piece(df, dh, half), self.relay.at[n, half], dev
                    )
                n += 1
        self.own = None
        if sem is not None:
            self.own = pltpu.make_async_copy(self.piece(0, 0), self.out.at[0], sem)
            self.own.start()

    def direct(self, along, half):
        k = self.k
        n = self.R // 2
        at = slice(half * n, half * n + n)
        if along == "c":
            for dh in range(1, k.H):
                to = self.out.at[k.F - 1 + dh, at]
                self.far.append(k.send(self.piece(0, dh, half), to, k.chip(0, dh)))
        else:
            for df in range(1, k.F):
                self.far.append(k.send(self.piece(df, 0, half), self.out.at[df, at], k.chip(df, 0)))

    def add(self, df, dh, half):
        piece = self.piece(df, dh, half)
        total = piece[...].astype(F32)
        for (ef, eh, other), (n, _, copy) in self.diag.items():
            if other == half and (ef == df or df == 0) and (eh == dh or dh == 0):
                copy.wait_recv()
                total = total + self.relay[n, half].astype(F32)
        piece[...] = total.astype(BF)

    def third(self, along="fc"):
        k = self.k
        if "f" in along:
            for df in range(1, k.F):
                if k.H > 1:
                    self.add(df, 0, 1)
            self.direct("f", 1)
        if "c" in along:
            for dh in range(1, k.H):
                if k.F > 1:
                    self.add(0, dh, 0)
            self.direct("c", 0)

    def done(self):
        for copy in self.far:
            copy.wait_recv()
        if self.own is not None:
            self.own.wait()

    def collect(self, room, sems):
        self.done()
        lines = self.k.F + self.k.H - 1
        first = self.k.F * self.k.H * self.R
        self.room, self.first_row = room, first
        self.loads = [
            pltpu.make_async_copy(
                self.out.at[n], room.at[first + (n - 1) * self.R:first + n * self.R], sems.at[n - 1]
            )
            for n in range(1, lines)
        ]
        for copy in self.loads:
            copy.start()

    def add_up(self, result, sem):
        for copy in self.loads:
            copy.wait()
        step = min(self.R, 64)

        @pl.loop(0, self.R // step)
        def _(n):
            total = self.twin[0, ds(n * step, step)].astype(F32)
            for i in range(len(self.loads)):
                total = total + self.room[ds(self.first_row + i * self.R + n * step, step)].astype(F32)
            self.twin[0, ds(n * step, step)] = total.astype(BF)

        self.own = pltpu.make_async_copy(self.twin.at[0], result, sem)
        self.own.start()


def n_semaphores(F, C, T):
    H = C // 2
    a, b, d = F - 1, H - 1, (F - 1) * (H - 1)
    gather = a + b + 1 + 2 * d + a + b + d
    grad = F * H + 2 * d + 2 * (a + b)
    return 5 * gather + 4 * (a + b) + 5 * grad + 2 * (F * C - 1) + 2 * (C - 1) + 9 * (T + 1)


def layer_kernel(
    sizes, hd,
    seg_hbm, pad_hbm, ga_hbm, gm_hbm,
    hidden_hbm, wq_hbm, wk_hbm, wv_hbm, wo_hbm, wd_hbm, cot_hbm, wg_hbm, wu_hbm,
    out_ref, hid_ref, gg_ref, sum_down, sum_gate, sum_up, sum_out, sum_qkv, all_down, all_gate, all_up,
    w_v, wo_v, gate_v, up_v, down_v, h_s, n1_s, n2_s, gall, gm, xt_a, xt_b, inner, g_gate, g_up,
    qt_s, attn_s, g_qkv, lse_s, kv_s, k_s, v_s, kt_s, vt_s, g_kv, g_kvb, kv_slots, bias, cos_s, sin_s,
    inv_s, gain_s,
    padc, part_b, part2_b, slots, slots2, middle_a, middle_b, mid_s,
    twin_down, twin_gate, twin_up, twin_out, twin_qkv,
    relay_down, relay_gate, relay_up, relay_out, relay_qkv,
    gains_s, gz, gz_slots, gx, gx_slots, hidden_ref, kvw_ref, wo_ref, wd_ref, cot_ref, seg_ref, pad_ref, ga_ref, gm_ref, sends, recvs, local, many,
):
    k = Links(sizes, sends, recvs)
    T, F, C, H = k.T, k.F, k.C, k.H
    rows, D = hidden_ref.shape
    R, QW = wq_hbm.shape
    FB = wg_hbm.shape[1]
    span, length = gall.shape[0], seg_hbm.shape[1]
    nh = QW // hd
    QKV = QW + 2 * hd
    pair = 2 * hd
    scale = hd ** (-0.5)
    at_t = ds(k.t * rows, rows)
    at_c = ds(k.c * span, span)
    back = k_s.shape[0] // span - 1
    kv_s[...] = jnp.zeros_like(kv_s)
    kv_slots[...] = jnp.zeros_like(kv_slots)
    k.greet()

    aw, ow, gw, uw, dw = (Gather(k, full, R) for full in (w_v, wo_v, gate_v, up_v, down_v))
    mine = k.block(0, 0, k.core)
    own_w, own_o = aw.part(), ow.part()
    loads = [
        pltpu.make_async_copy(src, dst, local.at[n])
        for n, (src, dst) in enumerate((
            (wk_hbm, kvw_ref.at[:hd]), (wv_hbm, kvw_ref.at[hd:]), (wo_hbm, wo_ref),
            (wq_hbm, own_w.at[:, :QW]), (hidden_hbm, hidden_ref), (hidden_hbm, h_s.at[at_t]),
            (wd_hbm, wd_ref), (cot_hbm, cot_ref), (seg_hbm, seg_ref), (pad_hbm, pad_ref),
            (ga_hbm, ga_ref), (gm_hbm, gm_ref), (wg_hbm, gw.part()), (wu_hbm, uw.part()),
        ))
    ]
    for copy in loads:
        copy.start()
    k.meet()
    h_gather = ZGather(k, h_s, rows, hidden_hbm)
    aw.lanes(wq_hbm, slice(0, QW))
    for copy in loads[10:12]:
        copy.wait()
    gains_s[mine, :, :R] = ga_ref[...].astype(F32).reshape(1, R)
    gains_s[mine, :, R:] = gm_ref[...].astype(F32).reshape(1, R)
    for copy in loads[:4]:
        copy.wait()
    own_w[:, QW:] = kvw_ref[...].astype(F32).T.astype(BF)
    own_o[...] = wo_ref[...].astype(F32).T.astype(BF)
    own_gain = gains_s.at[mine]
    gain_copies = [k.send(own_gain, own_gain, dev) for dev in k.plane_peers()]
    aw.lanes(own_w.at[:, QW:], slice(QW, QKV))
    aw.sibling(own_w)
    ow.first(own_o)

    def gain_row(which):
        return jnp.concatenate(
            [gains_s[b][:, which * R:(which + 1) * R] for b in range(F * C)], axis=1
        )

    for copy in loads[4:10]:
        copy.wait()
    down_v[ds(mine * R, R)] = wd_ref[...].astype(F32).T.astype(BF)

    def column_of(row):
        return jnp.broadcast_to(row.astype(F32), (8, span)).T[:, :1]

    seg = seg_ref[...].astype(F32)
    seg_row = seg_ref[:, at_c].astype(F32)
    seg_col = column_of(seg_row)
    padc[...] = column_of(pad_ref[:, at_c])
    win = k_s.shape[0]
    win_at = jnp.maximum(k.c * span + span - win, 0)
    at_w = pl.ds(pl.multiple_of(win_at, span), win)
    row_at = k.c * span + lax.broadcasted_iota(jnp.int32, (span, 1), 0)
    first = jnp.sum(jnp.where(seg < seg_col, 1.0, 0.0), axis=1, keepdims=True)
    lane = lax.broadcasted_iota(jnp.int32, (1, pair), 1)
    frequency = jnp.exp(-((lane % (hd // 2)).astype(F32) * (2.0 / hd)) * math.log(10000.0))
    low = (lane % hd) < (hd // 2)
    angles = (row_at.astype(F32) - first) * frequency
    cos_s[...] = jnp.cos(angles)
    sin_s[...] = jnp.where(low, -1.0, 1.0) * jnp.sin(angles)

    def tall_column(row):
        return jnp.broadcast_to(row.astype(F32), (8, win)).T[:, :1]

    key_at = win_at + lax.broadcasted_iota(jnp.int32, (win, span), 0)
    token_at = k.c * span + lax.broadcasted_iota(jnp.int32, (win, span), 1)
    allowed = (tall_column(seg_ref[:, at_w]) == seg_row) & (key_at <= token_at) & (
        (tall_column(pad_ref[:, at_w]) == 1.0) | (key_at == token_at)
    )
    terms = jnp.where(allowed, 0.0, NEG)
    for b in range(T):
        one = terms[:, b * rows:(b + 1) * rows]
        bias[b] = jnp.concatenate([one] * (128 // rows), axis=1)
    keep = padc[at_t]
    gall[at_t] = (cot_ref[...].astype(F32) * keep).astype(BF)

    def swap_halves(x):
        return jnp.where(low, pltpu.roll(x, pair - hd // 2, 1), pltpu.roll(x, hd // 2, 1))

    def turn(x):
        return x * cos_s[...] + swap_halves(x) * sin_s[...]

    def turn_back(x):
        return x * cos_s[...] - swap_halves(x) * sin_s[...]

    h_gather.relay()
    aw.second()
    ow.second()
    gw.some(wg_hbm, "f", 0, 4)
    gw.some(wg_hbm, "c", 0, 2)
    gw.sibling(wg_hbm)
    aw.third()
    for copy in gain_copies:
        copy.wait_recv()
    gain_one_row = gain_row(0)
    h_gather.wait()

    @pl.loop(0, T)
    def _(n):
        at = ds(n * rows, rows)
        h = h_s[at].astype(F32)
        inv = lax.rsqrt(jnp.mean(h * h, axis=-1, keepdims=True) + EPS)
        inv_s[at] = inv
        n1_s[at] = (h * inv * gain_one_row).astype(BF)

    g_gather = ZGather(k, gall, rows)
    aw.done()

    def down_rows(x):
        t = x.T
        return jnp.concatenate([t[n * hd:(n + 1) * hd] for n in range(nh)], axis=1)

    def across(x):
        t = x.T
        return jnp.concatenate([t[n * rows:(n + 1) * rows] for n in range(nh)], axis=1)

    pre = dot(n1_s[...], w_v[:, QW:])
    kv_s[at_c] = jnp.where(lane < hd, turn(pre), pre).astype(BF)
    own_kv = kv_s.at[at_c]
    kv_copies = {}
    for i in range(1, back + 1):
        kv_copies[i], _ = k.new(own_kv, own_kv, k.cpeer(i))
        k.start(kv_copies[i], k.c + i < C)
    gw.some(wg_hbm, "c", 2, 2)
    turned = []
    for at, n in chunks(QW, 256):
        pre = dot(n1_s[...], w_v[:, at:at + n])
        turned += [turn(pre[:, b:b + pair]) * scale for b in range(0, n, pair)]
    turned = jnp.concatenate(turned, axis=1)
    for b in range(T):
        qt_s[b] = down_rows(turned[b * rows:(b + 1) * rows]).astype(BF)
    ow.third()
    for i, copy in kv_copies.items():
        pl.when(k.c >= i)(copy.wait_recv)
    k_s[...] = kv_s[at_w, :hd]
    v_s[...] = kv_s[at_w, hd:]
    kvt = kv_s[at_w].astype(F32).T.astype(BF)
    kt_s[...] = kvt[:hd]
    vt_s[...] = kvt[hd:]
    uw.first(wu_hbm)
    g_gather.relay()
    wide = nh * rows
    group = min(256, wide)

    @pl.loop(0, T)
    def _(b):
        mask = jnp.concatenate([bias[b]] * (group // 128), axis=1)
        outs = []
        for a in range(0, wide, group):
            scores = dot(k_s[...], qt_s[b, :, a:a + group]) + mask
            top = jnp.max(scores, axis=0, keepdims=True)
            weights = jnp.exp(scores - top)
            total = jnp.sum(weights, axis=0, keepdims=True)
            outs.append(dot(vt_s[...], (weights * (1.0 / total)).astype(BF)))
            lse_s[b, :, a:a + group] = top + jnp.log(total)
        attn_s[ds(b * rows, rows)] = across(jnp.concatenate(outs, axis=1)).astype(BF)

    ow.done()

    @pl.loop(0, D // 256)
    def _(n):
        at = ds(n * 256, 256)
        part_b[:, at] = dot(attn_s[...], wo_v[at], 1, 1).astype(BF)

    h_gather.sent()
    one = ZScatter(k, part_b, slots, middle_a, rows)
    gw.second()
    one.relay()

    def turn_over(src, dst):
        @pl.loop(0, D // 256)
        def _(n):
            at = ds(n * 256, 256)
            dst[at] = src[:, at].astype(F32).T.astype(BF)

    g_gather.wait()
    turn_over(gall, xt_a)
    uw.second()
    dw.first_split(dw.part())
    mid = hidden_ref[...].astype(F32) + one.total()
    mid_s[...] = mid
    scale_two = lax.rsqrt(jnp.mean(mid * mid, axis=-1, keepdims=True) + EPS)
    n2_s[at_t] = (mid * scale_two * gain_row(1)).astype(BF)
    n2_gather = ZGather(k, n2_s, rows)
    n2_gather.relay()
    gw.third()
    uw.third()
    gw.done()
    uw.done()
    for copy in loads[12:]:
        copy.wait()
    n2_gather.wait()

    for at, n in chunks(FB, 256):
        gate = dot(n2_s[...], gate_v[:, at:at + n])
        up = dot(n2_s[...], up_v[:, at:at + n])
        sig = jax.nn.sigmoid(gate)
        inner[:, at:at + n] = (gate * sig * up).astype(BF)
        g_gate[:, at:at + n] = (up * sig * (1.0 + gate * (1.0 - sig))).astype(BF)
        g_up[:, at:at + n] = (gate * sig).astype(BF)

    down_g = Grad(k, xt_a, inner, FB, lambda s: twin_up.at[s], twin_down, relay_down, sum_down)
    down_g.first()
    dw.second()
    turn_over(n2_s, xt_b)
    down_g.second(None)
    down_g.direct("f", 0)
    down_g.direct("c", 1)
    k.finish(down_g.twins)
    dw.third()
    dw.done()
    for at, n in chunks(FB, 256):
        g_in = dot(gall[...], down_v[:, at:at + n])
        g_gate[:, at:at + n] = (g_in * g_gate[:, at:at + n].astype(F32)).astype(BF)
        g_up[:, at:at + n] = (g_in * g_up[:, at:at + n].astype(F32)).astype(BF)

    k.finish([one.far] * one.line + list(one.copies.values()))

    @pl.loop(0, D // 256)
    def _(n):
        at = ds(n * 256, 256)
        part = dot(g_gate[...], gate_v[at], 1, 1) + dot(g_up[...], up_v[at], 1, 1)
        part_b[:, at] = part.astype(BF)

    two = ZScatter(k, part_b, slots, middle_a, rows)
    for weight in (aw, ow, gw, uw, dw):
        weight.sent()

    def spare(room, lane, width):
        return lambda s: room.at[ds(s * R, R), lane:lane + width]

    gate_g = Grad(k, xt_b, g_gate, FB, spare(gate_v, 0, FB), twin_gate, relay_gate, sum_gate)
    up_g = Grad(k, xt_b, g_up, FB, spare(up_v, 0, FB), twin_up, relay_up, sum_up)
    down_g.third()
    gate_g.first()
    up_g.first()
    two.relay()
    gate_g.second(None)
    gate_g.direct("f", 0)
    gate_g.direct("c", 1)
    up_g.second(None)
    up_g.direct("f", 0)

    @pl.loop(0, D // 256)
    def _(n):
        at = ds(n * 256, 256)
        part2_b[:, at] = dot(inner[...], down_v[at], 1, 1).astype(BF)

    def norm_back(grad, vectors, gain):
        inv = lax.rsqrt(jnp.mean(vectors * vectors, axis=-1, keepdims=True) + EPS)
        unit = vectors * inv
        weighted = grad * gain
        g_gain = jnp.sum(grad * unit, axis=0, keepdims=True)
        return inv * (weighted - unit * jnp.mean(weighted * unit, axis=-1, keepdims=True)), g_gain

    d_mid, gain_two = norm_back(two.total(), mid_s[...], gain_row(1))
    g_mid = gall[at_t].astype(F32) + d_mid
    hid_ref[...] = g_mid
    gm[at_t] = g_mid.astype(BF)
    gm_gather = ZGather(k, gm, rows)
    turn_over(n1_s, xt_b)
    gate_g.third()
    g_kv[...] = jnp.zeros_like(g_kv)

    def attend_back(b):
        at_b = ds(b * rows, rows)
        mask = jnp.concatenate([bias[b]] * (group // 128), axis=1)
        g_block = dot(gm[at_b], wo_v[...])
        g_block = down_rows(g_block.astype(BF).astype(F32)).astype(BF)
        g_qs, g_keys, g_values = [], [], []
        for a in range(0, wide, group):
            q_one, g_one = qt_s[b, :, a:a + group], g_block[:, a:a + group]
            p = jnp.exp(dot(k_s[...], q_one) + mask - lse_s[b, :, a:a + group])
            dp = dot(v_s[...], g_one)
            delta = jnp.sum(p * dp, axis=0, keepdims=True)
            d_scores = (p * (dp - delta)).astype(BF)
            g_qs.append(dot(kt_s[...], d_scores))
            g_keys.append(dot(d_scores, q_one, 1, 1))
            g_values.append(dot(p.astype(BF), g_one, 1, 1))
        g_query = across(jnp.concatenate(g_qs, axis=1)) * scale
        cos, sin = cos_s[at_b], sin_s[at_b]
        for n in range(0, QW, pair):
            x = g_query[:, n:n + pair]
            g_qkv[at_b, n:n + pair] = (x * cos - swap_halves(x) * sin).astype(BF)
        g_kv[at_w] += jnp.concatenate([sum(g_keys), sum(g_values)], axis=1)

    attend_back(k.t)
    gm_gather.relay()
    branch = ZScatter(k, part2_b, slots2, middle_b, rows)
    for i in gm_gather.order:
        attend_back((k.t + T - gm_gather.arrival(i)) % T)
    g_kvb[...] = g_kv[...].astype(BF)
    kv_copies = {}
    for i in range(1, back + 1):
        piece = g_kvb.at[ds(((k.c + C - i) % C) * span, span)]
        kv_copies[i], _ = k.new(piece, kv_slots.at[i - 1], k.cpeer(C - i))
        k.start(kv_copies[i], k.c >= i)
    branch.relay()
    up_g.direct("c", 1)
    up_g.third()
    turn_over(gm, xt_a)
    out_g = Grad(k, xt_a, attn_s, QW, spare(wo_v, 0, QW), twin_out, relay_out, sum_out)
    out_g.first()
    own_kv = g_kv[at_c]
    for i, copy in kv_copies.items():
        pl.when(k.c + i < C)(copy.wait_recv)
        own_kv = own_kv + kv_slots[i - 1].astype(F32)
    g_qkv[:, QW:] = jnp.where(lane < hd, turn_back(own_kv), own_kv).astype(BF)
    k.finish([two.far] * two.line + list(two.copies.values()))

    @pl.loop(0, D // 256)
    def _(n):
        at = ds(n * 256, 256)
        part = dot(g_qkv[...], w_v[at], 1, 1)
        part_b[:, at] = part.astype(BF)
        gain_s[:, at] = jnp.sum(part * (h_s[:, at].astype(F32) * inv_s[...]), axis=0, keepdims=True)

    gain_one = gain_s[...]
    for b in range(F * C):
        gz[b] = jnp.concatenate(
            [gain_one[:, b * R:(b + 1) * R], gain_two[:, b * R:(b + 1) * R]], axis=1
        )
    z_copies = [k.send(gz, gz_slots.at[i - 1], k.zpeer(i)) for i in range(1, T)]
    last = ZScatter(k, part_b, slots, middle_a, rows)
    qkv_g = Grad(k, xt_b, g_qkv, QKV, spare(w_v, 0, QKV), twin_qkv, relay_qkv, sum_qkv)
    qkv_g.first()
    out_g.second(local.at[17])
    out_g.direct("f", 0)
    out_g.direct("c", 1)
    qkv_g.second(local.at[18])
    qkv_g.direct("f", 0)
    qkv_g.direct("c", 1)
    last.relay()
    out_ref[...] = (padc[at_t] * (mid_s[...] + branch.total())).astype(BF)
    out_g.third()
    both = gz[...]
    for i in range(1, T):
        z_copies[i - 1].wait_recv()
        both = both + gz_slots[i - 1]
    gx[...] = both
    x_copies = []
    for n, dev in enumerate(k.plane_peers()):
        x_copies.append(k.send(gx.at[dev[0] * C + dev[1]], gx_slots.at[n], dev))
    qkv_g.third()
    adding = ((down_g, down_v, all_down), (gate_g, gate_v, all_gate), (up_g, up_v, all_up))
    for n, (grad, room, _) in enumerate(adding):
        grad.collect(room, many.at[n])
    for n, (grad, _, result) in enumerate(adding):
        grad.add_up(result, local.at[14 + n])
    d_hid, _ = norm_back(last.total(), hidden_ref[...].astype(F32), gain_one_row)
    hid_ref[...] = hid_ref[...] + d_hid
    both = gx[mine]
    for n, copy in enumerate(x_copies):
        copy.wait_recv()
        both = both + gx_slots[n]
    gg_ref[...] = both
    for grad in (out_g, qkv_g):
        grad.done()
    for grad, _, _ in adding:
        grad.own.wait()
    k.finish()


def layer(sizes, hd, hidden, seg, pad, ga, gm, wq, wk, wv, wo, wd, cot, wg, wu):
    F, C, T = sizes
    H = C // 2
    rows, D = hidden.shape
    R, QW = wq.shape
    FB = wg.shape[1]
    span, length, QKV = rows * T, seg.shape[1], QW + 2 * hd
    vm = pl.BlockSpec(memory_space=pltpu.VMEM)
    hbm = pl.BlockSpec(memory_space=pl.ANY)
    wide = QW // hd * rows
    win = min(length, span + -(-DOC // span) * span)
    n_sems = n_semaphores(F, C, T)
    S = jax.ShapeDtypeStruct
    V = pltpu.VMEM
    FH, lines, diag = F * H, F + H - 1, max(1, (F - 1) * (H - 1))
    widths = (FB, FB, FB, QW, QKV)
    return pl.pallas_call(
        functools.partial(layer_kernel, sizes, hd),
        out_shape=(
            S((rows, D), BF), S((rows, D), F32), S((1, 2 * R), F32),
            *[S((lines, R, n), BF) for n in widths], *[S((R, FB), BF)] * 3,
        ),
        in_specs=[hbm] * 13,
        out_specs=[vm] * 3 + [hbm] * 8,
        scratch_shapes=[
            V((D, QKV), BF), V((D, QW), BF), V((D, FB), BF), V((D, FB), BF), V((D, FB), BF),
            V((span, D), BF), V((span, D), BF), V((span, D), BF), V((span, D), BF), V((span, D), BF),
            V((D, span), BF), V((D, span), BF),
            V((span, FB), BF), V((span, FB), BF), V((span, FB), BF),
            V((T, hd, wide), BF), V((span, QW), BF), V((span, QKV), BF), V((T, 1, wide), F32),
            V((length, 2 * hd), BF), V((win, hd), BF), V((win, hd), BF), V((hd, win), BF), V((hd, win), BF),
            V((length, 2 * hd), F32), V((length, 2 * hd), BF), V((win // span - 1, span, 2 * hd), BF),
            V((T, win, 128), F32), V((span, 2 * hd), F32), V((span, 2 * hd), F32),
            V((span, 1), F32), V((1, D), F32), V((span, 1), F32),
            V((span, D), BF), V((span, D), BF), V((T - 1, rows, D), BF), V((T - 1, rows, D), BF),
            V((rows, D), BF), V((rows, D), BF), V((rows, D), F32),
            *[V((FH, R, n), BF) for n in widths],
            *[V((diag, 2, R // 2, n), BF) for n in widths],
            V((F * C, 1, 2 * R), F32), V((F * C, 1, 2 * R), F32), V((T - 1, F * C, 1, 2 * R), F32),
            V((F * C, 1, 2 * R), F32), V((F * C - 1, 1, 2 * R), F32),
            V((rows, D), BF), V((2 * hd, R), BF), V((QW, R), BF), V((FB, R), BF), V((rows, D), BF),
            V((1, length), jnp.int32), V((1, length), jnp.int32), V((R,), BF), V((R,), BF),
            pltpu.SemaphoreType.DMA((n_sems,)), pltpu.SemaphoreType.DMA((n_sems,)),
            pltpu.SemaphoreType.DMA((19,)), pltpu.SemaphoreType.DMA((3, lines - 1)),
        ],
        compiler_params=pltpu.CompilerParams(
            collective_id=0, has_side_effects=True, vmem_limit_bytes=62 * 2**20
        ),
        name="layer",
    )(seg, pad, ga, gm, hidden, wq, wk, wv, wo, wd, cot, wg, wu)


def final_kernel(
    hd, out_ref, hid_ref, gg_ref, down_ref, gate_ref, up_ref, wo_ref, qkv_ref,
    block_out, grad_hidden, gain_one, gain_two, g_query, g_key, g_value, g_out, g_gate, g_up, g_down,
):
    def total(ref):
        return sum(ref[i].astype(F32) for i in range(ref.shape[0]))

    QW, R = g_query.shape[1], gain_one.shape[0]
    block_out[...] = out_ref[...]
    grad_hidden[...] = hid_ref[...]
    gain_one[...] = gg_ref[:, :R].reshape(R)
    gain_two[...] = gg_ref[:, R:].reshape(R)
    qkv = total(qkv_ref)
    g_query[...] = qkv[:, :QW]
    kv = qkv[:, QW:].T
    g_key[...] = kv[:hd]
    g_value[...] = kv[hd:]
    g_out[...] = total(wo_ref).T
    g_gate[...] = gate_ref[...].astype(F32)
    g_up[...] = up_ref[...].astype(F32)
    g_down[...] = down_ref[...].astype(F32).T


def final(hd, block_out, grad_hidden, gg, s_out, s_qkv, down, gate, up):
    L, R, QW = s_out.shape
    FB = gate.shape[1]
    rows, D = block_out.shape
    steps = R // 128 if R % 128 == 0 else 1
    r = R // steps
    S = jax.ShapeDtypeStruct

    def parts(x):
        return pl.BlockSpec((L, r, x.shape[2]), lambda i: (0, i, 0))

    def tall(n):
        return pl.BlockSpec((r, n), lambda i: (i, 0))

    def wide(n):
        return pl.BlockSpec((n, r), lambda i: (0, i))

    acts = pl.BlockSpec((rows // steps, D), lambda i: (i, 0))
    gain = pl.BlockSpec((R,), lambda i: (0,))
    return pl.pallas_call(
        functools.partial(final_kernel, hd),
        grid=(steps,),
        out_shape=(
            S((rows, D), BF), S((rows, D), F32), S((R,), F32), S((R,), F32), S((R, QW), F32),
            S((hd, R), F32), S((hd, R), F32), S((QW, R), F32), S((R, FB), F32), S((R, FB), F32),
            S((FB, R), F32),
        ),
        in_specs=[acts, acts, pl.BlockSpec((1, 2 * R), lambda i: (0, 0))]
        + [tall(FB)] * 3 + [parts(s_out), parts(s_qkv)],
        out_specs=[acts, acts, gain, gain, tall(QW), wide(hd), wide(hd), wide(QW), tall(FB), tall(FB),
                   wide(FB)],
        compiler_params=pltpu.CompilerParams(vmem_limit_bytes=62 * 2**20),
        name="final",
    )(block_out, grad_hidden, gg, down, gate, up, s_out, s_qkv)


def body(hidden_in, segment_ids, pad_mask, attn_gain, w_query, w_key, w_value, w_out,
         mlp_gain, w_gate, w_up, w_down, cotangent):
    sizes = tuple(lax.axis_size(n) for n in ("fsdp", "context", "tensor"))
    hd = w_key.shape[1]
    block_out, grad_hidden, gg, _, _, _, s_out, s_qkv, down, gate, up = layer(
        sizes, hd, hidden_in[0], segment_ids, pad_mask, attn_gain, mlp_gain,
        w_query, w_key.T, w_value.T, w_out, w_down, cotangent[0], w_gate, w_up,
    )
    (block_out, grad_hidden, gain_one, gain_two, g_query, g_key, g_value, g_out, g_gate, g_up,
     g_down) = final(hd, block_out, grad_hidden, gg, s_out, s_qkv, down, gate, up)
    return (
        block_out[None], grad_hidden[None], gain_one, g_query, g_key.T, g_value.T, g_out, gain_two,
        g_gate, g_up, g_down,
    )


def solution(mesh):
    rows = P("fsdp", ("context", "tensor"), None)
    tail = (P(FC), P(FC, "tensor"), P(FC, "tensor"), P(FC, "tensor"), P("tensor", FC),
            P(FC), P(FC, "tensor"), P(FC, "tensor"), P("tensor", FC))
    in_specs = (rows, P("fsdp", None), P("fsdp", None)) + tail + (rows,)
    out_specs = (rows, rows) + tail
    return jax.shard_map(body, mesh=mesh, in_specs=in_specs, out_specs=out_specs, check_vma=False)
```
